256 devices in a mesh: grp: 8 (over x, y_hi), tile: 32 (over y_lo, z, core).
Axes of the slice: x: 4, y: 4 (y_hi: 2, y_lo: 2; y = y_hi * 2 + y_lo), z: 8, core: 2. Of those that a mesh axis runs over, the one named last changes fastest.
Arguments:
- adjoint_in: float32 [262144, 128], P(('grp', 'tile')), may hold values from -6 to 6
- departure: int32 [2, 262144], P(None, ('grp', 'tile')), may hold values from 0 to 262143, as said below
- fraction: float32 [2, 262144], P(None, ('grp', 'tile')), may hold values from 0 to 1
- level_map: float32 [2, 128, 128], replicated, may hold values from -0.5 to 0.5
- coarse_map: float32 [128, 8, 8], replicated, may hold values from -2 to 2
Outputs:
- adjoint_out: float32 [262144, 128], P(('grp', 'tile'))
The draws below stay inside these ranges and needn't reach their ends.
Inputs may be any that keep to these rules, and one draw needn't show every extreme that they name: For each step, the departure cell of a column lies in the same block row, on the device whose tile index differs from the column's own by at most 2, counted periodically along tile. Of the columns of one device, at most 512 have departure cells on any one device, and on every device exactly 512 of them share one device.
All inputs are finite; a program needn't handle non-finite values.
Results may differ from the reference program's by a relative error of at most 0.00013.
Values sent between devices are 32-bit elements; how exact they have to be, the bound alone decides.
No kernel may reach another device: no remote copies, remote signals or barrier semaphores. Data moves between devices by JAX's collectives and lax.ppermute only.
A program may use at most 64 MiB of HBM per device.

```python
import jax
import jax.numpy as jnp
from jax import lax

LEV = 128
COLS_DEV = 1024
REACH = 2
NCOLS = 262144
N_GRP = 8
N_TILE = 32


def draw_departure(key, part):
    devices_all = N_GRP * N_TILE
    width_span = 2 * REACH + 1
    key_wind, key_order, key_other, key_place = jax.random.split(key, 4)
    wind = jax.random.randint(key_wind, (2, devices_all, 1), -REACH, REACH + 1)
    scores = jax.random.randint(key_order, (2, devices_all, COLS_DEV), 0, 2 ** 18) * COLS_DEV + jnp.arange(COLS_DEV, dtype=jnp.int32)
    ranking = jnp.argsort(jnp.argsort(scores, axis=-1), axis=-1)
    leading = ranking < COLS_DEV // 2
    stride = jax.random.randint(key_other, (2, devices_all, COLS_DEV), 1, width_span)
    other = (wind + REACH + stride) % width_span - REACH
    offset = jnp.where(leading, wind, other)
    device_ids = jnp.arange(devices_all, dtype=jnp.int32)
    group_ids = device_ids // N_TILE
    tile_ids = device_ids % N_TILE
    target_tile = (tile_ids[None, :, None] + offset) % N_TILE
    place = jax.random.randint(key_place, (2, devices_all, COLS_DEV), 0, COLS_DEV)
    result = (group_ids[None, :, None] * N_TILE + target_tile) * COLS_DEV + place
    return result.reshape(2, devices_all * COLS_DEV).astype(jnp.int32)


def block_scale(own_key, extent, shards, low, largest):
    level, own = 1.0, jax.random.fold_in(own_key, 6)
    for dim, shards_of in shards:
        draws = jnp.exp(jax.random.uniform(jax.random.fold_in(own, dim), (shards_of,), jnp.float32, low / len(shards), largest / len(shards)))
        level = level * jnp.repeat(draws, extent[dim] // shards_of).reshape([-1 if axis == dim else 1 for axis in range(len(extent))])
    return level


def noise(own_key, shape, width, limit, shards=(), held_as=jnp.bfloat16):
    drawn = width * jax.random.normal(own_key, shape, jnp.float32)
    if shards:
        drawn = drawn * block_scale(own_key, shape, shards, -0.22, 0.18)
    return jnp.clip(drawn, -limit, limit).astype(held_as)


def setup_inputs(seed: int = 0) -> dict:
    key_of = jax.random.split(jax.random.key(seed), 6)
    return {
        "adjoint_in": noise(key_of[0], (NCOLS, LEV), 1.0, 6.0, ((0, 256),), jnp.float32),
        "departure": draw_departure(jax.random.fold_in(key_of[5], 71), 0),
        "fraction": jnp.clip(1.0 * jax.random.uniform(key_of[2], (2, NCOLS), jnp.float32) ** block_scale(key_of[2], (2, NCOLS), ((1, 256),), -0.2, 0.2), 0.0, 1.0),
        "level_map": noise(key_of[3], (2, LEV, LEV), LEV ** -0.5, 0.5, (), jnp.float32),
        "coarse_map": noise(key_of[4], (LEV, N_GRP, N_GRP), N_GRP ** -0.5, 2.0, (), jnp.float32),
    }


def cubic_weights(fraction):
    alpha = fraction
    return [-alpha * (1.0 - alpha) * (2.0 - alpha) / 6.0,
            (1.0 + alpha) * (1.0 - alpha) * (2.0 - alpha) / 2.0,
            (1.0 + alpha) * alpha * (2.0 - alpha) / 2.0,
            -(1.0 + alpha) * alpha * (1.0 - alpha) / 6.0]


def transport_adjoint(field, departure, fraction, level_map):
    lifted = jnp.dot(field, level_map.T, precision=lax.Precision.HIGHEST, preferred_element_type=jnp.float32)
    row_span = COLS_DEV * N_TILE
    row_start = (departure // row_span) * row_span
    result = jnp.zeros_like(lifted)
    for stencil, weight in enumerate(cubic_weights(fraction)):
        target = row_start + (departure - row_start + stencil - 1) % row_span
        result = result.at[target].add(weight[:, None] * lifted)
    return result


def couple_rows(field, coarse_map):
    blocks = field.reshape(N_GRP, COLS_DEV * N_TILE, LEV)
    mixed = jnp.einsum("ecl,lbe->bcl", blocks, coarse_map, precision=lax.Precision.HIGHEST)
    return mixed.reshape(N_GRP * COLS_DEV * N_TILE, LEV)


def reference(adjoint_in, departure, fraction, level_map, coarse_map):
    second = transport_adjoint(adjoint_in, departure[1], fraction[1], level_map[1])
    coupled = couple_rows(second, coarse_map)
    return transport_adjoint(coupled, departure[0], fraction[0], level_map[0])
```

```python
import functools

import jax
import jax.numpy as jnp
from jax import lax
from jax.experimental import pallas as pl
from jax.experimental.pallas import tpu as pltpu
from jax.sharding import PartitionSpec as P

REACH = 2
SHIFTS = (-2, 2, -1, 1)
COLS = 1024
LEV = 128
CAP = 512
ROWS = CAP + 16
BF = jnp.bfloat16
F32 = jnp.float32


def shifted(x, axis, by):
    length = lax.axis_size(axis)
    return lax.ppermute(x, axis, [(i, (i + by) % length) for i in range(length)])


def halves(x):
    high = x.astype(BF)
    low = (x - high.astype(F32)).astype(BF)
    return high, low


def dot(a, b):
    return lax.dot_general(a, b, (((1,), (0,)), ((), ())), preferred_element_type=F32)


def dot_nt(a, b):
    return lax.dot_general(a, b, (((1,), (1,)), ((), ())), preferred_element_type=F32)


def cubic_weights(a):
    return (
        -a * (1.0 - a) * (2.0 - a) * (1.0 / 6.0),
        (1.0 + a) * (1.0 - a) * (2.0 - a) * 0.5,
        (1.0 + a) * a * (2.0 - a) * 0.5,
        -(1.0 + a) * a * (1.0 - a) * (1.0 / 6.0),
    )


def locate(departure, tile_self, tile_count):
    place = departure % COLS
    target = (departure // COLS) % tile_count
    offset = (target - tile_self + REACH + tile_count) % tile_count - REACH
    return place, offset


def slots_of(offset):
    row = lax.broadcasted_iota(jnp.int32, (8, LEV), 0)
    lane_a = lax.broadcasted_iota(jnp.int32, (LEV, LEV), 0)
    lane_b = lax.broadcasted_iota(jnp.int32, (LEV, LEV), 1)
    before = jnp.where(lane_a < lane_b, 1.0, 0.0).astype(BF)
    number = jnp.full((1, COLS), 4, jnp.int32)
    for which, shift in enumerate(SHIFTS):
        number = jnp.where(offset == shift, which, number)
    members = []
    for c in range(COLS // LEV):
        part = number[:, c * LEV : (c + 1) * LEV]
        members.append(jnp.where(row == part, 1.0, 0.0))
    member = jnp.concatenate(members, axis=0)
    inside = dot(member.astype(BF), before)
    totals = jnp.sum(member, axis=1, keepdims=True)
    start = jnp.zeros((8, 1), F32)
    keys = []
    for c in range(COLS // LEV):
        block = slice(8 * c, 8 * c + 8)
        rank = inside[block] + start
        start = start + totals[block]
        key = jnp.sum(member[block] * (rank + row.astype(F32) * CAP), axis=0, keepdims=True)
        keys.append(key)
    return jnp.concatenate(keys, axis=1).astype(jnp.int32)


def spill_rows(place, offset, weights):
    row = lax.broadcasted_iota(jnp.int32, (8, COLS), 0)
    last = place == COLS - 1
    first_a = jnp.where(last, weights[2], jnp.where(place == COLS - 2, weights[3], 0.0))
    first_b = jnp.where(last, weights[3], 0.0)
    end = jnp.where(place == 0, weights[0], 0.0)
    rows = jnp.where(row == 0, first_a, jnp.where(row == 1, first_b, jnp.where(row == 7, end, 0.0)))
    spread = [jnp.where(offset == o, rows, 0.0) for o in range(-REACH, REACH + 1)]
    high, low = halves(jnp.concatenate(spread, axis=0))
    return jnp.concatenate([high, low], axis=0)


def meta_rows(place, fraction):
    a = fraction.astype(BF)
    rest = fraction - a.astype(F32)
    b = rest.astype(BF)
    c = rest - b.astype(F32)
    p_high = (place // 32).astype(F32)
    p_low = (place % 32).astype(F32)
    row = lax.broadcasted_iota(jnp.int32, (8, COLS), 0)
    out = jnp.where(row == 0, a.astype(F32), 0.0)
    out = jnp.where(row == 1, b.astype(F32), out)
    out = jnp.where(row == 2, c, out)
    out = jnp.where(row == 3, p_high, out)
    out = jnp.where(row == 4, p_low, out)
    return out.astype(BF)


def choose(keys, which):
    slot = lax.broadcasted_iota(jnp.int32, (CAP, COLS), 0) + which * CAP
    return jnp.where(slot == keys, 1.0, 0.0).astype(BF)


def spill_block(spilled, target):
    row = lax.broadcasted_iota(jnp.int32, (8, LEV), 0)
    out = jnp.zeros((8, LEV), F32)
    for o in (target - 1, target + 1):
        if -REACH <= o <= REACH:
            block = spilled[8 * (o + REACH) : 8 * (o + REACH) + 8]
            keep = row < 2 if o == target - 1 else row == 7
            out = out + jnp.where(keep, block, 0.0)
    return out


def spill_sums(spills, both):
    wide = dot(spills, both)
    count = 8 * (2 * REACH + 1)
    return (wide[:count, :LEV] + wide[:count, LEV:]) + (wide[count:, :LEV] + wide[count:, LEV:])


def index_values(self_ref, departure, fraction, tile_count):
    place, offset = locate(departure, self_ref[0], tile_count)
    keys = slots_of(offset)
    weights = cubic_weights(fraction)
    return place, offset, keys, weights


def write_meta(meta_out, base, meta, one_hot):
    got = dot_nt(meta, one_hot)
    fraction = got[0:1] + got[1:2] + got[2:3]
    place = got[3:4] * 32.0 + got[4:5]
    for c in range(CAP // LEV):
        meta_out[base + c : base + c + 1, :] = fraction[:, c * LEV : (c + 1) * LEV]
        meta_out[base + 4 + c : base + 5 + c, :] = place[:, c * LEV : (c + 1) * LEV]


def pack_payload(out, one_hot, both, spilled, shift):
    wide = dot(one_hot, both)
    out[0:CAP, :] = wide[:, :LEV] + wide[:, LEV:]
    out[CAP : CAP + 8, :] = spill_block(spilled, shift)


def first_pack_kernel(tile_count, self_ref, field, departure, fraction, *outs):
    place, offset, keys, weights = index_values(self_ref, departure[1:2, :], fraction[1:2, :], tile_count)
    meta = meta_rows(place, fraction[1:2, :])
    high, low = halves(field[...])
    both = jnp.concatenate([high, low], axis=1)
    spilled = spill_sums(spill_rows(place, offset, weights), both)
    outs[4][...] = spill_block(spilled, -3)
    outs[5][...] = spill_block(spilled, 3)
    outs[6][...] = spill_block(spilled, 0)
    for which, shift in enumerate(SHIFTS):
        one_hot = choose(keys, which)
        pack_payload(outs[which], one_hot, both, spilled, shift)
        write_meta(outs[which], CAP + 8, meta, one_hot)


def index_kernel(tile_count, self_ref, departure, fraction, keys_out, spill_out, meta_out):
    place, offset, keys, weights = index_values(self_ref, departure[0:1, :], fraction[0:1, :], tile_count)
    meta = meta_rows(place, fraction[0:1, :])
    keys_out[...] = keys
    spill_out[...] = spill_rows(place, offset, weights)
    for which in range(len(SHIFTS)):
        write_meta(meta_out, 8 * which, meta, choose(keys, which))


def second_pack_kernel(field, keys, spills, meta, *outs):
    high, low = halves(field[...])
    both = jnp.concatenate([high, low], axis=1)
    spilled = spill_sums(spills[...], both)
    outs[4][...] = spill_block(spilled, -3)
    outs[5][...] = spill_block(spilled, 3)
    outs[6][...] = spill_block(spilled, 0)
    for which, shift in enumerate(SHIFTS):
        pack_payload(outs[which], choose(keys[...], which), both, spilled, shift)
        outs[which][CAP + 8 : CAP + 16, :] = meta[8 * which : 8 * which + 8, :]


BLOCK = 128


def spread_block(first_cell, places, weights):
    cells = lax.broadcasted_iota(jnp.int32, (BLOCK, places.shape[1]), 0)
    distance = cells - (places - 1 - first_cell)
    spread = jnp.where(distance == 0, weights[0], 0.0)
    for k in (1, 2, 3):
        spread = jnp.where(distance == k, weights[k], spread)
    return halves(spread)


def own_kernel(step, tile_count, self_ref, field, departure, fraction, spilled, out, both_ref):
    departure = departure[step : step + 1, :]
    fraction = fraction[step : step + 1, :]
    place, offset = locate(departure, self_ref[0], tile_count)
    weights = [jnp.where(offset == 0, w, 0.0) for w in cubic_weights(fraction)]
    high, low = halves(field[...])
    both_ref[:, :LEV] = high
    both_ref[:, LEV:] = low

    @pl.loop(0, COLS // BLOCK)
    def _(b):
        high, low = spread_block(b * BLOCK, place, weights)
        wide = dot(high, both_ref[...]) + dot(low, both_ref[...])
        out[pl.ds(b * BLOCK, BLOCK), :] = wide[:, :LEV] + wide[:, LEV:]

    add_spill(out, spilled[...])


def add_spill(out, block):
    row = lax.broadcasted_iota(jnp.int32, (8, LEV), 0)
    out[0:8, :] = out[0:8, :] + jnp.where(row < 2, block, 0.0)
    out[COLS - 8 : COLS, :] = out[COLS - 8 : COLS, :] + jnp.where(row == 7, block, 0.0)


def deposit_kernel(step, own, p0, p1, p2, p3, tiny_a, tiny_b, level_map, out, both_ref, sum_ref):
    payloads = (p0, p1, p2, p3)
    spill = tiny_a[...] + tiny_b[...]
    for which, payload in enumerate(payloads):
        high, low = halves(payload[0:CAP, :])
        both_ref[which, :, :LEV] = high
        both_ref[which, :, LEV:] = low
        spill = spill + payload[CAP : CAP + 8, :]
    tables = []
    for payload in payloads:
        rows = [payload[CAP + 8 + c : CAP + 9 + c, :] for c in range(8)]
        fraction = jnp.concatenate(rows[:4], axis=1)
        place = jnp.concatenate(rows[4:], axis=1).astype(jnp.int32)
        tables.append((place, cubic_weights(fraction)))

    @pl.loop(0, COLS // BLOCK)
    def _(b):
        wide = jnp.zeros((BLOCK, 2 * LEV), F32)
        for which in range(4):
            place, weights = tables[which]
            high, low = spread_block(b * BLOCK, place, weights)
            wide = wide + dot(high, both_ref[which]) + dot(low, both_ref[which])
        sum_ref[pl.ds(b * BLOCK, BLOCK), :] = own[pl.ds(b * BLOCK, BLOCK), :] + wide[:, :LEV] + wide[:, LEV:]

    add_spill(sum_ref, spill)
    map_high, map_low = halves(level_map[step])
    high, low = halves(sum_ref[...])
    out[...] = dot_nt(high, map_high) + (dot_nt(high, map_low) + dot_nt(low, map_high))


def couple_kernel(table, x, out):
    count = x.shape[0]

    @pl.loop(0, x.shape[1] // 8)
    def _(r):
        rows = [x[e, pl.ds(r * 8, 8), :] for e in range(count)]
        for b in range(count):
            total = rows[0] * table[count * b : count * b + 1, :]
            for e in range(1, count):
                total = total + rows[e] * table[count * b + e : count * b + e + 1, :]
            out[b, pl.ds(r * 8, 8), :] = total


VM = pl.BlockSpec(memory_space=pltpu.MemorySpace.VMEM)
SM = pl.BlockSpec(memory_space=pltpu.MemorySpace.SMEM)
PARAMS = pltpu.CompilerParams(vmem_limit_bytes=40 * 1024 * 1024)
PACKED = [jax.ShapeDtypeStruct((ROWS, LEV), F32)] * 4 + [jax.ShapeDtypeStruct((8, LEV), F32)] * 3


def call(kernel, out_shape, in_specs, scratch=()):
    multiple = isinstance(out_shape, (list, tuple))
    return pl.pallas_call(
        kernel,
        out_shape=out_shape,
        in_specs=in_specs,
        out_specs=[VM] * len(out_shape) if multiple else VM,
        scratch_shapes=list(scratch),
        compiler_params=PARAMS,
    )


def send(packed):
    tiny = [shifted(packed[4], "tile", -3), shifted(packed[5], "tile", 3)]
    return [shifted(packed[w], "tile", s) for w, s in enumerate(SHIFTS)] + tiny


def own_part(step, tile_count, tile_self, field, departure, fraction, spilled):
    return call(
        functools.partial(own_kernel, step, tile_count),
        jax.ShapeDtypeStruct((COLS, LEV), F32),
        [SM, VM, VM, VM, VM],
        [pltpu.VMEM((COLS, 2 * LEV), BF)],
    )(tile_self, field, departure, fraction, spilled)


def deposited(step, own, arrived, level_map):
    return call(
        functools.partial(deposit_kernel, step),
        jax.ShapeDtypeStruct((COLS, LEV), F32),
        [VM] * 8,
        [pltpu.VMEM((4, CAP, 2 * LEV), BF), pltpu.VMEM((COLS, LEV), F32)],
    )(own, *arrived, level_map)


def body(adjoint_in, departure, fraction, level_map, coarse_map):
    tile_count = lax.axis_size("tile")
    groups = lax.axis_size("grp")
    tile_self = lax.axis_index("tile").astype(jnp.int32).reshape(1)
    packed = call(functools.partial(first_pack_kernel, tile_count), PACKED, [SM, VM, VM, VM])(
        tile_self, adjoint_in, departure, fraction
    )
    arrived = send(packed)
    own = own_part(1, tile_count, tile_self, adjoint_in, departure, fraction, packed[6])
    keys, spills, meta = call(
        functools.partial(index_kernel, tile_count),
        [
            jax.ShapeDtypeStruct((1, COLS), jnp.int32),
            jax.ShapeDtypeStruct((16 * (2 * REACH + 1), COLS), BF),
            jax.ShapeDtypeStruct((32, LEV), F32),
        ],
        [SM, VM, VM],
    )(tile_self, departure, fraction)
    table = coarse_map.transpose(1, 2, 0).reshape(groups * groups, LEV)
    second = deposited(1, own, arrived, level_map)

    parts = lax.all_to_all(second.reshape(groups, COLS // groups, LEV), "grp", 0, 0)
    mixed = call(couple_kernel, jax.ShapeDtypeStruct(parts.shape, F32), [VM, VM])(table, parts)
    coupled = lax.all_to_all(mixed, "grp", 0, 0).reshape(COLS, LEV)

    packed = call(second_pack_kernel, PACKED, [VM] * 4)(coupled, keys, spills, meta)
    arrived = send(packed)
    own = own_part(0, tile_count, tile_self, coupled, departure, fraction, packed[6])
    return deposited(0, own, arrived, level_map)


def solution(mesh):
    return jax.shard_map(
        body,
        mesh=mesh,
        in_specs=(
            P(("grp", "tile"), None),
            P(None, ("grp", "tile")),
            P(None, ("grp", "tile")),
            P(),
            P(),
        ),
        out_specs=P(("grp", "tile"), None),
        check_vma=False,
    )
```

```python
import functools

import jax
import jax.numpy as jnp
from jax import lax
from jax.experimental import pallas as pl
from jax.experimental.pallas import tpu as pltpu
from jax.sharding import PartitionSpec as P

REACH = 2
SHIFTS = (-2, 2, -1, 1)
COLS = 1024
LEV = 128
CAP = 512
ROWS = CAP + 16
BF = jnp.bfloat16
F32 = jnp.float32


def shifted(x, axis, by):
    length = lax.axis_size(axis)
    return lax.ppermute(x, axis, [(i, (i + by) % length) for i in range(length)])


def halves(x):
    high = x.astype(BF)
    low = (x - high.astype(F32)).astype(BF)
    return high, low


def dot(a, b):
    return lax.dot_general(a, b, (((1,), (0,)), ((), ())), preferred_element_type=F32)


def dot_nt(a, b):
    return lax.dot_general(a, b, (((1,), (1,)), ((), ())), preferred_element_type=F32)


def cubic_weights(a):
    return (
        -a * (1.0 - a) * (2.0 - a) * (1.0 / 6.0),
        (1.0 + a) * (1.0 - a) * (2.0 - a) * 0.5,
        (1.0 + a) * a * (2.0 - a) * 0.5,
        -(1.0 + a) * a * (1.0 - a) * (1.0 / 6.0),
    )


def locate(departure, tile_self, tile_count):
    place = departure % COLS
    target = (departure // COLS) % tile_count
    offset = (target - tile_self + REACH + tile_count) % tile_count - REACH
    return place, offset


def slots_of(offset):
    row = lax.broadcasted_iota(jnp.int32, (8, LEV), 0)
    lane_a = lax.broadcasted_iota(jnp.int32, (LEV, LEV), 0)
    lane_b = lax.broadcasted_iota(jnp.int32, (LEV, LEV), 1)
    before = jnp.where(lane_a < lane_b, 1.0, 0.0).astype(BF)
    number = jnp.full((1, COLS), 4, jnp.int32)
    for which, shift in enumerate(SHIFTS):
        number = jnp.where(offset == shift, which, number)
    members = []
    for c in range(COLS // LEV):
        part = number[:, c * LEV : (c + 1) * LEV]
        members.append(jnp.where(row == part, 1.0, 0.0))
    member = jnp.concatenate(members, axis=0)
    inside = dot(member.astype(BF), before)
    totals = jnp.sum(member, axis=1, keepdims=True)
    start = jnp.zeros((8, 1), F32)
    keys = []
    for c in range(COLS // LEV):
        block = slice(8 * c, 8 * c + 8)
        rank = inside[block] + start
        start = start + totals[block]
        key = jnp.sum(member[block] * (rank + row.astype(F32) * CAP), axis=0, keepdims=True)
        keys.append(key)
    return jnp.concatenate(keys, axis=1).astype(jnp.int32)


def spill_rows(place, offset, weights):
    row = lax.broadcasted_iota(jnp.int32, (8, COLS), 0)
    last = place == COLS - 1
    first_a = jnp.where(last, weights[2], jnp.where(place == COLS - 2, weights[3], 0.0))
    first_b = jnp.where(last, weights[3], 0.0)
    end = jnp.where(place == 0, weights[0], 0.0)
    rows = jnp.where(row == 0, first_a, jnp.where(row == 1, first_b, jnp.where(row == 7, end, 0.0)))
    spread = [jnp.where(offset == o, rows, 0.0) for o in range(-REACH, REACH + 1)]
    high, low = halves(jnp.concatenate(spread, axis=0))
    return jnp.concatenate([high, low], axis=0)


def meta_rows(place, fraction):
    a = fraction.astype(BF)
    rest = fraction - a.astype(F32)
    b = rest.astype(BF)
    c = rest - b.astype(F32)
    p_high = (place // 32).astype(F32)
    p_low = (place % 32).astype(F32)
    row = lax.broadcasted_iota(jnp.int32, (8, COLS), 0)
    out = jnp.where(row == 0, a.astype(F32), 0.0)
    out = jnp.where(row == 1, b.astype(F32), out)
    out = jnp.where(row == 2, c, out)
    out = jnp.where(row == 3, p_high, out)
    out = jnp.where(row == 4, p_low, out)
    return out.astype(BF)


def choose(keys, which):
    slot = lax.broadcasted_iota(jnp.int32, (CAP, COLS), 0).astype(jnp.int16)
    wanted = jnp.broadcast_to(keys - which * CAP, (16, COLS)).astype(jnp.int16)
    wanted = jnp.concatenate([wanted] * (CAP // 16), axis=0)
    return jnp.where(slot == wanted, BF(1.0), BF(0.0))


def spill_block(spilled, target):
    row = lax.broadcasted_iota(jnp.int32, (8, LEV), 0)
    out = jnp.zeros((8, LEV), F32)
    for o in (target - 1, target + 1):
        if -REACH <= o <= REACH:
            block = spilled[8 * (o + REACH) : 8 * (o + REACH) + 8]
            keep = row < 2 if o == target - 1 else row == 7
            out = out + jnp.where(keep, block, 0.0)
    return out


def spill_sums(spills, both):
    wide = dot(spills, both)
    count = 8 * (2 * REACH + 1)
    return (wide[:count, :LEV] + wide[:count, LEV:]) + (wide[count:, :LEV] + wide[count:, LEV:])


def index_values(self_ref, departure, fraction, tile_count):
    place, offset = locate(departure, self_ref[0], tile_count)
    keys = slots_of(offset)
    weights = cubic_weights(fraction)
    return place, offset, keys, weights


def write_meta(meta_out, base, meta, one_hot):
    got = dot_nt(meta, one_hot)
    fraction = got[0:1] + got[1:2] + got[2:3]
    place = got[3:4] * 32.0 + got[4:5]
    for c in range(CAP // LEV):
        meta_out[base + c : base + c + 1, :] = fraction[:, c * LEV : (c + 1) * LEV]
        meta_out[base + 4 + c : base + 5 + c, :] = place[:, c * LEV : (c + 1) * LEV]


def pack_payload(out, one_hot, both, spilled, shift):
    wide = dot(one_hot, both)
    out[0:CAP, :] = wide[:, :LEV] + wide[:, LEV:]
    out[CAP : CAP + 8, :] = spill_block(spilled, shift)


def first_pack_kernel(tile_count, self_ref, field_hbm, departure_hbm, fraction_hbm, *refs):
    outs, (field, departure, fraction, sems) = refs[:-4], refs[-4:]
    copies = [
        pltpu.make_async_copy(departure_hbm, departure, sems.at[0]),
        pltpu.make_async_copy(fraction_hbm, fraction, sems.at[1]),
        pltpu.make_async_copy(field_hbm, field, sems.at[2]),
    ]
    for copy in copies:
        copy.start()
    copies[0].wait()
    copies[1].wait()
    place, offset, keys, weights = index_values(self_ref, departure[1:2, :], fraction[1:2, :], tile_count)
    meta = meta_rows(place, fraction[1:2, :])
    spills = spill_rows(place, offset, weights)
    copies[2].wait()
    high, low = halves(field[...])
    both = jnp.concatenate([high, low], axis=1)
    spilled = spill_sums(spills, both)
    outs[4][...] = spill_block(spilled, -3)
    outs[5][...] = spill_block(spilled, 3)
    outs[6][...] = spill_block(spilled, 0)
    for which, shift in enumerate(SHIFTS):
        one_hot = choose(keys, which)
        pack_payload(outs[which], one_hot, both, spilled, shift)
        write_meta(outs[which], CAP + 8, meta, one_hot)


def index_kernel(tile_count, self_ref, departure, fraction, keys_out, spill_out, meta_out):
    place, offset, keys, weights = index_values(self_ref, departure[0:1, :], fraction[0:1, :], tile_count)
    meta = meta_rows(place, fraction[0:1, :])
    keys_out[...] = keys
    spill_out[...] = spill_rows(place, offset, weights)
    for which in range(len(SHIFTS)):
        write_meta(meta_out, 8 * which, meta, choose(keys, which))


def second_pack_kernel(field, keys, spills, meta, *outs):
    high, low = halves(field[...])
    both = jnp.concatenate([high, low], axis=1)
    spilled = spill_sums(spills[...], both)
    outs[4][...] = spill_block(spilled, -3)
    outs[5][...] = spill_block(spilled, 3)
    outs[6][...] = spill_block(spilled, 0)
    for which, shift in enumerate(SHIFTS):
        pack_payload(outs[which], choose(keys[...], which), both, spilled, shift)
        outs[which][CAP + 8 : CAP + 16, :] = meta[8 * which : 8 * which + 8, :]


BLOCK = 512
I16 = jnp.int16


def tiled(x, rows):
    return jnp.concatenate([x] * (rows // 16), axis=0)


def spread_table(place, weights):
    shape = (16, place.shape[1])
    start = jnp.broadcast_to(place - 1, shape).astype(I16)
    return start, [halves(jnp.broadcast_to(w, shape)) for w in weights]


def spread_block(first_cell, table):
    start, weights = table
    columns = start.shape[1]
    cells = lax.broadcasted_iota(jnp.int32, (BLOCK, columns), 0).astype(I16)
    first = jnp.full((16, columns), first_cell, jnp.int32).astype(I16)
    distance = cells - tiled(start - first, BLOCK)
    high = jnp.zeros((BLOCK, columns), BF)
    low = high
    for k in range(4):
        here = distance == I16(k)
        high = jnp.where(here, tiled(weights[k][0], BLOCK), high)
        low = jnp.where(here, tiled(weights[k][1], BLOCK), low)
    return high, low


def own_kernel(step, tile_count, self_ref, field, departure, fraction, spilled, out, both_ref):
    departure = departure[step : step + 1, :]
    fraction = fraction[step : step + 1, :]
    place, offset = locate(departure, self_ref[0], tile_count)
    table = spread_table(place, [jnp.where(offset == 0, w, 0.0) for w in cubic_weights(fraction)])
    high, low = halves(field[...])
    both_ref[:, :LEV] = high
    both_ref[:, LEV:] = low

    @pl.loop(0, COLS // BLOCK)
    def _(b):
        high, low = spread_block(b * BLOCK, table)
        wide = dot(high, both_ref[...]) + dot(low, both_ref[...])
        out[pl.ds(b * BLOCK, BLOCK), :] = wide[:, :LEV] + wide[:, LEV:]

    add_spill(out, spilled[...])


def add_spill(out, block):
    row = lax.broadcasted_iota(jnp.int32, (8, LEV), 0)
    out[0:8, :] = out[0:8, :] + jnp.where(row < 2, block, 0.0)
    out[COLS - 8 : COLS, :] = out[COLS - 8 : COLS, :] + jnp.where(row == 7, block, 0.0)


def deposit_sums(start, payloads, out, both_ref):
    tables = []
    for which, payload in enumerate(payloads):
        high, low = halves(payload[0:CAP, :])
        both_ref[which, :, :LEV] = high
        both_ref[which, :, LEV:] = low
        rows = [payload[CAP + 8 + c : CAP + 9 + c, :] for c in range(8)]
        fraction = jnp.concatenate(rows[:4], axis=1)
        place = jnp.concatenate(rows[4:], axis=1).astype(jnp.int32)
        tables.append(spread_table(place, cubic_weights(fraction)))

    @pl.loop(0, COLS // BLOCK)
    def _(b):
        wide = jnp.zeros((BLOCK, 2 * LEV), F32)
        for which, table in enumerate(tables):
            high, low = spread_block(b * BLOCK, table)
            wide = wide + dot(high, both_ref[which]) + dot(low, both_ref[which])
        out[pl.ds(b * BLOCK, BLOCK), :] = start[pl.ds(b * BLOCK, BLOCK), :] + wide[:, :LEV] + wide[:, LEV:]

    spill = payloads[0][CAP : CAP + 8, :]
    for payload in payloads[1:]:
        spill = spill + payload[CAP : CAP + 8, :]
    return spill


def near_kernel(start, p0, p1, out, both_ref):
    spill = deposit_sums(start, (p0, p1), out, both_ref)
    add_spill(out, spill)


def far_kernel(step, start, p0, p1, tiny_a, tiny_b, level_map, out, both_ref, sum_ref):
    spill = deposit_sums(start, (p0, p1), sum_ref, both_ref)
    add_spill(sum_ref, spill + tiny_a[...] + tiny_b[...])
    map_high, map_low = halves(level_map[step])
    high, low = halves(sum_ref[...])
    out[...] = dot_nt(high, map_high) + (dot_nt(high, map_low) + dot_nt(low, map_high))


def couple_kernel(table, x, out):
    count = x.shape[0]

    @pl.loop(0, x.shape[1] // 8)
    def _(r):
        rows = [x[e, pl.ds(r * 8, 8), :] for e in range(count)]
        for b in range(count):
            total = rows[0] * table[count * b : count * b + 1, :]
            for e in range(1, count):
                total = total + rows[e] * table[count * b + e : count * b + e + 1, :]
            out[b, pl.ds(r * 8, 8), :] = total


VM = pl.BlockSpec(memory_space=pltpu.MemorySpace.VMEM)
HBM = pl.BlockSpec(memory_space=pltpu.MemorySpace.HBM)
SM = pl.BlockSpec(memory_space=pltpu.MemorySpace.SMEM)
PARAMS = pltpu.CompilerParams(vmem_limit_bytes=40 * 1024 * 1024)
PACKED = [jax.ShapeDtypeStruct((ROWS, LEV), F32)] * 4 + [jax.ShapeDtypeStruct((8, LEV), F32)] * 3


def call(kernel, out_shape, in_specs, scratch=(), flops=0):
    multiple = isinstance(out_shape, (list, tuple))
    return pl.pallas_call(
        kernel,
        out_shape=out_shape,
        in_specs=in_specs,
        out_specs=[VM] * len(out_shape) if multiple else VM,
        scratch_shapes=list(scratch),
        compiler_params=PARAMS,
        cost_estimate=pl.CostEstimate(flops=flops, transcendentals=0, bytes_accessed=flops // 256),
    )


def transported(step, packed, tile_count, tile_self, field, departure, fraction, level_map):
    near = [shifted(packed[2], "tile", SHIFTS[2]), shifted(packed[3], "tile", SHIFTS[3])]
    far = [shifted(packed[0], "tile", SHIFTS[0]), shifted(packed[1], "tile", SHIFTS[1])]
    tiny = [shifted(packed[4], "tile", -3), shifted(packed[5], "tile", 3)]
    total = jax.ShapeDtypeStruct((COLS, LEV), F32)
    work = 3 * 10**9
    own = call(
        functools.partial(own_kernel, step, tile_count),
        total,
        [SM, VM, VM, VM, VM],
        [pltpu.VMEM((COLS, 2 * LEV), BF)],
        work,
    )(tile_self, field, departure, fraction, packed[6])
    both = pltpu.VMEM((2, CAP, 2 * LEV), BF)
    summed = call(near_kernel, total, [VM] * 3, [both], work)(own, *near)
    return call(
        functools.partial(far_kernel, step),
        total,
        [VM] * 6,
        [both, pltpu.VMEM((COLS, LEV), F32)],
        work,
    )(summed, *far, *tiny, level_map)


def body(adjoint_in, departure, fraction, level_map, coarse_map):
    tile_count = lax.axis_size("tile")
    groups = lax.axis_size("grp")
    tile_self = lax.axis_index("tile").astype(jnp.int32).reshape(1)
    first_scratch = [
        pltpu.VMEM((COLS, LEV), F32),
        pltpu.VMEM((2, COLS), jnp.int32),
        pltpu.VMEM((2, COLS), F32),
        pltpu.SemaphoreType.DMA((3,)),
    ]
    packed = call(functools.partial(first_pack_kernel, tile_count), PACKED, [SM, HBM, HBM, HBM], first_scratch)(
        tile_self, *[pltpu.with_memory_space_constraint(x, pltpu.MemorySpace.HBM) for x in (adjoint_in, departure, fraction)]
    )
    keys, spills, meta = call(
        functools.partial(index_kernel, tile_count),
        [
            jax.ShapeDtypeStruct((1, COLS), jnp.int32),
            jax.ShapeDtypeStruct((16 * (2 * REACH + 1), COLS), BF),
            jax.ShapeDtypeStruct((32, LEV), F32),
        ],
        [SM, VM, VM],
        (),
        2 * 10**9,
    )(tile_self, departure, fraction)
    table = coarse_map.transpose(1, 2, 0).reshape(groups * groups, LEV)
    second = transported(1, packed, tile_count, tile_self, adjoint_in, departure, fraction, level_map)

    parts = lax.all_to_all(second.reshape(groups, COLS // groups, LEV), "grp", 0, 0)
    mixed = call(couple_kernel, jax.ShapeDtypeStruct(parts.shape, F32), [VM, VM])(table, parts)
    coupled = lax.all_to_all(mixed, "grp", 0, 0).reshape(COLS, LEV)

    packed = call(second_pack_kernel, PACKED, [VM] * 4)(coupled, keys, spills, meta)
    return transported(0, packed, tile_count, tile_self, coupled, departure, fraction, level_map)


def solution(mesh):
    return jax.shard_map(
        body,
        mesh=mesh,
        in_specs=(
            P(("grp", "tile"), None),
            P(None, ("grp", "tile")),
            P(None, ("grp", "tile")),
            P(),
            P(),
        ),
        out_specs=P(("grp", "tile"), None),
        check_vma=False,
    )
```

```python
import functools

import jax
import jax.numpy as jnp
from jax import lax
from jax.experimental import pallas as pl
from jax.experimental.pallas import tpu as pltpu
from jax.sharding import PartitionSpec as P

REACH = 2
SWAPS = 4
COLS = 1024
LEV = 128
CAP = 512
ROWS = CAP + 16
BF = jnp.bfloat16
F32 = jnp.float32


def signs(tile):
    core = 1 - 2 * (tile % 2)
    chip = 1 - 2 * ((tile // 2) % 2)
    return (2 * chip, -2 * chip, -core, core, 3 * core, -3 * core)


def swapped(x, which):
    length = lax.axis_size("tile")
    return lax.ppermute(x, "tile", [(i, (i + signs(i)[which]) % length) for i in range(length)])


def halves(x):
    high = x.astype(BF)
    low = (x - high.astype(F32)).astype(BF)
    return high, low


def dot(a, b):
    return lax.dot_general(a, b, (((1,), (0,)), ((), ())), preferred_element_type=F32)


def dot_nt(a, b):
    return lax.dot_general(a, b, (((1,), (1,)), ((), ())), preferred_element_type=F32)


def cubic_weights(a):
    return (
        -a * (1.0 - a) * (2.0 - a) * (1.0 / 6.0),
        (1.0 + a) * (1.0 - a) * (2.0 - a) * 0.5,
        (1.0 + a) * a * (2.0 - a) * 0.5,
        -(1.0 + a) * a * (1.0 - a) * (1.0 / 6.0),
    )


def locate(departure, tile_self, tile_count):
    place = departure % COLS
    target = (departure // COLS) % tile_count
    offset = (target - tile_self + REACH + tile_count) % tile_count - REACH
    return place, offset


def slots_of(offset, shifts):
    row = lax.broadcasted_iota(jnp.int32, (8, LEV), 0)
    lane_a = lax.broadcasted_iota(jnp.int32, (LEV, LEV), 0)
    lane_b = lax.broadcasted_iota(jnp.int32, (LEV, LEV), 1)
    before = jnp.where(lane_a < lane_b, 1.0, 0.0).astype(BF)
    number = jnp.full((1, COLS), 4, jnp.int32)
    for which, shift in enumerate(shifts[:SWAPS]):
        number = jnp.where(offset == shift, which, number)
    members = []
    for c in range(COLS // LEV):
        part = number[:, c * LEV : (c + 1) * LEV]
        members.append(jnp.where(row == part, 1.0, 0.0))
    member = jnp.concatenate(members, axis=0)
    inside = dot(member.astype(BF), before)
    totals = jnp.sum(member, axis=1, keepdims=True)
    start = jnp.zeros((8, 1), F32)
    keys = []
    for c in range(COLS // LEV):
        block = slice(8 * c, 8 * c + 8)
        rank = inside[block] + start
        start = start + totals[block]
        key = jnp.sum(member[block] * (rank + row.astype(F32) * CAP), axis=0, keepdims=True)
        keys.append(key)
    return jnp.concatenate(keys, axis=1).astype(jnp.int32)


def spill_rows(place, offset, weights):
    row = lax.broadcasted_iota(jnp.int32, (8, COLS), 0)
    last = place == COLS - 1
    first_a = jnp.where(last, weights[2], jnp.where(place == COLS - 2, weights[3], 0.0))
    first_b = jnp.where(last, weights[3], 0.0)
    end = jnp.where(place == 0, weights[0], 0.0)
    rows = jnp.where(row == 0, first_a, jnp.where(row == 1, first_b, jnp.where(row == 7, end, 0.0)))
    spread = [jnp.where(offset == o, rows, 0.0) for o in range(-REACH, REACH + 1)]
    high, low = halves(jnp.concatenate(spread, axis=0))
    return jnp.concatenate([high, low], axis=0)


def meta_rows(place, fraction):
    a = fraction.astype(BF)
    rest = fraction - a.astype(F32)
    b = rest.astype(BF)
    c = rest - b.astype(F32)
    p_high = (place // 32).astype(F32)
    p_low = (place % 32).astype(F32)
    row = lax.broadcasted_iota(jnp.int32, (8, COLS), 0)
    out = jnp.where(row == 0, a.astype(F32), 0.0)
    out = jnp.where(row == 1, b.astype(F32), out)
    out = jnp.where(row == 2, c, out)
    out = jnp.where(row == 3, p_high, out)
    out = jnp.where(row == 4, p_low, out)
    return out.astype(BF)


def choose(keys, which):
    slot = lax.broadcasted_iota(jnp.int32, (CAP, COLS), 0).astype(jnp.int16)
    wanted = jnp.broadcast_to(keys - which * CAP, (16, COLS)).astype(jnp.int16)
    wanted = jnp.concatenate([wanted] * (CAP // 16), axis=0)
    return jnp.where(slot == wanted, BF(1.0), BF(0.0))


def spill_block(spilled, target):
    row = lax.broadcasted_iota(jnp.int32, (8, LEV), 0)
    from_cell = jnp.where(row < 2, target - 1, jnp.where(row == 7, target + 1, -9))
    out = jnp.zeros((8, LEV), F32)
    for o in range(-REACH, REACH + 1):
        block = spilled[8 * (o + REACH) : 8 * (o + REACH) + 8]
        out = out + jnp.where(from_cell == o, block, 0.0)
    return out


def spill_sums(spills, both):
    wide = dot(spills, both)
    count = 8 * (2 * REACH + 1)
    return (wide[:count, :LEV] + wide[:count, LEV:]) + (wide[count:, :LEV] + wide[count:, LEV:])


def index_values(self_ref, departure, fraction, tile_count):
    place, offset = locate(departure, self_ref[0], tile_count)
    keys = slots_of(offset, signs(self_ref[0]))
    weights = cubic_weights(fraction)
    return place, offset, keys, weights


def write_meta(meta_out, base, meta, one_hot):
    got = dot_nt(meta, one_hot)
    fraction = got[0:1] + got[1:2] + got[2:3]
    place = got[3:4] * 32.0 + got[4:5]
    for c in range(CAP // LEV):
        meta_out[base + c : base + c + 1, :] = fraction[:, c * LEV : (c + 1) * LEV]
        meta_out[base + 4 + c : base + 5 + c, :] = place[:, c * LEV : (c + 1) * LEV]


def pack_payload(out, one_hot, both, spilled, shift):
    wide = dot(one_hot, both)
    out[0:CAP, :] = wide[:, :LEV] + wide[:, LEV:]
    out[CAP : CAP + 8, :] = spill_block(spilled, shift)


def first_pack_kernel(tile_count, self_ref, field_hbm, departure_hbm, fraction_hbm, *refs):
    outs, (field, departure, fraction, sems) = refs[:-4], refs[-4:]
    copies = [
        pltpu.make_async_copy(departure_hbm, departure, sems.at[0]),
        pltpu.make_async_copy(fraction_hbm, fraction, sems.at[1]),
        pltpu.make_async_copy(field_hbm, field, sems.at[2]),
    ]
    for copy in copies:
        copy.start()
    copies[0].wait()
    copies[1].wait()
    place, offset, keys, weights = index_values(self_ref, departure[1:2, :], fraction[1:2, :], tile_count)
    meta = meta_rows(place, fraction[1:2, :])
    spills = spill_rows(place, offset, weights)
    copies[2].wait()
    high, low = halves(field[...])
    both = jnp.concatenate([high, low], axis=1)
    spilled = spill_sums(spills, both)
    shifts = signs(self_ref[0])
    outs[4][...] = spill_block(spilled, shifts[4])
    outs[5][...] = spill_block(spilled, shifts[5])
    outs[6][...] = spill_block(spilled, 0)
    for which, shift in enumerate(shifts[:SWAPS]):
        one_hot = choose(keys, which)
        pack_payload(outs[which], one_hot, both, spilled, shift)
        write_meta(outs[which], CAP + 8, meta, one_hot)


def index_kernel(tile_count, self_ref, departure, fraction, keys_out, spill_out, meta_out):
    place, offset, keys, weights = index_values(self_ref, departure[0:1, :], fraction[0:1, :], tile_count)
    meta = meta_rows(place, fraction[0:1, :])
    keys_out[...] = keys
    spill_out[...] = spill_rows(place, offset, weights)
    for which in range(SWAPS):
        write_meta(meta_out, 8 * which, meta, choose(keys, which))


def second_pack_kernel(self_ref, field, keys, spills, meta, *outs):
    high, low = halves(field[...])
    both = jnp.concatenate([high, low], axis=1)
    spilled = spill_sums(spills[...], both)
    shifts = signs(self_ref[0])
    outs[4][...] = spill_block(spilled, shifts[4])
    outs[5][...] = spill_block(spilled, shifts[5])
    outs[6][...] = spill_block(spilled, 0)
    for which, shift in enumerate(shifts[:SWAPS]):
        pack_payload(outs[which], choose(keys[...], which), both, spilled, shift)
        outs[which][CAP + 8 : CAP + 16, :] = meta[8 * which : 8 * which + 8, :]


BLOCK = 512
I16 = jnp.int16


def tiled(x, rows):
    return jnp.concatenate([x] * (rows // 16), axis=0)


def spread_table(place, weights):
    shape = (16, place.shape[1])
    start = jnp.broadcast_to(place - 1, shape).astype(I16)
    return start, [halves(jnp.broadcast_to(w, shape)) for w in weights]


def spread_block(first_cell, table):
    start, weights = table
    columns = start.shape[1]
    cells = lax.broadcasted_iota(jnp.int32, (BLOCK, columns), 0).astype(I16)
    first = jnp.full((16, columns), first_cell, jnp.int32).astype(I16)
    distance = cells - tiled(start - first, BLOCK)
    high = jnp.zeros((BLOCK, columns), BF)
    low = high
    for k in range(4):
        here = distance == I16(k)
        high = jnp.where(here, tiled(weights[k][0], BLOCK), high)
        low = jnp.where(here, tiled(weights[k][1], BLOCK), low)
    return high, low


def own_kernel(step, tile_count, self_ref, field, departure, fraction, spilled, tiny_a, tiny_b, out, both_ref):
    departure = departure[step : step + 1, :]
    fraction = fraction[step : step + 1, :]
    place, offset = locate(departure, self_ref[0], tile_count)
    table = spread_table(place, [jnp.where(offset == 0, w, 0.0) for w in cubic_weights(fraction)])
    high, low = halves(field[...])
    both_ref[:, :LEV] = high
    both_ref[:, LEV:] = low

    @pl.loop(0, COLS // BLOCK)
    def _(b):
        high, low = spread_block(b * BLOCK, table)
        wide = dot(high, both_ref[...]) + dot(low, both_ref[...])
        out[pl.ds(b * BLOCK, BLOCK), :] = wide[:, :LEV] + wide[:, LEV:]

    add_spill(out, spilled[...] + tiny_a[...] + tiny_b[...])


def add_spill(out, block):
    row = lax.broadcasted_iota(jnp.int32, (8, LEV), 0)
    out[0:8, :] = out[0:8, :] + jnp.where(row < 2, block, 0.0)
    out[COLS - 8 : COLS, :] = out[COLS - 8 : COLS, :] + jnp.where(row == 7, block, 0.0)


def deposit_sums(start, payloads, out, both_ref):
    tables = []
    for which, payload in enumerate(payloads):
        high, low = halves(payload[0:CAP, :])
        both_ref[which, :, :LEV] = high
        both_ref[which, :, LEV:] = low
        rows = [payload[CAP + 8 + c : CAP + 9 + c, :] for c in range(8)]
        fraction = jnp.concatenate(rows[:4], axis=1)
        place = jnp.concatenate(rows[4:], axis=1).astype(jnp.int32)
        tables.append(spread_table(place, cubic_weights(fraction)))

    @pl.loop(0, COLS // BLOCK)
    def _(b):
        wide = jnp.zeros((BLOCK, 2 * LEV), F32)
        for which, table in enumerate(tables):
            high, low = spread_block(b * BLOCK, table)
            wide = wide + dot(high, both_ref[which]) + dot(low, both_ref[which])
        out[pl.ds(b * BLOCK, BLOCK), :] = start[pl.ds(b * BLOCK, BLOCK), :] + wide[:, :LEV] + wide[:, LEV:]

    spill = payloads[0][CAP : CAP + 8, :]
    for payload in payloads[1:]:
        spill = spill + payload[CAP : CAP + 8, :]
    return spill


def near_kernel(start, p0, p1, out, both_ref):
    spill = deposit_sums(start, (p0, p1), out, both_ref)
    add_spill(out, spill)


def far_kernel(step, start, p0, p1, level_map, out, both_ref, sum_ref):
    spill = deposit_sums(start, (p0, p1), sum_ref, both_ref)
    add_spill(sum_ref, spill)
    map_high, map_low = halves(level_map[step])
    high, low = halves(sum_ref[...])
    out[...] = dot_nt(high, map_high) + (dot_nt(high, map_low) + dot_nt(low, map_high))


def couple_kernel(table, x, out):
    count = x.shape[0]

    @pl.loop(0, x.shape[1] // 8)
    def _(r):
        rows = [x[e, pl.ds(r * 8, 8), :] for e in range(count)]
        for b in range(count):
            total = rows[0] * table[count * b : count * b + 1, :]
            for e in range(1, count):
                total = total + rows[e] * table[count * b + e : count * b + e + 1, :]
            out[b, pl.ds(r * 8, 8), :] = total


VM = pl.BlockSpec(memory_space=pltpu.MemorySpace.VMEM)
HBM = pl.BlockSpec(memory_space=pltpu.MemorySpace.HBM)
SM = pl.BlockSpec(memory_space=pltpu.MemorySpace.SMEM)
PARAMS = pltpu.CompilerParams(vmem_limit_bytes=40 * 1024 * 1024)
PACKED = [jax.ShapeDtypeStruct((ROWS, LEV), F32)] * 4 + [jax.ShapeDtypeStruct((8, LEV), F32)] * 3


def call(kernel, out_shape, in_specs, scratch=(), flops=0):
    multiple = isinstance(out_shape, (list, tuple))
    return pl.pallas_call(
        kernel,
        out_shape=out_shape,
        in_specs=in_specs,
        out_specs=[VM] * len(out_shape) if multiple else VM,
        scratch_shapes=list(scratch),
        compiler_params=PARAMS,
        cost_estimate=pl.CostEstimate(flops=flops, transcendentals=0, bytes_accessed=flops // 256),
    )


def transported(step, packed, tile_count, tile_self, field, departure, fraction, level_map):
    tiny = [swapped(packed[w], w) for w in (4, 5)]
    far = [swapped(packed[w], w) for w in (0, 1)]
    near = [swapped(packed[w], w) for w in (2, 3)]
    total = jax.ShapeDtypeStruct((COLS, LEV), F32)
    work = 3 * 10**9
    own = call(
        functools.partial(own_kernel, step, tile_count),
        total,
        [SM] + [VM] * 6,
        [pltpu.VMEM((COLS, 2 * LEV), BF)],
        work,
    )(tile_self, field, departure, fraction, packed[6], *tiny)
    both = pltpu.VMEM((2, CAP, 2 * LEV), BF)
    summed = call(near_kernel, total, [VM] * 3, [both], work)(own, *near)
    return call(
        functools.partial(far_kernel, step),
        total,
        [VM] * 4,
        [both, pltpu.VMEM((COLS, LEV), F32)],
        work,
    )(summed, *far, level_map)


def body(adjoint_in, departure, fraction, level_map, coarse_map):
    tile_count = lax.axis_size("tile")
    groups = lax.axis_size("grp")
    tile_self = lax.axis_index("tile").astype(jnp.int32).reshape(1)
    first_scratch = [
        pltpu.VMEM((COLS, LEV), F32),
        pltpu.VMEM((2, COLS), jnp.int32),
        pltpu.VMEM((2, COLS), F32),
        pltpu.SemaphoreType.DMA((3,)),
    ]
    packed = call(functools.partial(first_pack_kernel, tile_count), PACKED, [SM, HBM, HBM, HBM], first_scratch)(
        tile_self, *[pltpu.with_memory_space_constraint(x, pltpu.MemorySpace.HBM) for x in (adjoint_in, departure, fraction)]
    )
    keys, spills, meta = call(
        functools.partial(index_kernel, tile_count),
        [
            jax.ShapeDtypeStruct((1, COLS), jnp.int32),
            jax.ShapeDtypeStruct((16 * (2 * REACH + 1), COLS), BF),
            jax.ShapeDtypeStruct((32, LEV), F32),
        ],
        [SM, VM, VM],
        (),
        2 * 10**9,
    )(tile_self, departure, fraction)
    table = coarse_map.transpose(1, 2, 0).reshape(groups * groups, LEV)
    second = transported(1, packed, tile_count, tile_self, adjoint_in, departure, fraction, level_map)

    parts = lax.all_to_all(second.reshape(groups, COLS // groups, LEV), "grp", 0, 0)
    mixed = call(couple_kernel, jax.ShapeDtypeStruct(parts.shape, F32), [VM, VM])(table, parts)
    coupled = lax.all_to_all(mixed, "grp", 0, 0).reshape(COLS, LEV)

    packed = call(second_pack_kernel, PACKED, [SM] + [VM] * 4)(tile_self, coupled, keys, spills, meta)
    return transported(0, packed, tile_count, tile_self, coupled, departure, fraction, level_map)


def solution(mesh):
    return jax.shard_map(
        body,
        mesh=mesh,
        in_specs=(
            P(("grp", "tile"), None),
            P(None, ("grp", "tile")),
            P(None, ("grp", "tile")),
            P(),
            P(),
        ),
        out_specs=P(("grp", "tile"), None),
        check_vma=False,
    )
```

```python
import functools

import jax
import jax.numpy as jnp
from jax import lax
from jax.experimental import pallas as pl
from jax.experimental.pallas import tpu as pltpu
from jax.sharding import PartitionSpec as P

REACH = 2
SWAPS = 4
COLS = 1024
LEV = 128
CAP = 512
ROWS = CAP + 16
BF = jnp.bfloat16
F32 = jnp.float32


def signs(tile):
    core = 1 - 2 * (tile % 2)
    chip = 1 - 2 * ((tile // 2) % 2)
    return (2 * chip, -2 * chip, -core, core, 3 * core, -3 * core)


def swapped(x, which):
    length = lax.axis_size("tile")
    return lax.ppermute(x, "tile", [(i, (i + signs(i)[which]) % length) for i in range(length)])


def halves(x):
    high = x.astype(BF)
    low = (x - high.astype(F32)).astype(BF)
    return high, low


def dot(a, b):
    return lax.dot_general(a, b, (((1,), (0,)), ((), ())), preferred_element_type=F32)


def dot_nt(a, b):
    return lax.dot_general(a, b, (((1,), (1,)), ((), ())), preferred_element_type=F32)


def cubic_weights(a):
    return (
        -a * (1.0 - a) * (2.0 - a) * (1.0 / 6.0),
        (1.0 + a) * (1.0 - a) * (2.0 - a) * 0.5,
        (1.0 + a) * a * (2.0 - a) * 0.5,
        -(1.0 + a) * a * (1.0 - a) * (1.0 / 6.0),
    )


def locate(departure, tile_self, tile_count):
    place = departure % COLS
    target = (departure // COLS) % tile_count
    offset = (target - tile_self + REACH + tile_count) % tile_count - REACH
    return place, offset


def slots_of(offset, shifts):
    row = lax.broadcasted_iota(jnp.int32, (8, LEV), 0)
    lane_a = lax.broadcasted_iota(jnp.int32, (LEV, LEV), 0)
    lane_b = lax.broadcasted_iota(jnp.int32, (LEV, LEV), 1)
    before = jnp.where(lane_a < lane_b, 1.0, 0.0).astype(BF)
    number = jnp.full((1, COLS), 4, jnp.int32)
    for which, shift in enumerate(shifts[:SWAPS]):
        number = jnp.where(offset == shift, which, number)
    members = []
    for c in range(COLS // LEV):
        part = number[:, c * LEV : (c + 1) * LEV]
        members.append(jnp.where(row == part, 1.0, 0.0))
    member = jnp.concatenate(members, axis=0)
    inside = dot(member.astype(BF), before)
    totals = jnp.sum(member, axis=1, keepdims=True)
    start = jnp.zeros((8, 1), F32)
    keys = []
    for c in range(COLS // LEV):
        block = slice(8 * c, 8 * c + 8)
        rank = inside[block] + start
        start = start + totals[block]
        key = jnp.sum(member[block] * (rank + row.astype(F32) * CAP), axis=0, keepdims=True)
        keys.append(key)
    return jnp.concatenate(keys, axis=1).astype(jnp.int32)


def spill_rows(place, offset, weights):
    row = lax.broadcasted_iota(jnp.int32, (8, COLS), 0)
    last = place == COLS - 1
    first_a = jnp.where(last, weights[2], jnp.where(place == COLS - 2, weights[3], 0.0))
    first_b = jnp.where(last, weights[3], 0.0)
    end = jnp.where(place == 0, weights[0], 0.0)
    rows = jnp.where(row == 0, first_a, jnp.where(row == 1, first_b, jnp.where(row == 7, end, 0.0)))
    spread = [jnp.where(offset == o, rows, 0.0) for o in range(-REACH, REACH + 1)]
    high, low = halves(jnp.concatenate(spread, axis=0))
    return jnp.concatenate([high, low], axis=0)


def meta_rows(place, fraction):
    a = fraction.astype(BF)
    rest = fraction - a.astype(F32)
    b = rest.astype(BF)
    c = rest - b.astype(F32)
    p_high = (place // 32).astype(F32)
    p_low = (place % 32).astype(F32)
    row = lax.broadcasted_iota(jnp.int32, (8, COLS), 0)
    out = jnp.where(row == 0, a.astype(F32), 0.0)
    out = jnp.where(row == 1, b.astype(F32), out)
    out = jnp.where(row == 2, c, out)
    out = jnp.where(row == 3, p_high, out)
    out = jnp.where(row == 4, p_low, out)
    return out.astype(BF)


def choose(keys, which):
    slot = lax.broadcasted_iota(jnp.int32, (CAP, COLS), 0).astype(jnp.int16)
    wanted = jnp.broadcast_to(keys - which * CAP, (16, COLS)).astype(jnp.int16)
    wanted = jnp.concatenate([wanted] * (CAP // 16), axis=0)
    return jnp.where(slot == wanted, BF(1.0), BF(0.0))


def spill_block(spilled, target):
    row = lax.broadcasted_iota(jnp.int32, (8, LEV), 0)
    from_cell = jnp.where(row < 2, target - 1, jnp.where(row == 7, target + 1, -9))
    out = jnp.zeros((8, LEV), F32)
    for o in range(-REACH, REACH + 1):
        block = spilled[8 * (o + REACH) : 8 * (o + REACH) + 8]
        out = out + jnp.where(from_cell == o, block, 0.0)
    return out


def spill_sums(spills, both):
    wide = dot(spills, both)
    count = 8 * (2 * REACH + 1)
    return (wide[:count, :LEV] + wide[:count, LEV:]) + (wide[count:, :LEV] + wide[count:, LEV:])


def index_values(self_ref, departure, fraction, tile_count):
    place, offset = locate(departure, self_ref[0], tile_count)
    keys = slots_of(offset, signs(self_ref[0]))
    weights = cubic_weights(fraction)
    return place, offset, keys, weights


def write_meta(meta_out, base, meta, one_hot):
    got = dot_nt(meta, one_hot)
    fraction = got[0:1] + got[1:2] + got[2:3]
    place = got[3:4] * 32.0 + got[4:5]
    for c in range(CAP // LEV):
        meta_out[base + c : base + c + 1, :] = fraction[:, c * LEV : (c + 1) * LEV]
        meta_out[base + 4 + c : base + 5 + c, :] = place[:, c * LEV : (c + 1) * LEV]


def pack_payload(out, one_hot, both, spilled, shift):
    wide = dot(one_hot, both)
    out[0:CAP, :] = wide[:, :LEV] + wide[:, LEV:]
    out[CAP : CAP + 8, :] = spill_block(spilled, shift)


def first_pack_kernel(tile_count, self_ref, field_hbm, departure_hbm, fraction_hbm, *refs):
    outs, (field, departure, fraction, sems) = refs[:-4], refs[-4:]
    copies = [
        pltpu.make_async_copy(departure_hbm, departure, sems.at[0]),
        pltpu.make_async_copy(fraction_hbm, fraction, sems.at[1]),
        pltpu.make_async_copy(field_hbm, field, sems.at[2]),
    ]
    for copy in copies:
        copy.start()
    copies[0].wait()
    copies[1].wait()
    place, offset, keys, weights = index_values(self_ref, departure[1:2, :], fraction[1:2, :], tile_count)
    meta = meta_rows(place, fraction[1:2, :])
    spills = spill_rows(place, offset, weights)
    copies[2].wait()
    high, low = halves(field[...])
    both = jnp.concatenate([high, low], axis=1)
    spilled = spill_sums(spills, both)
    shifts = signs(self_ref[0])
    outs[4][...] = spill_block(spilled, shifts[4])
    outs[5][...] = spill_block(spilled, shifts[5])
    outs[6][...] = spill_block(spilled, 0)
    for which, shift in enumerate(shifts[:SWAPS]):
        one_hot = choose(keys, which)
        pack_payload(outs[which], one_hot, both, spilled, shift)
        write_meta(outs[which], CAP + 8, meta, one_hot)


def index_kernel(tile_count, self_ref, departure, fraction, keys_out, spill_out, meta_out):
    place, offset, keys, weights = index_values(self_ref, departure[0:1, :], fraction[0:1, :], tile_count)
    meta = meta_rows(place, fraction[0:1, :])
    keys_out[...] = keys
    spill_out[...] = spill_rows(place, offset, weights)
    for which in range(SWAPS):
        write_meta(meta_out, 8 * which, meta, choose(keys, which))


def second_pack_kernel(self_ref, field, keys, spills, meta, *outs):
    high, low = halves(field[...])
    both = jnp.concatenate([high, low], axis=1)
    spilled = spill_sums(spills[...], both)
    shifts = signs(self_ref[0])
    outs[4][...] = spill_block(spilled, shifts[4])
    outs[5][...] = spill_block(spilled, shifts[5])
    outs[6][...] = spill_block(spilled, 0)
    for which, shift in enumerate(shifts[:SWAPS]):
        pack_payload(outs[which], choose(keys[...], which), both, spilled, shift)
        outs[which][CAP + 8 : CAP + 16, :] = meta[8 * which : 8 * which + 8, :]


BLOCK = 512
I16 = jnp.int16


def tiled(x, rows):
    return jnp.concatenate([x] * (rows // 16), axis=0)


def spread_table(place, weights):
    shape = (16, place.shape[1])
    start = jnp.broadcast_to(place - 1, shape).astype(I16)
    return start, [halves(jnp.broadcast_to(w, shape)) for w in weights]


def spread_block(first_cell, table):
    start, weights = table
    columns = start.shape[1]
    cells = lax.broadcasted_iota(jnp.int32, (BLOCK, columns), 0).astype(I16)
    first = jnp.full((16, columns), first_cell, jnp.int32).astype(I16)
    distance = cells - tiled(start - first, BLOCK)
    high = jnp.zeros((BLOCK, columns), BF)
    low = high
    for k in range(4):
        here = distance == I16(k)
        high = jnp.where(here, tiled(weights[k][0], BLOCK), high)
        low = jnp.where(here, tiled(weights[k][1], BLOCK), low)
    return high, low


def own_kernel(step, tile_count, self_ref, field, departure, fraction, spilled, tiny_a, tiny_b, out, both_ref):
    departure = departure[step : step + 1, :]
    fraction = fraction[step : step + 1, :]
    place, offset = locate(departure, self_ref[0], tile_count)
    table = spread_table(place, [jnp.where(offset == 0, w, 0.0) for w in cubic_weights(fraction)])
    high, low = halves(field[...])
    both_ref[:, :LEV] = high
    both_ref[:, LEV:] = low

    @pl.loop(0, COLS // BLOCK)
    def _(b):
        high, low = spread_block(b * BLOCK, table)
        wide = dot(high, both_ref[...]) + dot(low, both_ref[...])
        out[pl.ds(b * BLOCK, BLOCK), :] = wide[:, :LEV] + wide[:, LEV:]

    add_spill(out, spilled[...] + tiny_a[...] + tiny_b[...])


def add_spill(out, block):
    row = lax.broadcasted_iota(jnp.int32, (8, LEV), 0)
    out[0:8, :] = out[0:8, :] + jnp.where(row < 2, block, 0.0)
    out[COLS - 8 : COLS, :] = out[COLS - 8 : COLS, :] + jnp.where(row == 7, block, 0.0)


def deposit_sums(start, payloads, out, both_ref):
    tables = []
    for which, payload in enumerate(payloads):
        high, low = halves(payload[0:CAP, :])
        both_ref[which, :, :LEV] = high
        both_ref[which, :, LEV:] = low
        rows = [payload[CAP + 8 + c : CAP + 9 + c, :] for c in range(8)]
        fraction = jnp.concatenate(rows[:4], axis=1)
        place = jnp.concatenate(rows[4:], axis=1).astype(jnp.int32)
        tables.append(spread_table(place, cubic_weights(fraction)))

    @pl.loop(0, COLS // BLOCK)
    def _(b):
        wide = jnp.zeros((BLOCK, 2 * LEV), F32)
        for which, table in enumerate(tables):
            high, low = spread_block(b * BLOCK, table)
            wide = wide + dot(high, both_ref[which]) + dot(low, both_ref[which])
        out[pl.ds(b * BLOCK, BLOCK), :] = start[pl.ds(b * BLOCK, BLOCK), :] + wide[:, :LEV] + wide[:, LEV:]

    spill = payloads[0][CAP : CAP + 8, :]
    for payload in payloads[1:]:
        spill = spill + payload[CAP : CAP + 8, :]
    return spill


def middle_kernel(start, p0, p1, p2, out, both_ref):
    add_spill(out, deposit_sums(start, (p0, p1, p2), out, both_ref))


def last_kernel(step, start, payload, level_map, out, both_ref, sum_ref):
    add_spill(sum_ref, deposit_sums(start, (payload,), sum_ref, both_ref))
    map_high, map_low = halves(level_map[step])
    high, low = halves(sum_ref[...])
    out[...] = dot_nt(high, map_high) + (dot_nt(high, map_low) + dot_nt(low, map_high))


def couple_kernel(table, x, out):
    count = x.shape[0]

    @pl.loop(0, x.shape[1] // 8)
    def _(r):
        rows = [x[e, pl.ds(r * 8, 8), :] for e in range(count)]
        for b in range(count):
            total = rows[0] * table[count * b : count * b + 1, :]
            for e in range(1, count):
                total = total + rows[e] * table[count * b + e : count * b + e + 1, :]
            out[b, pl.ds(r * 8, 8), :] = total


VM = pl.BlockSpec(memory_space=pltpu.MemorySpace.VMEM)
HBM = pl.BlockSpec(memory_space=pltpu.MemorySpace.HBM)
SM = pl.BlockSpec(memory_space=pltpu.MemorySpace.SMEM)
PARAMS = pltpu.CompilerParams(vmem_limit_bytes=40 * 1024 * 1024)
PACKED = [jax.ShapeDtypeStruct((ROWS, LEV), F32)] * 4 + [jax.ShapeDtypeStruct((8, LEV), F32)] * 3


def call(kernel, out_shape, in_specs, scratch=(), flops=0):
    multiple = isinstance(out_shape, (list, tuple))
    return pl.pallas_call(
        kernel,
        out_shape=out_shape,
        in_specs=in_specs,
        out_specs=[VM] * len(out_shape) if multiple else VM,
        scratch_shapes=list(scratch),
        compiler_params=PARAMS,
        cost_estimate=pl.CostEstimate(flops=flops, transcendentals=0, bytes_accessed=flops // 256),
    )


def transported(step, packed, tile_count, tile_self, field, departure, fraction, level_map):
    tiny = [swapped(packed[w], w) for w in (4, 5)]
    far = [swapped(packed[w], w) for w in (0, 1)]
    cross = swapped(packed[2], 2)
    partner = swapped(packed[3], 3)
    total = jax.ShapeDtypeStruct((COLS, LEV), F32)
    work = 3 * 10**9
    own = call(
        functools.partial(own_kernel, step, tile_count),
        total,
        [SM] + [VM] * 6,
        [pltpu.VMEM((COLS, 2 * LEV), BF)],
        work,
    )(tile_self, field, departure, fraction, packed[6], *tiny)
    summed = call(middle_kernel, total, [VM] * 4, [pltpu.VMEM((3, CAP, 2 * LEV), BF)], work)(own, *far, partner)
    return call(
        functools.partial(last_kernel, step),
        total,
        [VM] * 3,
        [pltpu.VMEM((1, CAP, 2 * LEV), BF), pltpu.VMEM((COLS, LEV), F32)],
        work,
    )(summed, cross, level_map)


def body(adjoint_in, departure, fraction, level_map, coarse_map):
    tile_count = lax.axis_size("tile")
    groups = lax.axis_size("grp")
    tile_self = lax.axis_index("tile").astype(jnp.int32).reshape(1)
    first_scratch = [
        pltpu.VMEM((COLS, LEV), F32),
        pltpu.VMEM((2, COLS), jnp.int32),
        pltpu.VMEM((2, COLS), F32),
        pltpu.SemaphoreType.DMA((3,)),
    ]
    packed = call(functools.partial(first_pack_kernel, tile_count), PACKED, [SM, HBM, HBM, HBM], first_scratch)(
        tile_self, *[pltpu.with_memory_space_constraint(x, pltpu.MemorySpace.HBM) for x in (adjoint_in, departure, fraction)]
    )
    keys, spills, meta = call(
        functools.partial(index_kernel, tile_count),
        [
            jax.ShapeDtypeStruct((1, COLS), jnp.int32),
            jax.ShapeDtypeStruct((16 * (2 * REACH + 1), COLS), BF),
            jax.ShapeDtypeStruct((32, LEV), F32),
        ],
        [SM, VM, VM],
        (),
        2 * 10**9,
    )(tile_self, departure, fraction)
    table = coarse_map.transpose(1, 2, 0).reshape(groups * groups, LEV)
    second = transported(1, packed, tile_count, tile_self, adjoint_in, departure, fraction, level_map)

    parts = lax.all_to_all(second.reshape(groups, COLS // groups, LEV), "grp", 0, 0)
    mixed = call(couple_kernel, jax.ShapeDtypeStruct(parts.shape, F32), [VM, VM])(table, parts)
    coupled = lax.all_to_all(mixed, "grp", 0, 0).reshape(COLS, LEV)

    packed = call(second_pack_kernel, PACKED, [SM] + [VM] * 4)(tile_self, coupled, keys, spills, meta)
    return transported(0, packed, tile_count, tile_self, coupled, departure, fraction, level_map)


def solution(mesh):
    return jax.shard_map(
        body,
        mesh=mesh,
        in_specs=(
            P(("grp", "tile"), None),
            P(None, ("grp", "tile")),
            P(None, ("grp", "tile")),
            P(),
            P(),
        ),
        out_specs=P(("grp", "tile"), None),
        check_vma=False,
    )
```

```python
import functools

import jax
import jax.numpy as jnp
from jax import lax
from jax.experimental import pallas as pl
from jax.experimental.pallas import tpu as pltpu
from jax.sharding import PartitionSpec as P

REACH = 2
SWAPS = 4
COLS = 1024
LEV = 128
CAP = 512
ROWS = CAP + 16
BF = jnp.bfloat16
F32 = jnp.float32


def signs(tile):
    core = 1 - 2 * (tile % 2)
    chip = 1 - 2 * ((tile // 2) % 2)
    return (2 * chip, -2 * chip, -core, core, 3 * core, -3 * core)


def swapped(x, which):
    length = lax.axis_size("tile")
    return lax.ppermute(x, "tile", [(i, (i + signs(i)[which]) % length) for i in range(length)])


def halves(x):
    high = x.astype(BF)
    low = (x - high.astype(F32)).astype(BF)
    return high, low


def dot(a, b):
    return lax.dot_general(a, b, (((1,), (0,)), ((), ())), preferred_element_type=F32)


def dot_nt(a, b):
    return lax.dot_general(a, b, (((1,), (1,)), ((), ())), preferred_element_type=F32)


def cubic_weights(a):
    return (
        -a * (1.0 - a) * (2.0 - a) * (1.0 / 6.0),
        (1.0 + a) * (1.0 - a) * (2.0 - a) * 0.5,
        (1.0 + a) * a * (2.0 - a) * 0.5,
        -(1.0 + a) * a * (1.0 - a) * (1.0 / 6.0),
    )


def locate(departure, tile_self, tile_count):
    place = departure % COLS
    target = (departure // COLS) % tile_count
    offset = (target - tile_self + REACH + tile_count) % tile_count - REACH
    return place, offset


def slots_of(offset, shifts):
    row = lax.broadcasted_iota(jnp.int32, (8, LEV), 0)
    lane_a = lax.broadcasted_iota(jnp.int32, (LEV, LEV), 0)
    lane_b = lax.broadcasted_iota(jnp.int32, (LEV, LEV), 1)
    before = jnp.where(lane_a < lane_b, 1.0, 0.0).astype(BF)
    number = jnp.full((1, COLS), 4, jnp.int32)
    for which, shift in enumerate(shifts[:SWAPS]):
        number = jnp.where(offset == shift, which, number)
    members = []
    for c in range(COLS // LEV):
        part = number[:, c * LEV : (c + 1) * LEV]
        members.append(jnp.where(row == part, 1.0, 0.0))
    member = jnp.concatenate(members, axis=0)
    inside = dot(member.astype(BF), before)
    totals = jnp.sum(member, axis=1, keepdims=True)
    start = jnp.zeros((8, 1), F32)
    keys = []
    for c in range(COLS // LEV):
        block = slice(8 * c, 8 * c + 8)
        rank = inside[block] + start
        start = start + totals[block]
        key = jnp.sum(member[block] * (rank + row.astype(F32) * CAP), axis=0, keepdims=True)
        keys.append(key)
    return jnp.concatenate(keys, axis=1).astype(jnp.int32)


def spill_rows(place, offset, weights):
    row = lax.broadcasted_iota(jnp.int32, (8, COLS), 0)
    last = place == COLS - 1
    first_a = jnp.where(last, weights[2], jnp.where(place == COLS - 2, weights[3], 0.0))
    first_b = jnp.where(last, weights[3], 0.0)
    end = jnp.where(place == 0, weights[0], 0.0)
    rows = jnp.where(row == 0, first_a, jnp.where(row == 1, first_b, jnp.where(row == 7, end, 0.0)))
    spread = [jnp.where(offset == o, rows, 0.0) for o in range(-REACH, REACH + 1)]
    high, low = halves(jnp.concatenate(spread, axis=0))
    return jnp.concatenate([high, low], axis=0)


def meta_rows(place, fraction):
    a = fraction.astype(BF)
    rest = fraction - a.astype(F32)
    b = rest.astype(BF)
    c = rest - b.astype(F32)
    p_high = (place // 32).astype(F32)
    p_low = (place % 32).astype(F32)
    row = lax.broadcasted_iota(jnp.int32, (8, COLS), 0)
    out = jnp.where(row == 0, a.astype(F32), 0.0)
    out = jnp.where(row == 1, b.astype(F32), out)
    out = jnp.where(row == 2, c, out)
    out = jnp.where(row == 3, p_high, out)
    out = jnp.where(row == 4, p_low, out)
    return out.astype(BF)


def choose(keys, which):
    slot = lax.broadcasted_iota(jnp.int32, (CAP, COLS), 0).astype(jnp.int16)
    wanted = jnp.broadcast_to(keys - which * CAP, (16, COLS)).astype(jnp.int16)
    wanted = jnp.concatenate([wanted] * (CAP // 16), axis=0)
    return jnp.where(slot == wanted, BF(1.0), BF(0.0))


def spill_block(spilled, target):
    row = lax.broadcasted_iota(jnp.int32, (8, LEV), 0)
    from_cell = jnp.where(row < 2, target - 1, jnp.where(row == 7, target + 1, -9))
    out = jnp.zeros((8, LEV), F32)
    for o in range(-REACH, REACH + 1):
        block = spilled[8 * (o + REACH) : 8 * (o + REACH) + 8]
        out = out + jnp.where(from_cell == o, block, 0.0)
    return out


def spill_sums(spills, both):
    wide = dot(spills, both)
    count = 8 * (2 * REACH + 1)
    return (wide[:count, :LEV] + wide[:count, LEV:]) + (wide[count:, :LEV] + wide[count:, LEV:])


def index_values(self_ref, departure, fraction, tile_count):
    place, offset = locate(departure, self_ref[0], tile_count)
    keys = slots_of(offset, signs(self_ref[0]))
    weights = cubic_weights(fraction)
    return place, offset, keys, weights


def write_meta(meta_out, base, meta, one_hot):
    got = dot_nt(meta, one_hot)
    fraction = got[0:1] + got[1:2] + got[2:3]
    place = got[3:4] * 32.0 + got[4:5]
    for c in range(CAP // LEV):
        meta_out[base + c : base + c + 1, :] = fraction[:, c * LEV : (c + 1) * LEV]
        meta_out[base + 4 + c : base + 5 + c, :] = place[:, c * LEV : (c + 1) * LEV]


def pack_payload(out, one_hot, both, spilled, shift):
    wide = dot(one_hot, both)
    out[0:CAP, :] = wide[:, :LEV] + wide[:, LEV:]
    out[CAP : CAP + 8, :] = spill_block(spilled, shift)


def first_pack_kernel(tile_count, self_ref, field_hbm, departure_hbm, fraction_hbm, *refs):
    outs, (field, departure, fraction, sems) = refs[:-4], refs[-4:]
    copies = [
        pltpu.make_async_copy(departure_hbm, departure, sems.at[0]),
        pltpu.make_async_copy(fraction_hbm, fraction, sems.at[1]),
        pltpu.make_async_copy(field_hbm, field, sems.at[2]),
    ]
    for copy in copies:
        copy.start()
    copies[0].wait()
    copies[1].wait()
    place, offset, keys, weights = index_values(self_ref, departure[1:2, :], fraction[1:2, :], tile_count)
    meta = meta_rows(place, fraction[1:2, :])
    spills = spill_rows(place, offset, weights)
    copies[2].wait()
    high, low = halves(field[...])
    both = jnp.concatenate([high, low], axis=1)
    spilled = spill_sums(spills, both)
    shifts = signs(self_ref[0])
    outs[4][...] = spill_block(spilled, shifts[4])
    outs[5][...] = spill_block(spilled, shifts[5])
    outs[6][...] = spill_block(spilled, 0)
    for which, shift in enumerate(shifts[:SWAPS]):
        one_hot = choose(keys, which)
        pack_payload(outs[which], one_hot, both, spilled, shift)
        write_meta(outs[which], CAP + 8, meta, one_hot)


def index_kernel(tile_count, self_ref, departure, fraction, keys_out, spill_out, meta_out):
    place, offset, keys, weights = index_values(self_ref, departure[0:1, :], fraction[0:1, :], tile_count)
    meta = meta_rows(place, fraction[0:1, :])
    keys_out[...] = keys
    spill_out[...] = spill_rows(place, offset, weights)
    for which in range(SWAPS):
        write_meta(meta_out, 8 * which, meta, choose(keys, which))


def second_pack_kernel(self_ref, field, keys, spills, meta, *outs):
    high, low = halves(field[...])
    both = jnp.concatenate([high, low], axis=1)
    spilled = spill_sums(spills[...], both)
    shifts = signs(self_ref[0])
    outs[4][...] = spill_block(spilled, shifts[4])
    outs[5][...] = spill_block(spilled, shifts[5])
    outs[6][...] = spill_block(spilled, 0)
    for which, shift in enumerate(shifts[:SWAPS]):
        pack_payload(outs[which], choose(keys[...], which), both, spilled, shift)
        outs[which][CAP + 8 : CAP + 16, :] = meta[8 * which : 8 * which + 8, :]


BLOCK = 512
I16 = jnp.int16


def tiled(x, rows):
    return jnp.concatenate([x] * (rows // 16), axis=0)


def spread_table(place, weights):
    shape = (16, place.shape[1])
    start = jnp.broadcast_to(place - 1, shape).astype(I16)
    return start, [halves(jnp.broadcast_to(w, shape)) for w in weights]


def spread_block(first_cell, table):
    start, weights = table
    columns = start.shape[1]
    cells = lax.broadcasted_iota(jnp.int32, (BLOCK, columns), 0).astype(I16)
    first = jnp.full((16, columns), first_cell, jnp.int32).astype(I16)
    distance = cells - tiled(start - first, BLOCK)
    high = jnp.zeros((BLOCK, columns), BF)
    low = high
    for k in range(4):
        here = distance == I16(k)
        high = jnp.where(here, tiled(weights[k][0], BLOCK), high)
        low = jnp.where(here, tiled(weights[k][1], BLOCK), low)
    return high, low


def own_kernel(step, tile_count, self_ref, field, departure, fraction, spilled, payload, out, own_ref, both_ref):
    departure = departure[step : step + 1, :]
    fraction = fraction[step : step + 1, :]
    place, offset = locate(departure, self_ref[0], tile_count)
    own_table = spread_table(place, [jnp.where(offset == 0, w, 0.0) for w in cubic_weights(fraction)])
    high, low = halves(field[...])
    own_ref[:, :LEV] = high
    own_ref[:, LEV:] = low
    table = payload_table(payload, both_ref, 0)

    @pl.loop(0, COLS // BLOCK)
    def _(b):
        high, low = spread_block(b * BLOCK, own_table)
        wide = dot(high, own_ref[...]) + dot(low, own_ref[...])
        high, low = spread_block(b * BLOCK, table)
        wide = wide + dot(high, both_ref[0]) + dot(low, both_ref[0])
        out[pl.ds(b * BLOCK, BLOCK), :] = wide[:, :LEV] + wide[:, LEV:]

    add_spill(out, spilled[...] + payload[CAP : CAP + 8, :])


def payload_table(payload, both_ref, which):
    high, low = halves(payload[0:CAP, :])
    both_ref[which, :, :LEV] = high
    both_ref[which, :, LEV:] = low
    rows = [payload[CAP + 8 + c : CAP + 9 + c, :] for c in range(8)]
    fraction = jnp.concatenate(rows[:4], axis=1)
    place = jnp.concatenate(rows[4:], axis=1).astype(jnp.int32)
    return spread_table(place, cubic_weights(fraction))


def add_spill(out, block):
    row = lax.broadcasted_iota(jnp.int32, (8, LEV), 0)
    out[0:8, :] = out[0:8, :] + jnp.where(row < 2, block, 0.0)
    out[COLS - 8 : COLS, :] = out[COLS - 8 : COLS, :] + jnp.where(row == 7, block, 0.0)


def deposit_block(b, start, tables, both_ref):
    wide = jnp.zeros((BLOCK, 2 * LEV), F32)
    for which, table in enumerate(tables):
        high, low = spread_block(b * BLOCK, table)
        wide = wide + dot(high, both_ref[which]) + dot(low, both_ref[which])
    return start[pl.ds(b * BLOCK, BLOCK), :] + wide[:, :LEV] + wide[:, LEV:]


def middle_kernel(start, p0, p1, out, both_ref):
    tables = [payload_table(p, both_ref, which) for which, p in enumerate((p0, p1))]

    @pl.loop(0, COLS // BLOCK)
    def _(b):
        out[pl.ds(b * BLOCK, BLOCK), :] = deposit_block(b, start, tables, both_ref)

    add_spill(out, p0[CAP : CAP + 8, :] + p1[CAP : CAP + 8, :])


def last_kernel(step, start, payload, tiny_a, tiny_b, level_map, out, both_ref, sum_ref, lifted_ref, sems):
    table = payload_table(payload, both_ref, 0)
    spill = payload[CAP : CAP + 8, :] + tiny_a[...] + tiny_b[...]
    row = lax.broadcasted_iota(jnp.int32, (8, LEV), 0)
    map_high, map_low = halves(level_map[step])

    def copy(b):
        rows = pl.ds(b * BLOCK, BLOCK)
        return pltpu.make_async_copy(lifted_ref.at[rows, :], out.at[rows, :], sems.at[b])

    for b in range(COLS // BLOCK):
        sum_ref[...] = deposit_block(b, start, (table,), both_ref)
        if b == 0:
            sum_ref[0:8, :] = sum_ref[0:8, :] + jnp.where(row < 2, spill, 0.0)
        if b == COLS // BLOCK - 1:
            sum_ref[BLOCK - 8 : BLOCK, :] = sum_ref[BLOCK - 8 : BLOCK, :] + jnp.where(row == 7, spill, 0.0)
        high, low = halves(sum_ref[...])
        lifted = dot_nt(high, map_high) + (dot_nt(high, map_low) + dot_nt(low, map_high))
        if step == 0:
            lifted_ref[b * BLOCK : (b + 1) * BLOCK, :] = lifted
            copy(b).start()
        else:
            out[b * BLOCK : (b + 1) * BLOCK, :] = lifted
    if step == 0:
        for b in range(COLS // BLOCK):
            copy(b).wait()


def couple_kernel(table, x, out):
    count = x.shape[0]

    @pl.loop(0, x.shape[1] // 8)
    def _(r):
        rows = [x[e, pl.ds(r * 8, 8), :] for e in range(count)]
        for b in range(count):
            total = rows[0] * table[count * b : count * b + 1, :]
            for e in range(1, count):
                total = total + rows[e] * table[count * b + e : count * b + e + 1, :]
            out[b, pl.ds(r * 8, 8), :] = total


VM = pl.BlockSpec(memory_space=pltpu.MemorySpace.VMEM)
HBM = pl.BlockSpec(memory_space=pltpu.MemorySpace.HBM)
SM = pl.BlockSpec(memory_space=pltpu.MemorySpace.SMEM)
PARAMS = pltpu.CompilerParams(vmem_limit_bytes=40 * 1024 * 1024)
PACKED = [jax.ShapeDtypeStruct((ROWS, LEV), F32)] * 4 + [jax.ShapeDtypeStruct((8, LEV), F32)] * 3


def call(kernel, out_shape, in_specs, scratch=(), flops=0, out_spec=None):
    multiple = isinstance(out_shape, (list, tuple))
    return pl.pallas_call(
        kernel,
        out_shape=out_shape,
        in_specs=in_specs,
        out_specs=[VM] * len(out_shape) if multiple else out_spec or VM,
        scratch_shapes=list(scratch),
        compiler_params=PARAMS,
        cost_estimate=pl.CostEstimate(flops=flops, transcendentals=0, bytes_accessed=flops // 256),
    )


def transported(step, packed, tile_count, tile_self, field, departure, fraction, level_map):
    far = [swapped(packed[w], w) for w in (0, 1)]
    partner = swapped(packed[3], 3)
    cross = swapped(packed[2], 2)
    late = lax.optimization_barrier((packed[4], packed[5], partner))
    tiny = [swapped(late[w - 4], w) for w in (4, 5)]
    total = jax.ShapeDtypeStruct((COLS, LEV), F32)
    one = pltpu.VMEM((1, CAP, 2 * LEV), BF)
    work = 3 * 10**9
    own = call(
        functools.partial(own_kernel, step, tile_count),
        total,
        [SM] + [VM] * 5,
        [pltpu.VMEM((COLS, 2 * LEV), BF), one],
        work,
    )(tile_self, field, departure, fraction, packed[6], partner)
    summed = call(middle_kernel, total, [VM] * 3, [pltpu.VMEM((2, CAP, 2 * LEV), BF)], work)(own, *far)
    return call(
        functools.partial(last_kernel, step),
        total,
        [VM] * 5,
        [
            one,
            pltpu.VMEM((BLOCK, LEV), F32),
            pltpu.VMEM((COLS, LEV), F32),
            pltpu.SemaphoreType.DMA((COLS // BLOCK,)),
        ],
        work,
        HBM if step == 0 else VM,
    )(summed, cross, *tiny, level_map)


def body(adjoint_in, departure, fraction, level_map, coarse_map):
    tile_count = lax.axis_size("tile")
    groups = lax.axis_size("grp")
    tile_self = lax.axis_index("tile").astype(jnp.int32).reshape(1)
    first_scratch = [
        pltpu.VMEM((COLS, LEV), F32),
        pltpu.VMEM((2, COLS), jnp.int32),
        pltpu.VMEM((2, COLS), F32),
        pltpu.SemaphoreType.DMA((3,)),
    ]
    packed = call(functools.partial(first_pack_kernel, tile_count), PACKED, [SM, HBM, HBM, HBM], first_scratch)(
        tile_self, *[pltpu.with_memory_space_constraint(x, pltpu.MemorySpace.HBM) for x in (adjoint_in, departure, fraction)]
    )
    keys, spills, meta = call(
        functools.partial(index_kernel, tile_count),
        [
            jax.ShapeDtypeStruct((1, COLS), jnp.int32),
            jax.ShapeDtypeStruct((16 * (2 * REACH + 1), COLS), BF),
            jax.ShapeDtypeStruct((32, LEV), F32),
        ],
        [SM, VM, VM],
        (),
        2 * 10**9,
    )(tile_self, departure, fraction)
    table = coarse_map.transpose(1, 2, 0).reshape(groups * groups, LEV)
    second = transported(1, packed, tile_count, tile_self, adjoint_in, departure, fraction, level_map)

    parts = lax.all_to_all(second.reshape(groups, COLS // groups, LEV), "grp", 0, 0)
    mixed = call(couple_kernel, jax.ShapeDtypeStruct(parts.shape, F32), [VM, VM])(table, parts)
    coupled = lax.all_to_all(mixed, "grp", 0, 0).reshape(COLS, LEV)

    packed = call(second_pack_kernel, PACKED, [SM] + [VM] * 4)(tile_self, coupled, keys, spills, meta)
    return transported(0, packed, tile_count, tile_self, coupled, departure, fraction, level_map)


def solution(mesh):
    return jax.shard_map(
        body,
        mesh=mesh,
        in_specs=(
            P(("grp", "tile"), None),
            P(None, ("grp", "tile")),
            P(None, ("grp", "tile")),
            P(),
            P(),
        ),
        out_specs=P(("grp", "tile"), None),
        check_vma=False,
    )
```

```python
import functools

import jax
import jax.numpy as jnp
from jax import lax
from jax.experimental import pallas as pl
from jax.experimental.pallas import tpu as pltpu
from jax.sharding import PartitionSpec as P

REACH = 2
SWAPS = 4
COLS = 1024
LEV = 128
CAP = 512
ROWS = CAP + 16
WIDE_ROWS = CAP + 24
BF = jnp.bfloat16
F32 = jnp.float32


def signs(tile):
    core = 1 - 2 * (tile % 2)
    chip = 1 - 2 * ((tile // 2) % 2)
    return (2 * chip, -2 * chip, -core, core, 3 * core, -3 * core)


def swapped(x, which):
    length = lax.axis_size("tile")
    return lax.ppermute(x, "tile", [(i, (i + signs(i)[which]) % length) for i in range(length)])


def halves(x):
    high = x.astype(BF)
    low = (x - high.astype(F32)).astype(BF)
    return high, low


def dot(a, b):
    return lax.dot_general(a, b, (((1,), (0,)), ((), ())), preferred_element_type=F32)


def dot_nt(a, b):
    return lax.dot_general(a, b, (((1,), (1,)), ((), ())), preferred_element_type=F32)


def cubic_weights(a):
    return (
        -a * (1.0 - a) * (2.0 - a) * (1.0 / 6.0),
        (1.0 + a) * (1.0 - a) * (2.0 - a) * 0.5,
        (1.0 + a) * a * (2.0 - a) * 0.5,
        -(1.0 + a) * a * (1.0 - a) * (1.0 / 6.0),
    )


def locate(departure, tile_self, tile_count):
    place = departure % COLS
    target = (departure // COLS) % tile_count
    offset = (target - tile_self + REACH + tile_count) % tile_count - REACH
    return place, offset


def slots_of(offset, shifts):
    row = lax.broadcasted_iota(jnp.int32, (8, LEV), 0)
    lane_a = lax.broadcasted_iota(jnp.int32, (LEV, LEV), 0)
    lane_b = lax.broadcasted_iota(jnp.int32, (LEV, LEV), 1)
    before = jnp.where(lane_a < lane_b, 1.0, 0.0).astype(BF)
    number = jnp.full((1, COLS), 4, jnp.int32)
    for which, shift in enumerate(shifts[:SWAPS]):
        number = jnp.where(offset == shift, which, number)
    members = []
    for c in range(COLS // LEV):
        part = number[:, c * LEV : (c + 1) * LEV]
        members.append(jnp.where(row == part, 1.0, 0.0))
    member = jnp.concatenate(members, axis=0)
    inside = dot(member.astype(BF), before)
    totals = jnp.sum(member, axis=1, keepdims=True)
    start = jnp.zeros((8, 1), F32)
    keys = []
    for c in range(COLS // LEV):
        block = slice(8 * c, 8 * c + 8)
        rank = inside[block] + start
        start = start + totals[block]
        key = jnp.sum(member[block] * (rank + row.astype(F32) * CAP), axis=0, keepdims=True)
        keys.append(key)
    return jnp.concatenate(keys, axis=1).astype(jnp.int32)


def spill_rows(place, offset, weights):
    row = lax.broadcasted_iota(jnp.int32, (8, COLS), 0)
    last = place == COLS - 1
    first_a = jnp.where(last, weights[2], jnp.where(place == COLS - 2, weights[3], 0.0))
    first_b = jnp.where(last, weights[3], 0.0)
    end = jnp.where(place == 0, weights[0], 0.0)
    rows = jnp.where(row == 0, first_a, jnp.where(row == 1, first_b, jnp.where(row == 7, end, 0.0)))
    spread = [jnp.where(offset == o, rows, 0.0) for o in range(-REACH, REACH + 1)]
    high, low = halves(jnp.concatenate(spread, axis=0))
    return jnp.concatenate([high, low], axis=0)


def meta_rows(place, fraction):
    a = fraction.astype(BF)
    rest = fraction - a.astype(F32)
    b = rest.astype(BF)
    c = rest - b.astype(F32)
    p_high = (place // 32).astype(F32)
    p_low = (place % 32).astype(F32)
    row = lax.broadcasted_iota(jnp.int32, (8, COLS), 0)
    out = jnp.where(row == 0, a.astype(F32), 0.0)
    out = jnp.where(row == 1, b.astype(F32), out)
    out = jnp.where(row == 2, c, out)
    out = jnp.where(row == 3, p_high, out)
    out = jnp.where(row == 4, p_low, out)
    return out.astype(BF)


def choose(keys, which):
    slot = lax.broadcasted_iota(jnp.int32, (CAP, COLS), 0).astype(jnp.int16)
    wanted = jnp.broadcast_to(keys - which * CAP, (16, COLS)).astype(jnp.int16)
    wanted = jnp.concatenate([wanted] * (CAP // 16), axis=0)
    return jnp.where(slot == wanted, BF(1.0), BF(0.0))


def spill_block(spilled, target):
    row = lax.broadcasted_iota(jnp.int32, (8, LEV), 0)
    from_cell = jnp.where(row < 2, target - 1, jnp.where(row == 7, target + 1, -9))
    out = jnp.zeros((8, LEV), F32)
    for o in range(-REACH, REACH + 1):
        block = spilled[8 * (o + REACH) : 8 * (o + REACH) + 8]
        out = out + jnp.where(from_cell == o, block, 0.0)
    return out


def spill_sums(spills, both):
    wide = dot(spills, both)
    count = 8 * (2 * REACH + 1)
    return (wide[:count, :LEV] + wide[:count, LEV:]) + (wide[count:, :LEV] + wide[count:, LEV:])


def index_values(self_ref, departure, fraction, tile_count):
    place, offset = locate(departure, self_ref[0], tile_count)
    keys = slots_of(offset, signs(self_ref[0]))
    weights = cubic_weights(fraction)
    return place, offset, keys, weights


def write_meta(meta_out, base, meta, one_hot):
    got = dot_nt(meta, one_hot)
    fraction = got[0:1] + got[1:2] + got[2:3]
    place = got[3:4] * 32.0 + got[4:5]
    for c in range(CAP // LEV):
        meta_out[base + c : base + c + 1, :] = fraction[:, c * LEV : (c + 1) * LEV]
        meta_out[base + 4 + c : base + 5 + c, :] = place[:, c * LEV : (c + 1) * LEV]


def pack_payload(out, one_hot, both, spilled, shift):
    wide = dot(one_hot, both)
    out[0:CAP, :] = wide[:, :LEV] + wide[:, LEV:]
    out[CAP : CAP + 8, :] = spill_block(spilled, shift)


def beyond(outs, spilled, shifts):
    block = spill_block(spilled, shifts[4])
    for which in range(2):
        outs[which][CAP + 16 : CAP + 24, :] = jnp.where(shifts[which] * shifts[4] > 0, block, 0.0)


def first_pack_kernel(tile_count, self_ref, field_hbm, departure_hbm, fraction_hbm, *refs):
    outs, (field, departure, fraction, sems) = refs[:-4], refs[-4:]
    copies = [
        pltpu.make_async_copy(departure_hbm, departure, sems.at[0]),
        pltpu.make_async_copy(fraction_hbm, fraction, sems.at[1]),
        pltpu.make_async_copy(field_hbm, field, sems.at[2]),
    ]
    for copy in copies:
        copy.start()
    copies[0].wait()
    copies[1].wait()
    place, offset, keys, weights = index_values(self_ref, departure[1:2, :], fraction[1:2, :], tile_count)
    meta = meta_rows(place, fraction[1:2, :])
    spills = spill_rows(place, offset, weights)
    copies[2].wait()
    high, low = halves(field[...])
    both = jnp.concatenate([high, low], axis=1)
    spilled = spill_sums(spills, both)
    shifts = signs(self_ref[0])
    beyond(outs, spilled, shifts)
    outs[4][...] = spill_block(spilled, shifts[5])
    outs[5][...] = spill_block(spilled, 0)
    for which, shift in enumerate(shifts[:SWAPS]):
        one_hot = choose(keys, which)
        pack_payload(outs[which], one_hot, both, spilled, shift)
        write_meta(outs[which], CAP + 8, meta, one_hot)


def index_kernel(tile_count, self_ref, departure, fraction, keys_out, spill_out, meta_out):
    place, offset, keys, weights = index_values(self_ref, departure[0:1, :], fraction[0:1, :], tile_count)
    meta = meta_rows(place, fraction[0:1, :])
    keys_out[...] = keys
    spill_out[...] = spill_rows(place, offset, weights)
    for which in range(SWAPS):
        write_meta(meta_out, 8 * which, meta, choose(keys, which))


def second_pack_kernel(self_ref, field, keys, spills, meta, *outs):
    high, low = halves(field[...])
    both = jnp.concatenate([high, low], axis=1)
    spilled = spill_sums(spills[...], both)
    shifts = signs(self_ref[0])
    beyond(outs, spilled, shifts)
    outs[4][...] = spill_block(spilled, shifts[5])
    outs[5][...] = spill_block(spilled, 0)
    for which, shift in enumerate(shifts[:SWAPS]):
        pack_payload(outs[which], choose(keys[...], which), both, spilled, shift)
        outs[which][CAP + 8 : CAP + 16, :] = meta[8 * which : 8 * which + 8, :]


BLOCK = 512
I16 = jnp.int16


def tiled(x, rows):
    return jnp.concatenate([x] * (rows // 16), axis=0)


def spread_table(place, weights):
    shape = (16, place.shape[1])
    start = jnp.broadcast_to(place - 1, shape).astype(I16)
    return start, [halves(jnp.broadcast_to(w, shape)) for w in weights]


def spread_block(first_cell, table):
    start, weights = table
    columns = start.shape[1]
    cells = lax.broadcasted_iota(jnp.int32, (BLOCK, columns), 0).astype(I16)
    first = jnp.full((16, columns), first_cell, jnp.int32).astype(I16)
    distance = cells - tiled(start - first, BLOCK)
    high = jnp.zeros((BLOCK, columns), BF)
    low = high
    for k in range(4):
        here = distance == I16(k)
        high = jnp.where(here, tiled(weights[k][0], BLOCK), high)
        low = jnp.where(here, tiled(weights[k][1], BLOCK), low)
    return high, low


def own_kernel(step, tile_count, self_ref, field, departure, fraction, spilled, payload, out, own_ref, both_ref):
    departure = departure[step : step + 1, :]
    fraction = fraction[step : step + 1, :]
    place, offset = locate(departure, self_ref[0], tile_count)
    own_table = spread_table(place, [jnp.where(offset == 0, w, 0.0) for w in cubic_weights(fraction)])
    high, low = halves(field[...])
    own_ref[:, :LEV] = high
    own_ref[:, LEV:] = low
    table = payload_table(payload, both_ref, 0)

    @pl.loop(0, COLS // BLOCK)
    def _(b):
        high, low = spread_block(b * BLOCK, own_table)
        wide = dot(high, own_ref[...]) + dot(low, own_ref[...])
        high, low = spread_block(b * BLOCK, table)
        wide = wide + dot(high, both_ref[0]) + dot(low, both_ref[0])
        out[pl.ds(b * BLOCK, BLOCK), :] = wide[:, :LEV] + wide[:, LEV:]

    add_spill(out, spilled[...] + payload[CAP : CAP + 8, :])


def payload_table(payload, both_ref, which):
    high, low = halves(payload[0:CAP, :])
    both_ref[which, :, :LEV] = high
    both_ref[which, :, LEV:] = low
    rows = [payload[CAP + 8 + c : CAP + 9 + c, :] for c in range(8)]
    fraction = jnp.concatenate(rows[:4], axis=1)
    place = jnp.concatenate(rows[4:], axis=1).astype(jnp.int32)
    return spread_table(place, cubic_weights(fraction))


def add_spill(out, block):
    row = lax.broadcasted_iota(jnp.int32, (8, LEV), 0)
    out[0:8, :] = out[0:8, :] + jnp.where(row < 2, block, 0.0)
    out[COLS - 8 : COLS, :] = out[COLS - 8 : COLS, :] + jnp.where(row == 7, block, 0.0)


def deposit_block(b, start, tables, both_ref):
    wide = jnp.zeros((BLOCK, 2 * LEV), F32)
    for which, table in enumerate(tables):
        high, low = spread_block(b * BLOCK, table)
        wide = wide + dot(high, both_ref[which]) + dot(low, both_ref[which])
    return start[pl.ds(b * BLOCK, BLOCK), :] + wide[:, :LEV] + wide[:, LEV:]


def middle_kernel(start, p0, p1, out, both_ref):
    tables = [payload_table(p, both_ref, which) for which, p in enumerate((p0, p1))]

    @pl.loop(0, COLS // BLOCK)
    def _(b):
        out[pl.ds(b * BLOCK, BLOCK), :] = deposit_block(b, start, tables, both_ref)

    add_spill(out, p0[CAP : CAP + 8, :] + p1[CAP : CAP + 8, :])


def last_kernel(step, start, payload, tiny_a, tiny_b, level_map, out, both_ref, sum_ref, lifted_ref, sems):
    tables = [payload_table(payload, both_ref, 0)]

    @pl.loop(0, COLS // BLOCK)
    def _(b):
        sum_ref[pl.ds(b * BLOCK, BLOCK), :] = deposit_block(b, start, tables, both_ref)

    add_spill(sum_ref, payload[CAP : CAP + 8, :] + tiny_a[...] + tiny_b[...])
    map_high, map_low = halves(level_map[step])

    def lift(rows):
        high, low = halves(sum_ref[rows, :])
        return dot_nt(high, map_high) + (dot_nt(high, map_low) + dot_nt(low, map_high))

    if step == 1:
        out[...] = lift(slice(0, COLS))
        return
    copies = []
    for b in range(COLS // BLOCK):
        rows = slice(b * BLOCK, (b + 1) * BLOCK)
        lifted_ref[rows, :] = lift(rows)
        copies.append(pltpu.make_async_copy(lifted_ref.at[rows, :], out.at[rows, :], sems.at[b]))
        copies[-1].start()
    for copy in copies:
        copy.wait()


def couple_kernel(table, x, out):
    count = x.shape[0]

    @pl.loop(0, x.shape[1] // 8)
    def _(r):
        rows = [x[e, pl.ds(r * 8, 8), :] for e in range(count)]
        for b in range(count):
            total = rows[0] * table[count * b : count * b + 1, :]
            for e in range(1, count):
                total = total + rows[e] * table[count * b + e : count * b + e + 1, :]
            out[b, pl.ds(r * 8, 8), :] = total


VM = pl.BlockSpec(memory_space=pltpu.MemorySpace.VMEM)
HBM = pl.BlockSpec(memory_space=pltpu.MemorySpace.HBM)
SM = pl.BlockSpec(memory_space=pltpu.MemorySpace.SMEM)
PARAMS = pltpu.CompilerParams(vmem_limit_bytes=40 * 1024 * 1024)
PACKED = [jax.ShapeDtypeStruct((rows, LEV), F32) for rows in (WIDE_ROWS, WIDE_ROWS, ROWS, ROWS, 8, 8)]


def call(kernel, out_shape, in_specs, scratch=(), flops=0, out_spec=None):
    multiple = isinstance(out_shape, (list, tuple))
    return pl.pallas_call(
        kernel,
        out_shape=out_shape,
        in_specs=in_specs,
        out_specs=[VM] * len(out_shape) if multiple else out_spec or VM,
        scratch_shapes=list(scratch),
        compiler_params=PARAMS,
        cost_estimate=pl.CostEstimate(flops=flops, transcendentals=0, bytes_accessed=flops // 256),
    )


def transported(step, packed, tile_count, tile_self, field, departure, fraction, level_map):
    far = [swapped(packed[w], w) for w in (0, 1)]
    partner = swapped(packed[3], 3)
    late = lax.optimization_barrier((packed[2], packed[4], partner))
    cross = swapped(late[0], 2)
    tiny = swapped(late[1], 5)
    handed = swapped(far[0][CAP + 16 :] + far[1][CAP + 16 :], 3)
    total = jax.ShapeDtypeStruct((COLS, LEV), F32)
    one = pltpu.VMEM((1, CAP, 2 * LEV), BF)
    work = 3 * 10**9
    own = call(
        functools.partial(own_kernel, step, tile_count),
        total,
        [SM] + [VM] * 5,
        [pltpu.VMEM((COLS, 2 * LEV), BF), one],
        work,
    )(tile_self, field, departure, fraction, packed[5], partner)
    summed = call(middle_kernel, total, [VM] * 3, [pltpu.VMEM((2, CAP, 2 * LEV), BF)], work)(own, *far)
    return call(
        functools.partial(last_kernel, step),
        total,
        [VM] * 5,
        [
            one,
            pltpu.VMEM((COLS, LEV), F32),
            pltpu.VMEM((COLS, LEV), F32),
            pltpu.SemaphoreType.DMA((COLS // BLOCK,)),
        ],
        work,
        HBM if step == 0 else VM,
    )(summed, cross, tiny, handed, level_map)


def body(adjoint_in, departure, fraction, level_map, coarse_map):
    tile_count = lax.axis_size("tile")
    groups = lax.axis_size("grp")
    tile_self = lax.axis_index("tile").astype(jnp.int32).reshape(1)
    first_scratch = [
        pltpu.VMEM((COLS, LEV), F32),
        pltpu.VMEM((2, COLS), jnp.int32),
        pltpu.VMEM((2, COLS), F32),
        pltpu.SemaphoreType.DMA((3,)),
    ]
    packed = call(functools.partial(first_pack_kernel, tile_count), PACKED, [SM, HBM, HBM, HBM], first_scratch)(
        tile_self, *[pltpu.with_memory_space_constraint(x, pltpu.MemorySpace.HBM) for x in (adjoint_in, departure, fraction)]
    )
    keys, spills, meta = call(
        functools.partial(index_kernel, tile_count),
        [
            jax.ShapeDtypeStruct((1, COLS), jnp.int32),
            jax.ShapeDtypeStruct((16 * (2 * REACH + 1), COLS), BF),
            jax.ShapeDtypeStruct((32, LEV), F32),
        ],
        [SM, VM, VM],
        (),
        2 * 10**9,
    )(tile_self, departure, fraction)
    table = coarse_map.transpose(1, 2, 0).reshape(groups * groups, LEV)
    second = transported(1, packed, tile_count, tile_self, adjoint_in, departure, fraction, level_map)

    parts = lax.all_to_all(second.reshape(groups, COLS // groups, LEV), "grp", 0, 0)
    mixed = call(couple_kernel, jax.ShapeDtypeStruct(parts.shape, F32), [VM, VM])(table, parts)
    coupled = lax.all_to_all(mixed, "grp", 0, 0).reshape(COLS, LEV)

    packed = call(second_pack_kernel, PACKED, [SM] + [VM] * 4)(tile_self, coupled, keys, spills, meta)
    return transported(0, packed, tile_count, tile_self, coupled, departure, fraction, level_map)


def solution(mesh):
    return jax.shard_map(
        body,
        mesh=mesh,
        in_specs=(
            P(("grp", "tile"), None),
            P(None, ("grp", "tile")),
            P(None, ("grp", "tile")),
            P(),
            P(),
        ),
        out_specs=P(("grp", "tile"), None),
        check_vma=False,
    )
```

```python
import functools

import jax
import jax.numpy as jnp
from jax import lax
from jax.experimental import pallas as pl
from jax.experimental.pallas import tpu as pltpu
from jax.sharding import PartitionSpec as P

REACH = 2
SWAPS = 4
COLS = 1024
LEV = 128
CAP = 512
ROWS = CAP + 16
WIDE_ROWS = CAP + 24
BF = jnp.bfloat16
F32 = jnp.float32


def signs(tile):
    core = 1 - 2 * (tile % 2)
    chip = 1 - 2 * ((tile // 2) % 2)
    return (2 * chip, -2 * chip, -core, core, 3 * core, -3 * core)


def swapped(x, which):
    length = lax.axis_size("tile")
    return lax.ppermute(x, "tile", [(i, (i + signs(i)[which]) % length) for i in range(length)])


def halves(x):
    high = x.astype(BF)
    low = (x - high.astype(F32)).astype(BF)
    return high, low


def dot(a, b):
    return lax.dot_general(a, b, (((1,), (0,)), ((), ())), preferred_element_type=F32)


def dot_nt(a, b):
    return lax.dot_general(a, b, (((1,), (1,)), ((), ())), preferred_element_type=F32)


def cubic_weights(a):
    return (
        -a * (1.0 - a) * (2.0 - a) * (1.0 / 6.0),
        (1.0 + a) * (1.0 - a) * (2.0 - a) * 0.5,
        (1.0 + a) * a * (2.0 - a) * 0.5,
        -(1.0 + a) * a * (1.0 - a) * (1.0 / 6.0),
    )


def locate(departure, tile_self, tile_count):
    place = departure % COLS
    target = (departure // COLS) % tile_count
    offset = (target - tile_self + REACH + tile_count) % tile_count - REACH
    return place, offset


def slots_of(offset, shifts):
    row = lax.broadcasted_iota(jnp.int32, (8, LEV), 0)
    lane_a = lax.broadcasted_iota(jnp.int32, (LEV, LEV), 0)
    lane_b = lax.broadcasted_iota(jnp.int32, (LEV, LEV), 1)
    before = jnp.where(lane_a < lane_b, 1.0, 0.0).astype(BF)
    number = jnp.full((1, COLS), 4, jnp.int32)
    for which, shift in enumerate(shifts[:SWAPS]):
        number = jnp.where(offset == shift, which, number)
    members = []
    for c in range(COLS // LEV):
        part = number[:, c * LEV : (c + 1) * LEV]
        members.append(jnp.where(row == part, 1.0, 0.0))
    member = jnp.concatenate(members, axis=0)
    inside = dot(member.astype(BF), before)
    totals = jnp.sum(member, axis=1, keepdims=True)
    start = jnp.zeros((8, 1), F32)
    keys = []
    for c in range(COLS // LEV):
        block = slice(8 * c, 8 * c + 8)
        rank = inside[block] + start
        start = start + totals[block]
        key = jnp.sum(member[block] * (rank + row.astype(F32) * CAP), axis=0, keepdims=True)
        keys.append(key)
    return jnp.concatenate(keys, axis=1).astype(jnp.int32)


def spill_rows(place, offset, weights):
    row = lax.broadcasted_iota(jnp.int32, (8, COLS), 0)
    last = place == COLS - 1
    first_a = jnp.where(last, weights[2], jnp.where(place == COLS - 2, weights[3], 0.0))
    first_b = jnp.where(last, weights[3], 0.0)
    end = jnp.where(place == 0, weights[0], 0.0)
    rows = jnp.where(row == 0, first_a, jnp.where(row == 1, first_b, jnp.where(row == 7, end, 0.0)))
    spread = [jnp.where(offset == o, rows, 0.0) for o in range(-REACH, REACH + 1)]
    high, low = halves(jnp.concatenate(spread, axis=0))
    return jnp.concatenate([high, low], axis=0)


def meta_rows(place, fraction):
    a = fraction.astype(BF)
    rest = fraction - a.astype(F32)
    b = rest.astype(BF)
    c = rest - b.astype(F32)
    p_high = (place // 32).astype(F32)
    p_low = (place % 32).astype(F32)
    row = lax.broadcasted_iota(jnp.int32, (8, COLS), 0)
    out = jnp.where(row == 0, a.astype(F32), 0.0)
    out = jnp.where(row == 1, b.astype(F32), out)
    out = jnp.where(row == 2, c, out)
    out = jnp.where(row == 3, p_high, out)
    out = jnp.where(row == 4, p_low, out)
    return out.astype(BF)


def choose(keys, which):
    slot = lax.broadcasted_iota(jnp.int32, (CAP, COLS), 0).astype(jnp.int16)
    wanted = jnp.broadcast_to(keys - which * CAP, (16, COLS)).astype(jnp.int16)
    wanted = jnp.concatenate([wanted] * (CAP // 16), axis=0)
    return jnp.where(slot == wanted, BF(1.0), BF(0.0))


def spill_block(spilled, target):
    row = lax.broadcasted_iota(jnp.int32, (8, LEV), 0)
    from_cell = jnp.where(row < 2, target - 1, jnp.where(row == 7, target + 1, -9))
    out = jnp.zeros((8, LEV), F32)
    for o in range(-REACH, REACH + 1):
        block = spilled[8 * (o + REACH) : 8 * (o + REACH) + 8]
        out = out + jnp.where(from_cell == o, block, 0.0)
    return out


def spill_sums(spills, both):
    wide = dot(spills, both)
    count = 8 * (2 * REACH + 1)
    return (wide[:count, :LEV] + wide[:count, LEV:]) + (wide[count:, :LEV] + wide[count:, LEV:])


def index_values(self_ref, departure, fraction, tile_count):
    place, offset = locate(departure, self_ref[0], tile_count)
    keys = slots_of(offset, signs(self_ref[0]))
    weights = cubic_weights(fraction)
    return place, offset, keys, weights


def write_meta(meta_out, base, meta, one_hot):
    got = dot_nt(meta, one_hot)
    fraction = got[0:1] + got[1:2] + got[2:3]
    place = got[3:4] * 32.0 + got[4:5]
    for c in range(CAP // LEV):
        meta_out[base + c : base + c + 1, :] = fraction[:, c * LEV : (c + 1) * LEV]
        meta_out[base + 4 + c : base + 5 + c, :] = place[:, c * LEV : (c + 1) * LEV]


def pack_payload(out, one_hot, both, spilled, shift):
    wide = dot(one_hot, both)
    out[0:CAP, :] = wide[:, :LEV] + wide[:, LEV:]
    out[CAP : CAP + 8, :] = spill_block(spilled, shift)


def beyond(outs, spilled, shifts):
    block = spill_block(spilled, shifts[4])
    for which in range(2):
        outs[which][CAP + 16 : CAP + 24, :] = jnp.where(shifts[which] * shifts[4] > 0, block, 0.0)


def first_pack_kernel(tile_count, self_ref, field_hbm, departure_hbm, fraction_hbm, *refs):
    outs, (field, departure, fraction, sems) = refs[:-4], refs[-4:]
    copies = [
        pltpu.make_async_copy(departure_hbm, departure, sems.at[0]),
        pltpu.make_async_copy(fraction_hbm, fraction, sems.at[1]),
        pltpu.make_async_copy(field_hbm, field, sems.at[2]),
    ]
    for copy in copies:
        copy.start()
    copies[0].wait()
    copies[1].wait()
    place, offset, keys, weights = index_values(self_ref, departure[1:2, :], fraction[1:2, :], tile_count)
    meta = meta_rows(place, fraction[1:2, :])
    spills = spill_rows(place, offset, weights)
    copies[2].wait()
    high, low = halves(field[...])
    both = jnp.concatenate([high, low], axis=1)
    spilled = spill_sums(spills, both)
    shifts = signs(self_ref[0])
    beyond(outs, spilled, shifts)
    outs[4][...] = spill_block(spilled, shifts[5])
    outs[5][...] = spill_block(spilled, 0)
    for which, shift in enumerate(shifts[:SWAPS]):
        one_hot = choose(keys, which)
        pack_payload(outs[which], one_hot, both, spilled, shift)
        write_meta(outs[which], CAP + 8, meta, one_hot)


def index_kernel(tile_count, self_ref, departure, fraction, keys_out, spill_out, meta_out):
    place, offset, keys, weights = index_values(self_ref, departure[0:1, :], fraction[0:1, :], tile_count)
    meta = meta_rows(place, fraction[0:1, :])
    keys_out[...] = keys
    spill_out[...] = spill_rows(place, offset, weights)
    for which in range(SWAPS):
        write_meta(meta_out, 8 * which, meta, choose(keys, which))


def second_pack_kernel(self_ref, field, keys, spills, meta, *outs):
    high, low = halves(field[...])
    both = jnp.concatenate([high, low], axis=1)
    spilled = spill_sums(spills[...], both)
    shifts = signs(self_ref[0])
    beyond(outs, spilled, shifts)
    outs[4][...] = spill_block(spilled, shifts[5])
    outs[5][...] = spill_block(spilled, 0)
    for which, shift in enumerate(shifts[:SWAPS]):
        pack_payload(outs[which], choose(keys[...], which), both, spilled, shift)
        outs[which][CAP + 8 : CAP + 16, :] = meta[8 * which : 8 * which + 8, :]


BLOCK = 512
I16 = jnp.int16


def tiled(x, rows):
    return jnp.concatenate([x] * (rows // 16), axis=0)


def spread_table(place, weights):
    shape = (16, place.shape[1])
    start = jnp.broadcast_to(place - 1, shape).astype(I16)
    return start, [halves(jnp.broadcast_to(w, shape)) for w in weights]


def spread_block(first_cell, table):
    start, weights = table
    columns = start.shape[1]
    cells = lax.broadcasted_iota(jnp.int32, (BLOCK, columns), 0).astype(I16)
    first = jnp.full((16, columns), first_cell, jnp.int32).astype(I16)
    distance = cells - tiled(start - first, BLOCK)
    high = jnp.zeros((BLOCK, columns), BF)
    low = high
    for k in range(4):
        here = distance == I16(k)
        high = jnp.where(here, tiled(weights[k][0], BLOCK), high)
        low = jnp.where(here, tiled(weights[k][1], BLOCK), low)
    return high, low


def own_kernel(step, tile_count, self_ref, field, departure, fraction, spilled, payload, out, own_ref, both_ref):
    departure = departure[step : step + 1, :]
    fraction = fraction[step : step + 1, :]
    place, offset = locate(departure, self_ref[0], tile_count)
    own_table = spread_table(place, [jnp.where(offset == 0, w, 0.0) for w in cubic_weights(fraction)])
    high, low = halves(field[...])
    own_ref[:, :LEV] = high
    own_ref[:, LEV:] = low
    table = payload_table(payload, both_ref, 0)

    @pl.loop(0, COLS // BLOCK)
    def _(b):
        high, low = spread_block(b * BLOCK, own_table)
        wide = dot(high, own_ref[...]) + dot(low, own_ref[...])
        high, low = spread_block(b * BLOCK, table)
        wide = wide + dot(high, both_ref[0]) + dot(low, both_ref[0])
        out[pl.ds(b * BLOCK, BLOCK), :] = wide[:, :LEV] + wide[:, LEV:]

    add_spill(out, spilled[...] + payload[CAP : CAP + 8, :])


def payload_table(payload, both_ref, which):
    high, low = halves(payload[0:CAP, :])
    both_ref[which, :, :LEV] = high
    both_ref[which, :, LEV:] = low
    rows = [payload[CAP + 8 + c : CAP + 9 + c, :] for c in range(8)]
    fraction = jnp.concatenate(rows[:4], axis=1)
    place = jnp.concatenate(rows[4:], axis=1).astype(jnp.int32)
    return spread_table(place, cubic_weights(fraction))


def add_spill(out, block):
    row = lax.broadcasted_iota(jnp.int32, (8, LEV), 0)
    out[0:8, :] = out[0:8, :] + jnp.where(row < 2, block, 0.0)
    out[COLS - 8 : COLS, :] = out[COLS - 8 : COLS, :] + jnp.where(row == 7, block, 0.0)


def deposit_block(b, start, tables, both_ref):
    wide = jnp.zeros((BLOCK, 2 * LEV), F32)
    for which, table in enumerate(tables):
        high, low = spread_block(b * BLOCK, table)
        wide = wide + dot(high, both_ref[which]) + dot(low, both_ref[which])
    return start[pl.ds(b * BLOCK, BLOCK), :] + wide[:, :LEV] + wide[:, LEV:]


def middle_kernel(start, p0, p1, out, both_ref):
    tables = [payload_table(p, both_ref, which) for which, p in enumerate((p0, p1))]

    @pl.loop(0, COLS // BLOCK)
    def _(b):
        out[pl.ds(b * BLOCK, BLOCK), :] = deposit_block(b, start, tables, both_ref)

    add_spill(out, p0[CAP : CAP + 8, :] + p1[CAP : CAP + 8, :])


def last_kernel(step, start, payload, tiny_a, tiny_b, level_map, out, both_ref, sum_ref, lifted_ref, sems):
    tables = [payload_table(payload, both_ref, 0)]

    @pl.loop(0, COLS // BLOCK)
    def _(b):
        sum_ref[pl.ds(b * BLOCK, BLOCK), :] = deposit_block(b, start, tables, both_ref)

    add_spill(sum_ref, payload[CAP : CAP + 8, :] + tiny_a[...] + tiny_b[...])
    map_high, map_low = halves(level_map[step])

    def lift(rows):
        high, low = halves(sum_ref[rows, :])
        return dot_nt(high, map_high) + (dot_nt(high, map_low) + dot_nt(low, map_high))

    if step == 1:
        out[...] = lift(slice(0, COLS))
        return
    copies = []
    for b in range(COLS // BLOCK):
        rows = slice(b * BLOCK, (b + 1) * BLOCK)
        lifted_ref[rows, :] = lift(rows)
        copies.append(pltpu.make_async_copy(lifted_ref.at[rows, :], out.at[rows, :], sems.at[b]))
        copies[-1].start()
    for copy in copies:
        copy.wait()


def couple_kernel(table, x, out):
    count = x.shape[0]

    @pl.loop(0, x.shape[1] // 8)
    def _(r):
        rows = [x[e, pl.ds(r * 8, 8), :] for e in range(count)]
        for b in range(count):
            total = rows[0] * table[count * b : count * b + 1, :]
            for e in range(1, count):
                total = total + rows[e] * table[count * b + e : count * b + e + 1, :]
            out[b, pl.ds(r * 8, 8), :] = total


VM = pl.BlockSpec(memory_space=pltpu.MemorySpace.VMEM)
HBM = pl.BlockSpec(memory_space=pltpu.MemorySpace.HBM)
SM = pl.BlockSpec(memory_space=pltpu.MemorySpace.SMEM)
PARAMS = pltpu.CompilerParams(vmem_limit_bytes=40 * 1024 * 1024)
PACKED = [jax.ShapeDtypeStruct((rows, LEV), F32) for rows in (WIDE_ROWS, WIDE_ROWS, ROWS, ROWS, 8, 8)]


def call(kernel, out_shape, in_specs, scratch=(), flops=0, out_spec=None):
    multiple = isinstance(out_shape, (list, tuple))
    return pl.pallas_call(
        kernel,
        out_shape=out_shape,
        in_specs=in_specs,
        out_specs=[VM] * len(out_shape) if multiple else out_spec or VM,
        scratch_shapes=list(scratch),
        compiler_params=PARAMS,
        cost_estimate=pl.CostEstimate(flops=flops, transcendentals=0, bytes_accessed=flops // 256),
    )


def transported(step, packed, tile_count, tile_self, field, departure, fraction, level_map):
    far = [swapped(packed[w], w) for w in (0, 1)]
    partner = swapped(packed[3], 3)
    late = lax.optimization_barrier((packed[2], packed[4], partner))
    cross = swapped(late[0], 2)
    tiny = swapped(late[1], 5)
    handed = swapped(far[0][CAP + 16 :] + far[1][CAP + 16 :], 3)
    total = jax.ShapeDtypeStruct((COLS, LEV), F32)
    one = pltpu.VMEM((1, CAP, 2 * LEV), BF)
    work = 3 * 10**9
    own = call(
        functools.partial(own_kernel, step, tile_count),
        total,
        [SM] + [VM] * 5,
        [pltpu.VMEM((COLS, 2 * LEV), BF), one],
        work,
    )(tile_self, field, departure, fraction, packed[5], partner)
    index = None
    if step == 1:
        after = lax.optimization_barrier((tile_self, own))
        index = call(
            functools.partial(index_kernel, tile_count),
            [
                jax.ShapeDtypeStruct((1, COLS), jnp.int32),
                jax.ShapeDtypeStruct((16 * (2 * REACH + 1), COLS), BF),
                jax.ShapeDtypeStruct((32, LEV), F32),
            ],
            [SM, VM, VM],
            (),
            2 * 10**9,
        )(after[0], departure, fraction)
        own, index = lax.optimization_barrier((after[1], index))
    summed = call(middle_kernel, total, [VM] * 3, [pltpu.VMEM((2, CAP, 2 * LEV), BF)], work)(own, *far)
    result = call(
        functools.partial(last_kernel, step),
        total,
        [VM] * 5,
        [
            one,
            pltpu.VMEM((COLS, LEV), F32),
            pltpu.VMEM((COLS, LEV), F32),
            pltpu.SemaphoreType.DMA((COLS // BLOCK,)),
        ],
        work,
        HBM if step == 0 else VM,
    )(summed, cross, tiny, handed, level_map)
    return result, index


def body(adjoint_in, departure, fraction, level_map, coarse_map):
    tile_count = lax.axis_size("tile")
    groups = lax.axis_size("grp")
    tile_self = lax.axis_index("tile").astype(jnp.int32).reshape(1)
    first_scratch = [
        pltpu.VMEM((COLS, LEV), F32),
        pltpu.VMEM((2, COLS), jnp.int32),
        pltpu.VMEM((2, COLS), F32),
        pltpu.SemaphoreType.DMA((3,)),
    ]
    packed = call(functools.partial(first_pack_kernel, tile_count), PACKED, [SM, HBM, HBM, HBM], first_scratch)(
        tile_self, *[pltpu.with_memory_space_constraint(x, pltpu.MemorySpace.HBM) for x in (adjoint_in, departure, fraction)]
    )
    table = coarse_map.transpose(1, 2, 0).reshape(groups * groups, LEV)
    second, index = transported(1, packed, tile_count, tile_self, adjoint_in, departure, fraction, level_map)

    parts = lax.all_to_all(second.reshape(groups, COLS // groups, LEV), "grp", 0, 0)
    mixed = call(couple_kernel, jax.ShapeDtypeStruct(parts.shape, F32), [VM, VM])(table, parts)
    coupled = lax.all_to_all(mixed, "grp", 0, 0).reshape(COLS, LEV)

    packed = call(second_pack_kernel, PACKED, [SM] + [VM] * 4)(tile_self, coupled, *index)
    return transported(0, packed, tile_count, tile_self, coupled, departure, fraction, level_map)[0]


def solution(mesh):
    return jax.shard_map(
        body,
        mesh=mesh,
        in_specs=(
            P(("grp", "tile"), None),
            P(None, ("grp", "tile")),
            P(None, ("grp", "tile")),
            P(),
            P(),
        ),
        out_specs=P(("grp", "tile"), None),
        check_vma=False,
    )
```

```python
import functools

import jax
import jax.numpy as jnp
from jax import lax
from jax.experimental import pallas as pl
from jax.experimental.pallas import tpu as pltpu
from jax.sharding import PartitionSpec as P

REACH = 2
SWAPS = 4
COLS = 1024
LEV = 128
CAP = 512
ROWS = CAP + 16
WIDE_ROWS = CAP + 24
BF = jnp.bfloat16
F32 = jnp.float32


def signs(tile):
    core = 1 - 2 * (tile % 2)
    chip = 1 - 2 * ((tile // 2) % 2)
    return (2 * chip, -2 * chip, -core, core, 3 * core, -3 * core)


def swapped(x, which):
    length = lax.axis_size("tile")
    return lax.ppermute(x, "tile", [(i, (i + signs(i)[which]) % length) for i in range(length)])


def halves(x):
    high = x.astype(BF)
    low = (x - high.astype(F32)).astype(BF)
    return high, low


def dot(a, b):
    return lax.dot_general(a, b, (((1,), (0,)), ((), ())), preferred_element_type=F32)


def dot_nt(a, b):
    return lax.dot_general(a, b, (((1,), (1,)), ((), ())), preferred_element_type=F32)


def cubic_weights(a):
    return (
        -a * (1.0 - a) * (2.0 - a) * (1.0 / 6.0),
        (1.0 + a) * (1.0 - a) * (2.0 - a) * 0.5,
        (1.0 + a) * a * (2.0 - a) * 0.5,
        -(1.0 + a) * a * (1.0 - a) * (1.0 / 6.0),
    )


def locate(departure, tile_self, tile_count):
    place = departure % COLS
    target = (departure // COLS) % tile_count
    offset = (target - tile_self + REACH + tile_count) % tile_count - REACH
    return place, offset


def slots_of(offset, shifts):
    row = lax.broadcasted_iota(jnp.int32, (8, LEV), 0)
    lane_a = lax.broadcasted_iota(jnp.int32, (LEV, LEV), 0)
    lane_b = lax.broadcasted_iota(jnp.int32, (LEV, LEV), 1)
    before = jnp.where(lane_a < lane_b, 1.0, 0.0).astype(BF)
    number = jnp.full((1, COLS), 4, jnp.int32)
    for which, shift in enumerate(shifts[:SWAPS]):
        number = jnp.where(offset == shift, which, number)
    members = []
    for c in range(COLS // LEV):
        part = number[:, c * LEV : (c + 1) * LEV]
        members.append(jnp.where(row == part, 1.0, 0.0))
    member = jnp.concatenate(members, axis=0)
    inside = dot(member.astype(BF), before)
    totals = jnp.sum(member, axis=1, keepdims=True)
    start = jnp.zeros((8, 1), F32)
    keys = []
    for c in range(COLS // LEV):
        block = slice(8 * c, 8 * c + 8)
        rank = inside[block] + start
        start = start + totals[block]
        key = jnp.sum(member[block] * (rank + row.astype(F32) * CAP), axis=0, keepdims=True)
        keys.append(key)
    return jnp.concatenate(keys, axis=1).astype(jnp.int32)


def spill_rows(place, offset, weights):
    row = lax.broadcasted_iota(jnp.int32, (8, COLS), 0)
    last = place == COLS - 1
    first_a = jnp.where(last, weights[2], jnp.where(place == COLS - 2, weights[3], 0.0))
    first_b = jnp.where(last, weights[3], 0.0)
    end = jnp.where(place == 0, weights[0], 0.0)
    rows = jnp.where(row == 0, first_a, jnp.where(row == 1, first_b, jnp.where(row == 7, end, 0.0)))
    spread = [jnp.where(offset == o, rows, 0.0) for o in range(-REACH, REACH + 1)]
    high, low = halves(jnp.concatenate(spread, axis=0))
    return jnp.concatenate([high, low], axis=0)


def meta_rows(place, fraction):
    a = fraction.astype(BF)
    rest = fraction - a.astype(F32)
    b = rest.astype(BF)
    c = rest - b.astype(F32)
    p_high = (place // 32).astype(F32)
    p_low = (place % 32).astype(F32)
    row = lax.broadcasted_iota(jnp.int32, (8, COLS), 0)
    out = jnp.where(row == 0, a.astype(F32), 0.0)
    out = jnp.where(row == 1, b.astype(F32), out)
    out = jnp.where(row == 2, c, out)
    out = jnp.where(row == 3, p_high, out)
    out = jnp.where(row == 4, p_low, out)
    return out.astype(BF)


def choose(keys, which):
    slot = lax.broadcasted_iota(jnp.int32, (CAP, COLS), 0).astype(jnp.int16)
    wanted = jnp.broadcast_to(keys - which * CAP, (16, COLS)).astype(jnp.int16)
    wanted = jnp.concatenate([wanted] * (CAP // 16), axis=0)
    return jnp.where(slot == wanted, BF(1.0), BF(0.0))


def spill_block(spilled, target):
    row = lax.broadcasted_iota(jnp.int32, (8, LEV), 0)
    from_cell = jnp.where(row < 2, target - 1, jnp.where(row == 7, target + 1, -9))
    out = jnp.zeros((8, LEV), F32)
    for o in range(-REACH, REACH + 1):
        block = spilled[8 * (o + REACH) : 8 * (o + REACH) + 8]
        out = out + jnp.where(from_cell == o, block, 0.0)
    return out


def spill_sums(spills, both):
    wide = dot(spills, both)
    count = 8 * (2 * REACH + 1)
    return (wide[:count, :LEV] + wide[:count, LEV:]) + (wide[count:, :LEV] + wide[count:, LEV:])


def index_values(self_ref, departure, fraction, tile_count):
    place, offset = locate(departure, self_ref[0], tile_count)
    keys = slots_of(offset, signs(self_ref[0]))
    weights = cubic_weights(fraction)
    return place, offset, keys, weights


def write_meta(meta_out, base, meta, one_hot):
    got = dot_nt(meta, one_hot)
    fraction = got[0:1] + got[1:2] + got[2:3]
    place = got[3:4] * 32.0 + got[4:5]
    for c in range(CAP // LEV):
        meta_out[base + c : base + c + 1, :] = fraction[:, c * LEV : (c + 1) * LEV]
        meta_out[base + 4 + c : base + 5 + c, :] = place[:, c * LEV : (c + 1) * LEV]


def pack_payload(out, one_hot, both, spilled, shift):
    wide = dot(one_hot, both)
    out[0:CAP, :] = wide[:, :LEV] + wide[:, LEV:]
    out[CAP : CAP + 8, :] = spill_block(spilled, shift)


def pack_far(outs, keys, both, spilled, shifts):
    block = spill_block(spilled, shifts[4])
    for which in range(2):
        one_hot = choose(keys, which)
        pack_payload(outs[which], one_hot, both, spilled, shifts[which])
        outs[which][CAP + 16 : CAP + 24, :] = jnp.where(shifts[which] * shifts[4] > 0, block, 0.0)
        yield one_hot


def first_far_kernel(tile_count, self_ref, field_hbm, departure_hbm, fraction_hbm, *refs):
    outs, (field, departure, fraction, sems) = refs[:-4], refs[-4:]
    copies = [
        pltpu.make_async_copy(departure_hbm, departure, sems.at[0]),
        pltpu.make_async_copy(fraction_hbm, fraction, sems.at[1]),
        pltpu.make_async_copy(field_hbm, field, sems.at[2]),
    ]
    for copy in copies:
        copy.start()
    copies[0].wait()
    copies[1].wait()
    place, offset, keys, weights = index_values(self_ref, departure[1:2, :], fraction[1:2, :], tile_count)
    meta = meta_rows(place, fraction[1:2, :])
    spills = spill_rows(place, offset, weights)
    copies[2].wait()
    high, low = halves(field[...])
    both = jnp.concatenate([high, low], axis=1)
    spilled = spill_sums(spills, both)
    outs[2][...] = both
    outs[3][...] = spilled
    outs[4][...] = keys
    outs[5][...] = meta
    for which, one_hot in enumerate(pack_far(outs, keys, both, spilled, signs(self_ref[0]))):
        write_meta(outs[which], CAP + 8, meta, one_hot)


def second_far_kernel(self_ref, field, keys, spills, meta, *outs):
    high, low = halves(field[...])
    both = jnp.concatenate([high, low], axis=1)
    spilled = spill_sums(spills[...], both)
    outs[2][...] = both
    outs[3][...] = spilled
    for which, _ in enumerate(pack_far(outs, keys[...], both, spilled, signs(self_ref[0]))):
        outs[which][CAP + 8 : CAP + 16, :] = meta[8 * which : 8 * which + 8, :]


def near_pack_kernel(step, self_ref, both, spilled, keys, meta, *outs):
    shifts = signs(self_ref[0])
    sums = spilled[...]
    outs[2][...] = spill_block(sums, shifts[5])
    outs[3][...] = spill_block(sums, 0)
    for out, which in zip(outs, (2, 3)):
        one_hot = choose(keys[...], which)
        pack_payload(out, one_hot, both[...], sums, shifts[which])
        if step == 1:
            write_meta(out, CAP + 8, meta[...], one_hot)
        else:
            out[CAP + 8 : CAP + 16, :] = meta[8 * which : 8 * which + 8, :]


def index_kernel(tile_count, self_ref, departure, fraction, keys_out, spill_out, meta_out):
    place, offset, keys, weights = index_values(self_ref, departure[0:1, :], fraction[0:1, :], tile_count)
    meta = meta_rows(place, fraction[0:1, :])
    keys_out[...] = keys
    spill_out[...] = spill_rows(place, offset, weights)
    for which in range(SWAPS):
        write_meta(meta_out, 8 * which, meta, choose(keys, which))


def second_pack_kernel(self_ref, field, keys, spills, meta, *outs):
    high, low = halves(field[...])
    both = jnp.concatenate([high, low], axis=1)
    spilled = spill_sums(spills[...], both)
    shifts = signs(self_ref[0])
    beyond(outs, spilled, shifts)
    outs[4][...] = spill_block(spilled, shifts[5])
    outs[5][...] = spill_block(spilled, 0)
    for which, shift in enumerate(shifts[:SWAPS]):
        pack_payload(outs[which], choose(keys[...], which), both, spilled, shift)
        outs[which][CAP + 8 : CAP + 16, :] = meta[8 * which : 8 * which + 8, :]


BLOCK = 512
I16 = jnp.int16


def tiled(x, rows):
    return jnp.concatenate([x] * (rows // 16), axis=0)


def spread_table(place, weights):
    shape = (16, place.shape[1])
    start = jnp.broadcast_to(place - 1, shape).astype(I16)
    return start, [halves(jnp.broadcast_to(w, shape)) for w in weights]


def spread_block(first_cell, table):
    start, weights = table
    columns = start.shape[1]
    cells = lax.broadcasted_iota(jnp.int32, (BLOCK, columns), 0).astype(I16)
    first = jnp.full((16, columns), first_cell, jnp.int32).astype(I16)
    distance = cells - tiled(start - first, BLOCK)
    high = jnp.zeros((BLOCK, columns), BF)
    low = high
    for k in range(4):
        here = distance == I16(k)
        high = jnp.where(here, tiled(weights[k][0], BLOCK), high)
        low = jnp.where(here, tiled(weights[k][1], BLOCK), low)
    return high, low


def own_kernel(step, tile_count, self_ref, field, departure, fraction, spilled, payload, out, own_ref, both_ref):
    departure = departure[step : step + 1, :]
    fraction = fraction[step : step + 1, :]
    place, offset = locate(departure, self_ref[0], tile_count)
    own_table = spread_table(place, [jnp.where(offset == 0, w, 0.0) for w in cubic_weights(fraction)])
    high, low = halves(field[...])
    own_ref[:, :LEV] = high
    own_ref[:, LEV:] = low
    table = payload_table(payload, both_ref, 0)

    @pl.loop(0, COLS // BLOCK)
    def _(b):
        high, low = spread_block(b * BLOCK, own_table)
        wide = dot(high, own_ref[...]) + dot(low, own_ref[...])
        high, low = spread_block(b * BLOCK, table)
        wide = wide + dot(high, both_ref[0]) + dot(low, both_ref[0])
        out[pl.ds(b * BLOCK, BLOCK), :] = wide[:, :LEV] + wide[:, LEV:]

    add_spill(out, spilled[...] + payload[CAP : CAP + 8, :])


def payload_table(payload, both_ref, which):
    high, low = halves(payload[0:CAP, :])
    both_ref[which, :, :LEV] = high
    both_ref[which, :, LEV:] = low
    rows = [payload[CAP + 8 + c : CAP + 9 + c, :] for c in range(8)]
    fraction = jnp.concatenate(rows[:4], axis=1)
    place = jnp.concatenate(rows[4:], axis=1).astype(jnp.int32)
    return spread_table(place, cubic_weights(fraction))


def add_spill(out, block):
    row = lax.broadcasted_iota(jnp.int32, (8, LEV), 0)
    out[0:8, :] = out[0:8, :] + jnp.where(row < 2, block, 0.0)
    out[COLS - 8 : COLS, :] = out[COLS - 8 : COLS, :] + jnp.where(row == 7, block, 0.0)


def deposit_block(b, start, tables, both_ref):
    wide = jnp.zeros((BLOCK, 2 * LEV), F32)
    for which, table in enumerate(tables):
        high, low = spread_block(b * BLOCK, table)
        wide = wide + dot(high, both_ref[which]) + dot(low, both_ref[which])
    return start[pl.ds(b * BLOCK, BLOCK), :] + wide[:, :LEV] + wide[:, LEV:]


def middle_kernel(start, p0, p1, out, both_ref):
    tables = [payload_table(p, both_ref, which) for which, p in enumerate((p0, p1))]

    @pl.loop(0, COLS // BLOCK)
    def _(b):
        out[pl.ds(b * BLOCK, BLOCK), :] = deposit_block(b, start, tables, both_ref)

    add_spill(out, p0[CAP : CAP + 8, :] + p1[CAP : CAP + 8, :])


def last_kernel(step, start, payload, tiny_a, tiny_b, level_map, out, both_ref, sum_ref, lifted_ref, sems):
    tables = [payload_table(payload, both_ref, 0)]

    @pl.loop(0, COLS // BLOCK)
    def _(b):
        sum_ref[pl.ds(b * BLOCK, BLOCK), :] = deposit_block(b, start, tables, both_ref)

    add_spill(sum_ref, payload[CAP : CAP + 8, :] + tiny_a[...] + tiny_b[...])
    map_high, map_low = halves(level_map[step])

    def lift(rows):
        high, low = halves(sum_ref[rows, :])
        return dot_nt(high, map_high) + (dot_nt(high, map_low) + dot_nt(low, map_high))

    if step == 1:
        out[...] = lift(slice(0, COLS))
        return
    copies = []
    for b in range(COLS // BLOCK):
        rows = slice(b * BLOCK, (b + 1) * BLOCK)
        lifted_ref[rows, :] = lift(rows)
        copies.append(pltpu.make_async_copy(lifted_ref.at[rows, :], out.at[rows, :], sems.at[b]))
        copies[-1].start()
    for copy in copies:
        copy.wait()


def couple_kernel(table, x, out):
    count = x.shape[0]

    @pl.loop(0, x.shape[1] // 8)
    def _(r):
        rows = [x[e, pl.ds(r * 8, 8), :] for e in range(count)]
        for b in range(count):
            total = rows[0] * table[count * b : count * b + 1, :]
            for e in range(1, count):
                total = total + rows[e] * table[count * b + e : count * b + e + 1, :]
            out[b, pl.ds(r * 8, 8), :] = total


VM = pl.BlockSpec(memory_space=pltpu.MemorySpace.VMEM)
HBM = pl.BlockSpec(memory_space=pltpu.MemorySpace.HBM)
SM = pl.BlockSpec(memory_space=pltpu.MemorySpace.SMEM)
PARAMS = pltpu.CompilerParams(vmem_limit_bytes=40 * 1024 * 1024)
SPREAD_ROWS = 8 * (2 * REACH + 1)
FAR = [
    jax.ShapeDtypeStruct((WIDE_ROWS, LEV), F32),
    jax.ShapeDtypeStruct((WIDE_ROWS, LEV), F32),
    jax.ShapeDtypeStruct((COLS, 2 * LEV), BF),
    jax.ShapeDtypeStruct((SPREAD_ROWS, LEV), F32),
]
NEAR = [jax.ShapeDtypeStruct((rows, LEV), F32) for rows in (ROWS, ROWS, 8, 8)]
KEYS = jax.ShapeDtypeStruct((1, COLS), jnp.int32)


def call(kernel, out_shape, in_specs, scratch=(), flops=0, out_spec=None):
    multiple = isinstance(out_shape, (list, tuple))
    return pl.pallas_call(
        kernel,
        out_shape=out_shape,
        in_specs=in_specs,
        out_specs=[VM] * len(out_shape) if multiple else out_spec or VM,
        scratch_shapes=list(scratch),
        compiler_params=PARAMS,
        cost_estimate=pl.CostEstimate(flops=flops, transcendentals=0, bytes_accessed=flops // 256),
    )


def transported(step, packed, keys, meta, tile_count, tile_self, field, departure, fraction, level_map):
    far = [swapped(packed[w], w) for w in (0, 1)]
    near = call(functools.partial(near_pack_kernel, step), NEAR, [SM] + [VM] * 4, (), 10**9)(
        tile_self, packed[2], packed[3], keys, meta
    )
    cross = swapped(near[0], 2)
    partner = swapped(near[1], 3)
    late = lax.optimization_barrier((near[2], partner))
    tiny = swapped(late[0], 5)
    handed = swapped(far[0][CAP + 16 :] + far[1][CAP + 16 :], 3)
    total = jax.ShapeDtypeStruct((COLS, LEV), F32)
    one = pltpu.VMEM((1, CAP, 2 * LEV), BF)
    work = 10**7
    own = call(
        functools.partial(own_kernel, step, tile_count),
        total,
        [SM] + [VM] * 5,
        [pltpu.VMEM((COLS, 2 * LEV), BF), one],
        work,
    )(tile_self, field, departure, fraction, near[3], partner)
    index = None
    if step == 1:
        after = lax.optimization_barrier((tile_self, own))
        index = call(
            functools.partial(index_kernel, tile_count),
            [
                KEYS,
                jax.ShapeDtypeStruct((2 * SPREAD_ROWS, COLS), BF),
                jax.ShapeDtypeStruct((32, LEV), F32),
            ],
            [SM, VM, VM],
            (),
            2 * 10**9,
        )(after[0], departure, fraction)
        own, index = lax.optimization_barrier((after[1], index))
    summed = call(middle_kernel, total, [VM] * 3, [pltpu.VMEM((2, CAP, 2 * LEV), BF)], work)(own, *far)
    result = call(
        functools.partial(last_kernel, step),
        total,
        [VM] * 5,
        [
            one,
            pltpu.VMEM((COLS, LEV), F32),
            pltpu.VMEM((COLS, LEV), F32),
            pltpu.SemaphoreType.DMA((COLS // BLOCK,)),
        ],
        work,
        HBM if step == 0 else VM,
    )(summed, cross, tiny, handed, level_map)
    return result, index


def body(adjoint_in, departure, fraction, level_map, coarse_map):
    tile_count = lax.axis_size("tile")
    groups = lax.axis_size("grp")
    tile_self = lax.axis_index("tile").astype(jnp.int32).reshape(1)
    first_scratch = [
        pltpu.VMEM((COLS, LEV), F32),
        pltpu.VMEM((2, COLS), jnp.int32),
        pltpu.VMEM((2, COLS), F32),
        pltpu.SemaphoreType.DMA((3,)),
    ]
    outputs = FAR + [KEYS, jax.ShapeDtypeStruct((8, COLS), BF)]
    packed = call(functools.partial(first_far_kernel, tile_count), outputs, [SM, HBM, HBM, HBM], first_scratch)(
        tile_self, *[pltpu.with_memory_space_constraint(x, pltpu.MemorySpace.HBM) for x in (adjoint_in, departure, fraction)]
    )
    table = coarse_map.transpose(1, 2, 0).reshape(groups * groups, LEV)
    second, index = transported(
        1, packed, packed[4], packed[5], tile_count, tile_self, adjoint_in, departure, fraction, level_map
    )

    parts = lax.all_to_all(second.reshape(groups, COLS // groups, LEV), "grp", 0, 0)
    mixed = call(couple_kernel, jax.ShapeDtypeStruct(parts.shape, F32), [VM, VM])(table, parts)
    coupled = lax.all_to_all(mixed, "grp", 0, 0).reshape(COLS, LEV)

    keys, spills, meta = index
    packed = call(second_far_kernel, FAR, [SM] + [VM] * 4)(tile_self, coupled, keys, spills, meta)
    return transported(
        0, packed, keys, meta, tile_count, tile_self, coupled, departure, fraction, level_map
    )[0]


def solution(mesh):
    return jax.shard_map(
        body,
        mesh=mesh,
        in_specs=(
            P(("grp", "tile"), None),
            P(None, ("grp", "tile")),
            P(None, ("grp", "tile")),
            P(),
            P(),
        ),
        out_specs=P(("grp", "tile"), None),
        check_vma=False,
    )
```

```python
import functools

import jax
import jax.numpy as jnp
from jax import lax
from jax.experimental import pallas as pl
from jax.experimental.pallas import tpu as pltpu
from jax.sharding import PartitionSpec as P

REACH = 2
SWAPS = 4
COLS = 1024
LEV = 128
CAP = 512
ROWS = CAP + 16
WIDE_ROWS = CAP + 24
BF = jnp.bfloat16
F32 = jnp.float32


def signs(tile):
    core = 1 - 2 * (tile % 2)
    chip = 1 - 2 * ((tile // 2) % 2)
    return (2 * chip, -2 * chip, -core, core, 3 * core, -3 * core)


def swapped(x, which):
    length = lax.axis_size("tile")
    return lax.ppermute(x, "tile", [(i, (i + signs(i)[which]) % length) for i in range(length)])


def halves(x):
    high = x.astype(BF)
    low = (x - high.astype(F32)).astype(BF)
    return high, low


def dot(a, b):
    return lax.dot_general(a, b, (((1,), (0,)), ((), ())), preferred_element_type=F32)


def dot_nt(a, b):
    return lax.dot_general(a, b, (((1,), (1,)), ((), ())), preferred_element_type=F32)


def cubic_weights(a):
    return (
        -a * (1.0 - a) * (2.0 - a) * (1.0 / 6.0),
        (1.0 + a) * (1.0 - a) * (2.0 - a) * 0.5,
        (1.0 + a) * a * (2.0 - a) * 0.5,
        -(1.0 + a) * a * (1.0 - a) * (1.0 / 6.0),
    )


def locate(departure, tile_self, tile_count):
    place = departure % COLS
    target = (departure // COLS) % tile_count
    offset = (target - tile_self + REACH + tile_count) % tile_count - REACH
    return place, offset


def slots_of(offset, shifts):
    row = lax.broadcasted_iota(jnp.int32, (8, LEV), 0)
    lane_a = lax.broadcasted_iota(jnp.int32, (LEV, LEV), 0)
    lane_b = lax.broadcasted_iota(jnp.int32, (LEV, LEV), 1)
    before = jnp.where(lane_a < lane_b, 1.0, 0.0).astype(BF)
    number = jnp.full((1, COLS), 4, jnp.int32)
    for which, shift in enumerate(shifts[:SWAPS]):
        number = jnp.where(offset == shift, which, number)
    members = []
    for c in range(COLS // LEV):
        part = number[:, c * LEV : (c + 1) * LEV]
        members.append(jnp.where(row == part, 1.0, 0.0))
    member = jnp.concatenate(members, axis=0)
    inside = dot(member.astype(BF), before)
    totals = jnp.sum(member, axis=1, keepdims=True)
    start = jnp.zeros((8, 1), F32)
    keys = []
    for c in range(COLS // LEV):
        block = slice(8 * c, 8 * c + 8)
        rank = inside[block] + start
        start = start + totals[block]
        key = jnp.sum(member[block] * (rank + row.astype(F32) * CAP), axis=0, keepdims=True)
        keys.append(key)
    return jnp.concatenate(keys, axis=1).astype(jnp.int32)


def spill_rows(place, offset, weights):
    row = lax.broadcasted_iota(jnp.int32, (8, COLS), 0)
    last = place == COLS - 1
    first_a = jnp.where(last, weights[2], jnp.where(place == COLS - 2, weights[3], 0.0))
    first_b = jnp.where(last, weights[3], 0.0)
    end = jnp.where(place == 0, weights[0], 0.0)
    rows = jnp.where(row == 0, first_a, jnp.where(row == 1, first_b, jnp.where(row == 7, end, 0.0)))
    spread = [jnp.where(offset == o, rows, 0.0) for o in range(-REACH, REACH + 1)]
    high, low = halves(jnp.concatenate(spread, axis=0))
    return jnp.concatenate([high, low], axis=0)


def meta_rows(place, fraction):
    a = fraction.astype(BF)
    rest = fraction - a.astype(F32)
    b = rest.astype(BF)
    c = rest - b.astype(F32)
    p_high = (place // 32).astype(F32)
    p_low = (place % 32).astype(F32)
    row = lax.broadcasted_iota(jnp.int32, (8, COLS), 0)
    out = jnp.where(row == 0, a.astype(F32), 0.0)
    out = jnp.where(row == 1, b.astype(F32), out)
    out = jnp.where(row == 2, c, out)
    out = jnp.where(row == 3, p_high, out)
    out = jnp.where(row == 4, p_low, out)
    return out.astype(BF)


def choose(keys, which):
    slot = lax.broadcasted_iota(jnp.int32, (CAP, COLS), 0).astype(jnp.int16)
    wanted = jnp.broadcast_to(keys - which * CAP, (16, COLS)).astype(jnp.int16)
    wanted = jnp.concatenate([wanted] * (CAP // 16), axis=0)
    return jnp.where(slot == wanted, BF(1.0), BF(0.0))


def spill_block(spilled, target):
    row = lax.broadcasted_iota(jnp.int32, (8, LEV), 0)
    from_cell = jnp.where(row < 2, target - 1, jnp.where(row == 7, target + 1, -9))
    out = jnp.zeros((8, LEV), F32)
    for o in range(-REACH, REACH + 1):
        block = spilled[8 * (o + REACH) : 8 * (o + REACH) + 8]
        out = out + jnp.where(from_cell == o, block, 0.0)
    return out


def spill_sums(spills, both):
    wide = dot(spills, both)
    count = 8 * (2 * REACH + 1)
    return (wide[:count, :LEV] + wide[:count, LEV:]) + (wide[count:, :LEV] + wide[count:, LEV:])


def index_values(self_ref, departure, fraction, tile_count):
    place, offset = locate(departure, self_ref[0], tile_count)
    keys = slots_of(offset, signs(self_ref[0]))
    weights = cubic_weights(fraction)
    return place, offset, keys, weights


def write_meta(meta_out, base, meta, one_hot):
    got = dot_nt(meta, one_hot)
    fraction = got[0:1] + got[1:2] + got[2:3]
    place = got[3:4] * 32.0 + got[4:5]
    for c in range(CAP // LEV):
        meta_out[base + c : base + c + 1, :] = fraction[:, c * LEV : (c + 1) * LEV]
        meta_out[base + 4 + c : base + 5 + c, :] = place[:, c * LEV : (c + 1) * LEV]


def pack_payload(out, one_hot, both, spilled, shift):
    wide = dot(one_hot, both)
    out[0:CAP, :] = wide[:, :LEV] + wide[:, LEV:]
    out[CAP : CAP + 8, :] = spill_block(spilled, shift)


def pack_far(outs, keys, both, spilled, shifts):
    block = spill_block(spilled, shifts[4])
    for which in range(2):
        one_hot = choose(keys, which)
        pack_payload(outs[which], one_hot, both, spilled, shifts[which])
        outs[which][CAP + 16 : CAP + 24, :] = jnp.where(shifts[which] * shifts[4] > 0, block, 0.0)
        yield one_hot


def first_far_kernel(tile_count, self_ref, field_hbm, departure_hbm, fraction_hbm, *refs):
    outs, (field, departure, fraction, sems) = refs[:-4], refs[-4:]
    copies = [
        pltpu.make_async_copy(departure_hbm, departure, sems.at[0]),
        pltpu.make_async_copy(fraction_hbm, fraction, sems.at[1]),
        pltpu.make_async_copy(field_hbm, field, sems.at[2]),
    ]
    for copy in copies:
        copy.start()
    copies[0].wait()
    copies[1].wait()
    place, offset, keys, weights = index_values(self_ref, departure[1:2, :], fraction[1:2, :], tile_count)
    meta = meta_rows(place, fraction[1:2, :])
    spills = spill_rows(place, offset, weights)
    copies[2].wait()
    high, low = halves(field[...])
    both = jnp.concatenate([high, low], axis=1)
    spilled = spill_sums(spills, both)
    outs[2][...] = both
    outs[3][...] = spilled
    outs[4][...] = keys
    outs[5][...] = meta
    for which, one_hot in enumerate(pack_far(outs, keys, both, spilled, signs(self_ref[0]))):
        write_meta(outs[which], CAP + 8, meta, one_hot)


def second_far_kernel(self_ref, field, keys, spills, meta, *outs):
    high, low = halves(field[...])
    both = jnp.concatenate([high, low], axis=1)
    spilled = spill_sums(spills[...], both)
    outs[2][...] = both
    outs[3][...] = spilled
    for which, _ in enumerate(pack_far(outs, keys[...], both, spilled, signs(self_ref[0]))):
        outs[which][CAP + 8 : CAP + 16, :] = meta[8 * which : 8 * which + 8, :]


def near_pack_kernel(step, self_ref, both, spilled, keys, meta, *outs):
    shifts = signs(self_ref[0])
    sums = spilled[...]
    outs[2][...] = spill_block(sums, shifts[5])
    outs[3][...] = spill_block(sums, 0)
    for out, which in zip(outs, (2, 3)):
        one_hot = choose(keys[...], which)
        pack_payload(out, one_hot, both[...], sums, shifts[which])
        if step == 1:
            write_meta(out, CAP + 8, meta[...], one_hot)
        else:
            out[CAP + 8 : CAP + 16, :] = meta[8 * which : 8 * which + 8, :]


def index_kernel(tile_count, self_ref, departure, fraction, keys_out, spill_out, meta_out):
    place, offset, keys, weights = index_values(self_ref, departure[0:1, :], fraction[0:1, :], tile_count)
    meta = meta_rows(place, fraction[0:1, :])
    keys_out[...] = keys
    spill_out[...] = spill_rows(place, offset, weights)
    for which in range(SWAPS):
        write_meta(meta_out, 8 * which, meta, choose(keys, which))


def second_pack_kernel(self_ref, field, keys, spills, meta, *outs):
    high, low = halves(field[...])
    both = jnp.concatenate([high, low], axis=1)
    spilled = spill_sums(spills[...], both)
    shifts = signs(self_ref[0])
    beyond(outs, spilled, shifts)
    outs[4][...] = spill_block(spilled, shifts[5])
    outs[5][...] = spill_block(spilled, 0)
    for which, shift in enumerate(shifts[:SWAPS]):
        pack_payload(outs[which], choose(keys[...], which), both, spilled, shift)
        outs[which][CAP + 8 : CAP + 16, :] = meta[8 * which : 8 * which + 8, :]


BLOCK = 512
I16 = jnp.int16


def tiled(x, rows):
    return jnp.concatenate([x] * (rows // 16), axis=0)


def spread_table(place, weights):
    shape = (16, place.shape[1])
    start = jnp.broadcast_to(place - 1, shape).astype(I16)
    return start, [halves(jnp.broadcast_to(w, shape)) for w in weights]


def spread_block(first_cell, table):
    start, weights = table
    columns = start.shape[1]
    cells = lax.broadcasted_iota(jnp.int32, (BLOCK, columns), 0).astype(I16)
    first = jnp.full((16, columns), first_cell, jnp.int32).astype(I16)
    distance = cells - tiled(start - first, BLOCK)
    high = jnp.zeros((BLOCK, columns), BF)
    low = high
    for k in range(4):
        here = distance == I16(k)
        high = jnp.where(here, tiled(weights[k][0], BLOCK), high)
        low = jnp.where(here, tiled(weights[k][1], BLOCK), low)
    return high, low


def own_kernel(step, tile_count, self_ref, field, departure, fraction, spilled, payload, out, own_ref, both_ref):
    departure = departure[step : step + 1, :]
    fraction = fraction[step : step + 1, :]
    place, offset = locate(departure, self_ref[0], tile_count)
    own_table = spread_table(place, [jnp.where(offset == 0, w, 0.0) for w in cubic_weights(fraction)])
    high, low = halves(field[...])
    own_ref[:, :LEV] = high
    own_ref[:, LEV:] = low
    table = payload_table(payload, both_ref, 0)

    @pl.loop(0, COLS // BLOCK)
    def _(b):
        high, low = spread_block(b * BLOCK, own_table)
        wide = dot(high, own_ref[...]) + dot(low, own_ref[...])
        high, low = spread_block(b * BLOCK, table)
        wide = wide + dot(high, both_ref[0]) + dot(low, both_ref[0])
        out[pl.ds(b * BLOCK, BLOCK), :] = wide[:, :LEV] + wide[:, LEV:]

    add_spill(out, spilled[...] + payload[CAP : CAP + 8, :])


def payload_table(payload, both_ref, which):
    high, low = halves(payload[0:CAP, :])
    both_ref[which, :, :LEV] = high
    both_ref[which, :, LEV:] = low
    rows = [payload[CAP + 8 + c : CAP + 9 + c, :] for c in range(8)]
    fraction = jnp.concatenate(rows[:4], axis=1)
    place = jnp.concatenate(rows[4:], axis=1).astype(jnp.int32)
    return spread_table(place, cubic_weights(fraction))


def add_spill(out, block):
    row = lax.broadcasted_iota(jnp.int32, (8, LEV), 0)
    out[0:8, :] = out[0:8, :] + jnp.where(row < 2, block, 0.0)
    out[COLS - 8 : COLS, :] = out[COLS - 8 : COLS, :] + jnp.where(row == 7, block, 0.0)


def deposit_block(b, start, tables, both_ref):
    wide = jnp.zeros((BLOCK, 2 * LEV), F32)
    for which, table in enumerate(tables):
        high, low = spread_block(b * BLOCK, table)
        wide = wide + dot(high, both_ref[which]) + dot(low, both_ref[which])
    return start[pl.ds(b * BLOCK, BLOCK), :] + wide[:, :LEV] + wide[:, LEV:]


def middle_kernel(start, p0, p1, out, both_ref):
    tables = [payload_table(p, both_ref, which) for which, p in enumerate((p0, p1))]

    @pl.loop(0, COLS // BLOCK)
    def _(b):
        out[pl.ds(b * BLOCK, BLOCK), :] = deposit_block(b, start, tables, both_ref)

    add_spill(out, p0[CAP : CAP + 8, :] + p1[CAP : CAP + 8, :])


def last_kernel(step, start, payload, tiny_a, tiny_b, level_map, out, both_ref, sum_ref, lifted_ref, sems):
    tables = [payload_table(payload, both_ref, 0)]

    @pl.loop(0, COLS // BLOCK)
    def _(b):
        sum_ref[pl.ds(b * BLOCK, BLOCK), :] = deposit_block(b, start, tables, both_ref)

    add_spill(sum_ref, payload[CAP : CAP + 8, :] + tiny_a[...] + tiny_b[...])
    map_high, map_low = halves(level_map[step])

    def lift(rows):
        high, low = halves(sum_ref[rows, :])
        return dot_nt(high, map_high) + (dot_nt(high, map_low) + dot_nt(low, map_high))

    if step == 1:
        out[...] = lift(slice(0, COLS))
        return
    copies = []
    for b in range(COLS // BLOCK):
        rows = slice(b * BLOCK, (b + 1) * BLOCK)
        lifted_ref[rows, :] = lift(rows)
        copies.append(pltpu.make_async_copy(lifted_ref.at[rows, :], out.at[rows, :], sems.at[b]))
        copies[-1].start()
    for copy in copies:
        copy.wait()


def couple_kernel(table, x, out):
    count = x.shape[0]

    @pl.loop(0, x.shape[1] // 8)
    def _(r):
        rows = [x[e, pl.ds(r * 8, 8), :] for e in range(count)]
        for b in range(count):
            total = rows[0] * table[count * b : count * b + 1, :]
            for e in range(1, count):
                total = total + rows[e] * table[count * b + e : count * b + e + 1, :]
            out[b, pl.ds(r * 8, 8), :] = total


VM = pl.BlockSpec(memory_space=pltpu.MemorySpace.VMEM)
HBM = pl.BlockSpec(memory_space=pltpu.MemorySpace.HBM)
SM = pl.BlockSpec(memory_space=pltpu.MemorySpace.SMEM)
PARAMS = pltpu.CompilerParams(vmem_limit_bytes=40 * 1024 * 1024)
SPREAD_ROWS = 8 * (2 * REACH + 1)
FAR = [
    jax.ShapeDtypeStruct((WIDE_ROWS, LEV), F32),
    jax.ShapeDtypeStruct((WIDE_ROWS, LEV), F32),
    jax.ShapeDtypeStruct((COLS, 2 * LEV), BF),
    jax.ShapeDtypeStruct((SPREAD_ROWS, LEV), F32),
]
NEAR = [jax.ShapeDtypeStruct((rows, LEV), F32) for rows in (ROWS, ROWS, 8, 8)]
KEYS = jax.ShapeDtypeStruct((1, COLS), jnp.int32)


def call(kernel, out_shape, in_specs, scratch=(), flops=0, out_spec=None):
    multiple = isinstance(out_shape, (list, tuple))
    return pl.pallas_call(
        kernel,
        out_shape=out_shape,
        in_specs=in_specs,
        out_specs=[VM] * len(out_shape) if multiple else out_spec or VM,
        scratch_shapes=list(scratch),
        compiler_params=PARAMS,
        cost_estimate=pl.CostEstimate(flops=flops, transcendentals=0, bytes_accessed=flops // 256),
    )


def transported(step, packed, keys, meta, tile_count, tile_self, field, departure, fraction, level_map):
    far = [swapped(packed[w], w) for w in (0, 1)]
    near = call(functools.partial(near_pack_kernel, step), NEAR, [SM] + [VM] * 4, (), 1000000000)(
        tile_self, packed[2], packed[3], keys, meta
    )
    cross = swapped(near[0], 2)
    partner = swapped(near[1], 3)
    late = lax.optimization_barrier((near[2], partner))
    tiny = swapped(late[0], 5)
    total = jax.ShapeDtypeStruct((COLS, LEV), F32)
    one = pltpu.VMEM((1, CAP, 2 * LEV), BF)
    work = 10000000
    own = call(
        functools.partial(own_kernel, step, tile_count),
        total,
        [SM] + [VM] * 5,
        [pltpu.VMEM((COLS, 2 * LEV), BF), one],
        10000000,
    )(tile_self, field, departure, fraction, near[3], partner)
    index = None
    if step == 1:
        after = lax.optimization_barrier((tile_self, own))
        index = call(
            functools.partial(index_kernel, tile_count),
            [
                KEYS,
                jax.ShapeDtypeStruct((2 * SPREAD_ROWS, COLS), BF),
                jax.ShapeDtypeStruct((32, LEV), F32),
            ],
            [SM, VM, VM],
            (),
            10000000,
        )(after[0], departure, fraction)
        own, index = lax.optimization_barrier((after[1], index))
    own, *far = lax.optimization_barrier((own, *far))
    handed = swapped(far[0][CAP + 16 :] + far[1][CAP + 16 :], 3)
    summed = call(middle_kernel, total, [VM] * 3, [pltpu.VMEM((2, CAP, 2 * LEV), BF)], work)(own, *far)
    result = call(
        functools.partial(last_kernel, step),
        total,
        [VM] * 5,
        [
            one,
            pltpu.VMEM((COLS, LEV), F32),
            pltpu.VMEM((COLS, LEV), F32),
            pltpu.SemaphoreType.DMA((COLS // BLOCK,)),
        ],
        work,
        HBM if step == 0 else VM,
    )(summed, cross, tiny, handed, level_map)
    return result, index


def body(adjoint_in, departure, fraction, level_map, coarse_map):
    tile_count = lax.axis_size("tile")
    groups = lax.axis_size("grp")
    tile_self = lax.axis_index("tile").astype(jnp.int32).reshape(1)
    first_scratch = [
        pltpu.VMEM((COLS, LEV), F32),
        pltpu.VMEM((2, COLS), jnp.int32),
        pltpu.VMEM((2, COLS), F32),
        pltpu.SemaphoreType.DMA((3,)),
    ]
    outputs = FAR + [KEYS, jax.ShapeDtypeStruct((8, COLS), BF)]
    packed = call(functools.partial(first_far_kernel, tile_count), outputs, [SM, HBM, HBM, HBM], first_scratch)(
        tile_self, *[pltpu.with_memory_space_constraint(x, pltpu.MemorySpace.HBM) for x in (adjoint_in, departure, fraction)]
    )
    table = coarse_map.transpose(1, 2, 0).reshape(groups * groups, LEV)
    second, index = transported(
        1, packed, packed[4], packed[5], tile_count, tile_self, adjoint_in, departure, fraction, level_map
    )

    parts = lax.all_to_all(second.reshape(groups, COLS // groups, LEV), "grp", 0, 0)
    mixed = call(couple_kernel, jax.ShapeDtypeStruct(parts.shape, F32), [VM, VM])(table, parts)
    coupled = lax.all_to_all(mixed, "grp", 0, 0).reshape(COLS, LEV)

    keys, spills, meta = index
    packed = call(second_far_kernel, FAR, [SM] + [VM] * 4)(tile_self, coupled, keys, spills, meta)
    return transported(
        0, packed, keys, meta, tile_count, tile_self, coupled, departure, fraction, level_map
    )[0]


def solution(mesh):
    return jax.shard_map(
        body,
        mesh=mesh,
        in_specs=(
            P(("grp", "tile"), None),
            P(None, ("grp", "tile")),
            P(None, ("grp", "tile")),
            P(),
            P(),
        ),
        out_specs=P(("grp", "tile"), None),
        check_vma=False,
    )
```

```python
import functools

import jax
import jax.numpy as jnp
from jax import lax
from jax.experimental import pallas as pl
from jax.experimental.pallas import tpu as pltpu
from jax.sharding import PartitionSpec as P

REACH = 2
SWAPS = 4
COLS = 1024
LEV = 128
CAP = 512
ROWS = CAP + 16
WIDE_ROWS = CAP + 24
BF = jnp.bfloat16
F32 = jnp.float32


def signs(tile):
    core = 1 - 2 * (tile % 2)
    chip = 1 - 2 * ((tile // 2) % 2)
    return (2 * chip, -2 * chip, -core, core, 3 * core, -3 * core)


def swapped(x, which):
    length = lax.axis_size("tile")
    return lax.ppermute(x, "tile", [(i, (i + signs(i)[which]) % length) for i in range(length)])


def halves(x):
    high = x.astype(BF)
    low = (x - high.astype(F32)).astype(BF)
    return high, low


def dot(a, b):
    return lax.dot_general(a, b, (((1,), (0,)), ((), ())), preferred_element_type=F32)


def dot_nt(a, b):
    return lax.dot_general(a, b, (((1,), (1,)), ((), ())), preferred_element_type=F32)


def cubic_weights(a):
    return (
        -a * (1.0 - a) * (2.0 - a) * (1.0 / 6.0),
        (1.0 + a) * (1.0 - a) * (2.0 - a) * 0.5,
        (1.0 + a) * a * (2.0 - a) * 0.5,
        -(1.0 + a) * a * (1.0 - a) * (1.0 / 6.0),
    )


def locate(departure, tile_self, tile_count):
    place = departure % COLS
    target = (departure // COLS) % tile_count
    offset = (target - tile_self + REACH + tile_count) % tile_count - REACH
    return place, offset


def slots_of(offset, shifts):
    row = lax.broadcasted_iota(jnp.int32, (8, LEV), 0)
    lane_a = lax.broadcasted_iota(jnp.int32, (LEV, LEV), 0)
    lane_b = lax.broadcasted_iota(jnp.int32, (LEV, LEV), 1)
    before = jnp.where(lane_a < lane_b, 1.0, 0.0).astype(BF)
    number = jnp.full((1, COLS), 4, jnp.int32)
    for which, shift in enumerate(shifts[:SWAPS]):
        number = jnp.where(offset == shift, which, number)
    members = []
    for c in range(COLS // LEV):
        part = number[:, c * LEV : (c + 1) * LEV]
        members.append(jnp.where(row == part, 1.0, 0.0))
    member = jnp.concatenate(members, axis=0)
    inside = dot(member.astype(BF), before)
    totals = jnp.sum(member, axis=1, keepdims=True)
    start = jnp.zeros((8, 1), F32)
    keys = []
    for c in range(COLS // LEV):
        block = slice(8 * c, 8 * c + 8)
        rank = inside[block] + start
        start = start + totals[block]
        key = jnp.sum(member[block] * (rank + row.astype(F32) * CAP), axis=0, keepdims=True)
        keys.append(key)
    return jnp.concatenate(keys, axis=1).astype(jnp.int32)


def spill_rows(place, offset, weights):
    row = lax.broadcasted_iota(jnp.int32, (8, COLS), 0)
    last = place == COLS - 1
    first_a = jnp.where(last, weights[2], jnp.where(place == COLS - 2, weights[3], 0.0))
    first_b = jnp.where(last, weights[3], 0.0)
    end = jnp.where(place == 0, weights[0], 0.0)
    rows = jnp.where(row == 0, first_a, jnp.where(row == 1, first_b, jnp.where(row == 7, end, 0.0)))
    spread = [jnp.where(offset == o, rows, 0.0) for o in range(-REACH, REACH + 1)]
    high, low = halves(jnp.concatenate(spread, axis=0))
    return jnp.concatenate([high, low], axis=0)


def meta_rows(place, fraction):
    a = fraction.astype(BF)
    rest = fraction - a.astype(F32)
    b = rest.astype(BF)
    c = rest - b.astype(F32)
    p_high = (place // 32).astype(F32)
    p_low = (place % 32).astype(F32)
    row = lax.broadcasted_iota(jnp.int32, (8, COLS), 0)
    out = jnp.where(row == 0, a.astype(F32), 0.0)
    out = jnp.where(row == 1, b.astype(F32), out)
    out = jnp.where(row == 2, c, out)
    out = jnp.where(row == 3, p_high, out)
    out = jnp.where(row == 4, p_low, out)
    return out.astype(BF)


def choose(keys, which):
    slot = lax.broadcasted_iota(jnp.int32, (CAP, COLS), 0).astype(jnp.int16)
    wanted = jnp.broadcast_to(keys - which * CAP, (16, COLS)).astype(jnp.int16)
    wanted = jnp.concatenate([wanted] * (CAP // 16), axis=0)
    return jnp.where(slot == wanted, BF(1.0), BF(0.0))


def spill_block(spilled, target):
    row = lax.broadcasted_iota(jnp.int32, (8, LEV), 0)
    from_cell = jnp.where(row < 2, target - 1, jnp.where(row == 7, target + 1, -9))
    out = jnp.zeros((8, LEV), F32)
    for o in range(-REACH, REACH + 1):
        block = spilled[8 * (o + REACH) : 8 * (o + REACH) + 8]
        out = out + jnp.where(from_cell == o, block, 0.0)
    return out


def spill_sums(spills, both):
    wide = dot(spills, both)
    count = 8 * (2 * REACH + 1)
    return (wide[:count, :LEV] + wide[:count, LEV:]) + (wide[count:, :LEV] + wide[count:, LEV:])


def index_values(self_ref, departure, fraction, tile_count):
    place, offset = locate(departure, self_ref[0], tile_count)
    keys = slots_of(offset, signs(self_ref[0]))
    weights = cubic_weights(fraction)
    return place, offset, keys, weights


def write_meta(meta_out, base, meta, one_hot):
    got = dot_nt(meta, one_hot)
    fraction = got[0:1] + got[1:2] + got[2:3]
    place = got[3:4] * 32.0 + got[4:5]
    for c in range(CAP // LEV):
        meta_out[base + c : base + c + 1, :] = fraction[:, c * LEV : (c + 1) * LEV]
        meta_out[base + 4 + c : base + 5 + c, :] = place[:, c * LEV : (c + 1) * LEV]


def pack_payload(out, one_hot, both, spilled, shift):
    wide = dot(one_hot, both)
    out[0:CAP, :] = wide[:, :LEV] + wide[:, LEV:]
    out[CAP : CAP + 8, :] = spill_block(spilled, shift)


def pack_far(outs, keys, both, spilled, shifts):
    block = spill_block(spilled, shifts[4])
    for which in range(2):
        one_hot = choose(keys, which)
        pack_payload(outs[which], one_hot, both, spilled, shifts[which])
        outs[which][CAP + 16 : CAP + 24, :] = jnp.where(shifts[which] * shifts[4] > 0, block, 0.0)
        yield one_hot


def first_far_kernel(tile_count, self_ref, field_hbm, departure_hbm, fraction_hbm, *refs):
    outs, (field, departure, fraction, sems) = refs[:-4], refs[-4:]
    copies = [
        pltpu.make_async_copy(departure_hbm, departure, sems.at[0]),
        pltpu.make_async_copy(fraction_hbm, fraction, sems.at[1]),
        pltpu.make_async_copy(field_hbm, field, sems.at[2]),
    ]
    for copy in copies:
        copy.start()
    copies[0].wait()
    copies[1].wait()
    place, offset, keys, weights = index_values(self_ref, departure[1:2, :], fraction[1:2, :], tile_count)
    meta = meta_rows(place, fraction[1:2, :])
    spills = spill_rows(place, offset, weights)
    copies[2].wait()
    high, low = halves(field[...])
    both = jnp.concatenate([high, low], axis=1)
    spilled = spill_sums(spills, both)
    outs[2][...] = both
    outs[3][...] = spilled
    outs[4][...] = keys
    outs[5][...] = meta
    for which, one_hot in enumerate(pack_far(outs, keys, both, spilled, signs(self_ref[0]))):
        write_meta(outs[which], CAP + 8, meta, one_hot)


def second_far_kernel(self_ref, field, keys, spills, meta, *outs):
    high, low = halves(field[...])
    both = jnp.concatenate([high, low], axis=1)
    spilled = spill_sums(spills[...], both)
    outs[2][...] = both
    outs[3][...] = spilled
    for which, _ in enumerate(pack_far(outs, keys[...], both, spilled, signs(self_ref[0]))):
        outs[which][CAP + 8 : CAP + 16, :] = meta[8 * which : 8 * which + 8, :]


def near_pack_kernel(step, self_ref, both, spilled, keys, meta, *outs):
    shifts = signs(self_ref[0])
    sums = spilled[...]
    outs[2][...] = spill_block(sums, shifts[5])
    outs[3][...] = spill_block(sums, 0)
    for out, which in zip(outs, (2, 3)):
        one_hot = choose(keys[...], which)
        pack_payload(out, one_hot, both[...], sums, shifts[which])
        if step == 1:
            write_meta(out, CAP + 8, meta[...], one_hot)
        else:
            out[CAP + 8 : CAP + 16, :] = meta[8 * which : 8 * which + 8, :]


def index_kernel(tile_count, self_ref, departure, fraction, keys_out, spill_out, meta_out):
    place, offset, keys, weights = index_values(self_ref, departure[0:1, :], fraction[0:1, :], tile_count)
    meta = meta_rows(place, fraction[0:1, :])
    keys_out[...] = keys
    spill_out[...] = spill_rows(place, offset, weights)
    for which in range(SWAPS):
        write_meta(meta_out, 8 * which, meta, choose(keys, which))


def second_pack_kernel(self_ref, field, keys, spills, meta, *outs):
    high, low = halves(field[...])
    both = jnp.concatenate([high, low], axis=1)
    spilled = spill_sums(spills[...], both)
    shifts = signs(self_ref[0])
    beyond(outs, spilled, shifts)
    outs[4][...] = spill_block(spilled, shifts[5])
    outs[5][...] = spill_block(spilled, 0)
    for which, shift in enumerate(shifts[:SWAPS]):
        pack_payload(outs[which], choose(keys[...], which), both, spilled, shift)
        outs[which][CAP + 8 : CAP + 16, :] = meta[8 * which : 8 * which + 8, :]


BLOCK = 512
I16 = jnp.int16


def tiled(x, rows):
    return jnp.concatenate([x] * (rows // 16), axis=0)


def spread_table(place, weights):
    shape = (16, place.shape[1])
    start = jnp.broadcast_to(place - 1, shape).astype(I16)
    return start, [halves(jnp.broadcast_to(w, shape)) for w in weights]


def spread_block(first_cell, table):
    start, weights = table
    columns = start.shape[1]
    cells = lax.broadcasted_iota(jnp.int32, (BLOCK, columns), 0).astype(I16)
    first = jnp.full((16, columns), first_cell, jnp.int32).astype(I16)
    distance = cells - tiled(start - first, BLOCK)
    high = jnp.zeros((BLOCK, columns), BF)
    low = high
    for k in range(4):
        here = distance == I16(k)
        high = jnp.where(here, tiled(weights[k][0], BLOCK), high)
        low = jnp.where(here, tiled(weights[k][1], BLOCK), low)
    return high, low


def own_kernel(step, tile_count, self_ref, field, departure, fraction, spilled, payload, out, own_ref, both_ref):
    departure = departure[step : step + 1, :]
    fraction = fraction[step : step + 1, :]
    place, offset = locate(departure, self_ref[0], tile_count)
    own_table = spread_table(place, [jnp.where(offset == 0, w, 0.0) for w in cubic_weights(fraction)])
    high, low = halves(field[...])
    own_ref[:, :LEV] = high
    own_ref[:, LEV:] = low
    table = payload_table(payload, both_ref, 0)

    @pl.loop(0, COLS // BLOCK)
    def _(b):
        high, low = spread_block(b * BLOCK, own_table)
        wide = dot(high, own_ref[...]) + dot(low, own_ref[...])
        high, low = spread_block(b * BLOCK, table)
        wide = wide + dot(high, both_ref[0]) + dot(low, both_ref[0])
        out[pl.ds(b * BLOCK, BLOCK), :] = wide[:, :LEV] + wide[:, LEV:]

    add_spill(out, spilled[...] + payload[CAP : CAP + 8, :])


def payload_table(payload, both_ref, which):
    high, low = halves(payload[0:CAP, :])
    both_ref[which, :, :LEV] = high
    both_ref[which, :, LEV:] = low
    rows = [payload[CAP + 8 + c : CAP + 9 + c, :] for c in range(8)]
    fraction = jnp.concatenate(rows[:4], axis=1)
    place = jnp.concatenate(rows[4:], axis=1).astype(jnp.int32)
    return spread_table(place, cubic_weights(fraction))


def add_spill(out, block):
    row = lax.broadcasted_iota(jnp.int32, (8, LEV), 0)
    out[0:8, :] = out[0:8, :] + jnp.where(row < 2, block, 0.0)
    out[COLS - 8 : COLS, :] = out[COLS - 8 : COLS, :] + jnp.where(row == 7, block, 0.0)


def deposit_block(b, start, tables, both_ref):
    wide = jnp.zeros((BLOCK, 2 * LEV), F32)
    for which, table in enumerate(tables):
        high, low = spread_block(b * BLOCK, table)
        wide = wide + dot(high, both_ref[which]) + dot(low, both_ref[which])
    return start[pl.ds(b * BLOCK, BLOCK), :] + wide[:, :LEV] + wide[:, LEV:]


def middle_kernel(start, p0, p1, out, both_ref):
    tables = [payload_table(p, both_ref, which) for which, p in enumerate((p0, p1))]

    @pl.loop(0, COLS // BLOCK)
    def _(b):
        out[pl.ds(b * BLOCK, BLOCK), :] = deposit_block(b, start, tables, both_ref)

    add_spill(out, p0[CAP : CAP + 8, :] + p1[CAP : CAP + 8, :])


def last_kernel(step, start, payload, tiny_a, tiny_b, level_map, out, both_ref, sum_ref, lifted_ref, sems):
    tables = [payload_table(payload, both_ref, 0)]

    @pl.loop(0, COLS // BLOCK)
    def _(b):
        sum_ref[pl.ds(b * BLOCK, BLOCK), :] = deposit_block(b, start, tables, both_ref)

    add_spill(sum_ref, payload[CAP : CAP + 8, :] + tiny_a[...] + tiny_b[...])
    map_high, map_low = halves(level_map[step])

    def lift(rows):
        high, low = halves(sum_ref[rows, :])
        return dot_nt(high, map_high) + (dot_nt(high, map_low) + dot_nt(low, map_high))

    if step == 1:
        out[...] = lift(slice(0, COLS))
        return
    copies = []
    for b in range(COLS // BLOCK):
        rows = slice(b * BLOCK, (b + 1) * BLOCK)
        lifted_ref[rows, :] = lift(rows)
        copies.append(pltpu.make_async_copy(lifted_ref.at[rows, :], out.at[rows, :], sems.at[b]))
        copies[-1].start()
    for copy in copies:
        copy.wait()


def couple_kernel(table, x, out):
    count = x.shape[0]

    @pl.loop(0, x.shape[1] // 8)
    def _(r):
        rows = [x[e, pl.ds(r * 8, 8), :] for e in range(count)]
        for b in range(count):
            total = rows[0] * table[count * b : count * b + 1, :]
            for e in range(1, count):
                total = total + rows[e] * table[count * b + e : count * b + e + 1, :]
            out[b, pl.ds(r * 8, 8), :] = total


VM = pl.BlockSpec(memory_space=pltpu.MemorySpace.VMEM)
HBM = pl.BlockSpec(memory_space=pltpu.MemorySpace.HBM)
SM = pl.BlockSpec(memory_space=pltpu.MemorySpace.SMEM)
PARAMS = pltpu.CompilerParams(vmem_limit_bytes=40 * 1024 * 1024)
SPREAD_ROWS = 8 * (2 * REACH + 1)
FAR = [
    jax.ShapeDtypeStruct((WIDE_ROWS, LEV), F32),
    jax.ShapeDtypeStruct((WIDE_ROWS, LEV), F32),
    jax.ShapeDtypeStruct((COLS, 2 * LEV), BF),
    jax.ShapeDtypeStruct((SPREAD_ROWS, LEV), F32),
]
NEAR = [jax.ShapeDtypeStruct((rows, LEV), F32) for rows in (ROWS, ROWS, 8, 8)]
KEYS = jax.ShapeDtypeStruct((1, COLS), jnp.int32)


def call(kernel, out_shape, in_specs, scratch=(), flops=0, out_spec=None):
    multiple = isinstance(out_shape, (list, tuple))
    return pl.pallas_call(
        kernel,
        out_shape=out_shape,
        in_specs=in_specs,
        out_specs=[VM] * len(out_shape) if multiple else out_spec or VM,
        scratch_shapes=list(scratch),
        compiler_params=PARAMS,
        cost_estimate=pl.CostEstimate(flops=flops, transcendentals=0, bytes_accessed=flops // 256),
    )


def transported(step, packed, keys, meta, tile_count, tile_self, field, departure, fraction, level_map):
    far = [swapped(packed[w], w) for w in (0, 1)]
    near = call(functools.partial(near_pack_kernel, step), NEAR, [SM] + [VM] * 4, (), 1000000000)(
        tile_self, packed[2], packed[3], keys, meta
    )
    cross = swapped(near[0], 2)
    partner = swapped(near[1], 3)
    late = lax.optimization_barrier((near[2], partner))
    tiny = swapped(late[0], 5)
    total = jax.ShapeDtypeStruct((COLS, LEV), F32)
    one = pltpu.VMEM((1, CAP, 2 * LEV), BF)
    work = 10000000
    own = call(
        functools.partial(own_kernel, step, tile_count),
        total,
        [SM] + [VM] * 5,
        [pltpu.VMEM((COLS, 2 * LEV), BF), one],
        10000000,
    )(tile_self, field, departure, fraction, near[3], partner)
    index = None
    if step == 1:
        after = lax.optimization_barrier((tile_self, own))
        index = call(
            functools.partial(index_kernel, tile_count),
            [
                KEYS,
                jax.ShapeDtypeStruct((2 * SPREAD_ROWS, COLS), BF),
                jax.ShapeDtypeStruct((32, LEV), F32),
            ],
            [SM, VM, VM],
            (),
            300000000,
        )(after[0], departure, fraction)
        own, index = lax.optimization_barrier((after[1], index))
    own, *far = lax.optimization_barrier((own, *far))
    handed = swapped(far[0][CAP + 16 :] + far[1][CAP + 16 :], 3)
    summed = call(middle_kernel, total, [VM] * 3, [pltpu.VMEM((2, CAP, 2 * LEV), BF)], work)(own, *far)
    result = call(
        functools.partial(last_kernel, step),
        total,
        [VM] * 5,
        [
            one,
            pltpu.VMEM((COLS, LEV), F32),
            pltpu.VMEM((COLS, LEV), F32),
            pltpu.SemaphoreType.DMA((COLS // BLOCK,)),
        ],
        work,
        HBM if step == 0 else VM,
    )(summed, cross, tiny, handed, level_map)
    return result, index


def body(adjoint_in, departure, fraction, level_map, coarse_map):
    tile_count = lax.axis_size("tile")
    groups = lax.axis_size("grp")
    tile_self = lax.axis_index("tile").astype(jnp.int32).reshape(1)
    first_scratch = [
        pltpu.VMEM((COLS, LEV), F32),
        pltpu.VMEM((2, COLS), jnp.int32),
        pltpu.VMEM((2, COLS), F32),
        pltpu.SemaphoreType.DMA((3,)),
    ]
    outputs = FAR + [KEYS, jax.ShapeDtypeStruct((8, COLS), BF)]
    packed = call(functools.partial(first_far_kernel, tile_count), outputs, [SM, HBM, HBM, HBM], first_scratch)(
        tile_self, *[pltpu.with_memory_space_constraint(x, pltpu.MemorySpace.HBM) for x in (adjoint_in, departure, fraction)]
    )
    table = coarse_map.transpose(1, 2, 0).reshape(groups * groups, LEV)
    second, index = transported(
        1, packed, packed[4], packed[5], tile_count, tile_self, adjoint_in, departure, fraction, level_map
    )

    parts = lax.all_to_all(second.reshape(groups, COLS // groups, LEV), "grp", 0, 0)
    mixed = call(couple_kernel, jax.ShapeDtypeStruct(parts.shape, F32), [VM, VM])(table, parts)
    coupled = lax.all_to_all(mixed, "grp", 0, 0).reshape(COLS, LEV)

    keys, spills, meta = index
    packed = call(second_far_kernel, FAR, [SM] + [VM] * 4)(tile_self, coupled, keys, spills, meta)
    return transported(
        0, packed, keys, meta, tile_count, tile_self, coupled, departure, fraction, level_map
    )[0]


def solution(mesh):
    return jax.shard_map(
        body,
        mesh=mesh,
        in_specs=(
            P(("grp", "tile"), None),
            P(None, ("grp", "tile")),
            P(None, ("grp", "tile")),
            P(),
            P(),
        ),
        out_specs=P(("grp", "tile"), None),
        check_vma=False,
    )
```

```python
import functools

import jax
import jax.numpy as jnp
from jax import lax
from jax.experimental import pallas as pl
from jax.experimental.pallas import tpu as pltpu
from jax.sharding import PartitionSpec as P

REACH = 2
SWAPS = 4
COLS = 1024
LEV = 128
CAP = 512
ROWS = CAP + 16
WIDE_ROWS = CAP + 24
BF = jnp.bfloat16
F32 = jnp.float32


def signs(tile):
    core = 1 - 2 * (tile % 2)
    chip = 1 - 2 * ((tile // 2) % 2)
    return (2 * chip, -2 * chip, -core, core, 3 * core, -3 * core)


def swapped(x, which):
    length = lax.axis_size("tile")
    return lax.ppermute(x, "tile", [(i, (i + signs(i)[which]) % length) for i in range(length)])


def halves(x):
    high = x.astype(BF)
    low = (x - high.astype(F32)).astype(BF)
    return high, low


def dot(a, b):
    return lax.dot_general(a, b, (((1,), (0,)), ((), ())), preferred_element_type=F32)


def dot_nt(a, b):
    return lax.dot_general(a, b, (((1,), (1,)), ((), ())), preferred_element_type=F32)


def cubic_weights(a):
    return (
        -a * (1.0 - a) * (2.0 - a) * (1.0 / 6.0),
        (1.0 + a) * (1.0 - a) * (2.0 - a) * 0.5,
        (1.0 + a) * a * (2.0 - a) * 0.5,
        -(1.0 + a) * a * (1.0 - a) * (1.0 / 6.0),
    )


def locate(departure, tile_self, tile_count):
    place = departure % COLS
    target = (departure // COLS) % tile_count
    offset = (target - tile_self + REACH + tile_count) % tile_count - REACH
    return place, offset


def slots_of(offset, shifts):
    row = lax.broadcasted_iota(jnp.int32, (8, LEV), 0)
    lane_a = lax.broadcasted_iota(jnp.int32, (LEV, LEV), 0)
    lane_b = lax.broadcasted_iota(jnp.int32, (LEV, LEV), 1)
    before = jnp.where(lane_a < lane_b, 1.0, 0.0).astype(BF)
    number = jnp.full((1, COLS), 4, jnp.int32)
    for which, shift in enumerate(shifts[:SWAPS]):
        number = jnp.where(offset == shift, which, number)
    members = []
    for c in range(COLS // LEV):
        part = number[:, c * LEV : (c + 1) * LEV]
        members.append(jnp.where(row == part, 1.0, 0.0))
    member = jnp.concatenate(members, axis=0)
    inside = dot(member.astype(BF), before)
    totals = jnp.sum(member, axis=1, keepdims=True)
    start = jnp.zeros((8, 1), F32)
    keys = []
    for c in range(COLS // LEV):
        block = slice(8 * c, 8 * c + 8)
        rank = inside[block] + start
        start = start + totals[block]
        key = jnp.sum(member[block] * (rank + row.astype(F32) * CAP), axis=0, keepdims=True)
        keys.append(key)
    return jnp.concatenate(keys, axis=1).astype(jnp.int32)


def spill_rows(place, offset, weights):
    row = lax.broadcasted_iota(jnp.int32, (8, COLS), 0)
    last = place == COLS - 1
    first_a = jnp.where(last, weights[2], jnp.where(place == COLS - 2, weights[3], 0.0))
    first_b = jnp.where(last, weights[3], 0.0)
    end = jnp.where(place == 0, weights[0], 0.0)
    rows = jnp.where(row == 0, first_a, jnp.where(row == 1, first_b, jnp.where(row == 7, end, 0.0)))
    spread = [jnp.where(offset == o, rows, 0.0) for o in range(-REACH, REACH + 1)]
    high, low = halves(jnp.concatenate(spread, axis=0))
    return jnp.concatenate([high, low], axis=0)


def meta_rows(place, fraction):
    a = fraction.astype(BF)
    rest = fraction - a.astype(F32)
    b = rest.astype(BF)
    c = rest - b.astype(F32)
    p_high = (place // 32).astype(F32)
    p_low = (place % 32).astype(F32)
    row = lax.broadcasted_iota(jnp.int32, (8, COLS), 0)
    out = jnp.where(row == 0, a.astype(F32), 0.0)
    out = jnp.where(row == 1, b.astype(F32), out)
    out = jnp.where(row == 2, c, out)
    out = jnp.where(row == 3, p_high, out)
    out = jnp.where(row == 4, p_low, out)
    return out.astype(BF)


def choose(keys, which):
    slot = lax.broadcasted_iota(jnp.int32, (CAP, COLS), 0).astype(jnp.int16)
    wanted = jnp.broadcast_to(keys - which * CAP, (16, COLS)).astype(jnp.int16)
    wanted = jnp.concatenate([wanted] * (CAP // 16), axis=0)
    return jnp.where(slot == wanted, BF(1.0), BF(0.0))


def spill_block(spilled, target):
    row = lax.broadcasted_iota(jnp.int32, (8, LEV), 0)
    from_cell = jnp.where(row < 2, target - 1, jnp.where(row == 7, target + 1, -9))
    out = jnp.zeros((8, LEV), F32)
    for o in range(-REACH, REACH + 1):
        block = spilled[8 * (o + REACH) : 8 * (o + REACH) + 8]
        out = out + jnp.where(from_cell == o, block, 0.0)
    return out


def spill_sums(spills, both):
    wide = dot(spills, both)
    count = 8 * (2 * REACH + 1)
    return (wide[:count, :LEV] + wide[:count, LEV:]) + (wide[count:, :LEV] + wide[count:, LEV:])


def index_values(self_ref, departure, fraction, tile_count):
    place, offset = locate(departure, self_ref[0], tile_count)
    keys = slots_of(offset, signs(self_ref[0]))
    weights = cubic_weights(fraction)
    return place, offset, keys, weights


def write_meta(meta_out, base, meta, one_hot):
    got = dot_nt(meta, one_hot)
    fraction = got[0:1] + got[1:2] + got[2:3]
    place = got[3:4] * 32.0 + got[4:5]
    for c in range(CAP // LEV):
        meta_out[base + c : base + c + 1, :] = fraction[:, c * LEV : (c + 1) * LEV]
        meta_out[base + 4 + c : base + 5 + c, :] = place[:, c * LEV : (c + 1) * LEV]


def pack_payload(out, one_hot, both, spilled, shift):
    wide = dot(one_hot, both)
    out[0:CAP, :] = wide[:, :LEV] + wide[:, LEV:]
    out[CAP : CAP + 8, :] = spill_block(spilled, shift)


def pack_far(outs, keys, both, spilled, shifts):
    block = spill_block(spilled, shifts[4])
    for which in range(2):
        one_hot = choose(keys, which)
        pack_payload(outs[which], one_hot, both, spilled, shifts[which])
        outs[which][CAP + 16 : CAP + 24, :] = jnp.where(shifts[which] * shifts[4] > 0, block, 0.0)
        yield one_hot


def first_far_kernel(tile_count, self_ref, field_hbm, departure_hbm, fraction_hbm, *refs):
    outs, (field, departure, fraction, sems) = refs[:-4], refs[-4:]
    copies = [
        pltpu.make_async_copy(departure_hbm, departure, sems.at[0]),
        pltpu.make_async_copy(fraction_hbm, fraction, sems.at[1]),
        pltpu.make_async_copy(field_hbm, field, sems.at[2]),
    ]
    for copy in copies:
        copy.start()
    copies[0].wait()
    copies[1].wait()
    place, offset, keys, weights = index_values(self_ref, departure[1:2, :], fraction[1:2, :], tile_count)
    meta = meta_rows(place, fraction[1:2, :])
    spills = spill_rows(place, offset, weights)
    copies[2].wait()
    high, low = halves(field[...])
    both = jnp.concatenate([high, low], axis=1)
    spilled = spill_sums(spills, both)
    outs[2][...] = both
    outs[3][...] = spilled
    outs[4][...] = keys
    outs[5][...] = meta
    for which, one_hot in enumerate(pack_far(outs, keys, both, spilled, signs(self_ref[0]))):
        write_meta(outs[which], CAP + 8, meta, one_hot)


def second_far_kernel(self_ref, field, keys, spills, meta, *outs):
    high, low = halves(field[...])
    both = jnp.concatenate([high, low], axis=1)
    spilled = spill_sums(spills[...], both)
    outs[2][...] = both
    outs[3][...] = spilled
    for which, _ in enumerate(pack_far(outs, keys[...], both, spilled, signs(self_ref[0]))):
        outs[which][CAP + 8 : CAP + 16, :] = meta[8 * which : 8 * which + 8, :]


def near_pack_kernel(step, self_ref, both, spilled, keys, meta, *outs):
    shifts = signs(self_ref[0])
    sums = spilled[...]
    outs[2][...] = spill_block(sums, shifts[5])
    outs[3][...] = spill_block(sums, 0)
    for out, which in zip(outs, (2, 3)):
        one_hot = choose(keys[...], which)
        pack_payload(out, one_hot, both[...], sums, shifts[which])
        if step == 1:
            write_meta(out, CAP + 8, meta[...], one_hot)
        else:
            out[CAP + 8 : CAP + 16, :] = meta[8 * which : 8 * which + 8, :]


def index_kernel(tile_count, self_ref, departure, fraction, keys_out, spill_out, meta_out):
    place, offset, keys, weights = index_values(self_ref, departure[0:1, :], fraction[0:1, :], tile_count)
    meta = meta_rows(place, fraction[0:1, :])
    keys_out[...] = keys
    spill_out[...] = spill_rows(place, offset, weights)
    for which in range(SWAPS):
        write_meta(meta_out, 8 * which, meta, choose(keys, which))


def second_pack_kernel(self_ref, field, keys, spills, meta, *outs):
    high, low = halves(field[...])
    both = jnp.concatenate([high, low], axis=1)
    spilled = spill_sums(spills[...], both)
    shifts = signs(self_ref[0])
    beyond(outs, spilled, shifts)
    outs[4][...] = spill_block(spilled, shifts[5])
    outs[5][...] = spill_block(spilled, 0)
    for which, shift in enumerate(shifts[:SWAPS]):
        pack_payload(outs[which], choose(keys[...], which), both, spilled, shift)
        outs[which][CAP + 8 : CAP + 16, :] = meta[8 * which : 8 * which + 8, :]


BLOCK = 512
I16 = jnp.int16


def tiled(x, rows):
    return jnp.concatenate([x] * (rows // 16), axis=0)


def spread_table(place, weights):
    shape = (16, place.shape[1])
    start = jnp.broadcast_to(place - 1, shape).astype(I16)
    return start, [halves(jnp.broadcast_to(w, shape)) for w in weights]


def spread_block(first_cell, table):
    start, weights = table
    columns = start.shape[1]
    cells = lax.broadcasted_iota(jnp.int32, (BLOCK, columns), 0).astype(I16)
    first = jnp.full((16, columns), first_cell, jnp.int32).astype(I16)
    distance = cells - tiled(start - first, BLOCK)
    high = jnp.zeros((BLOCK, columns), BF)
    low = high
    for k in range(4):
        here = distance == I16(k)
        high = jnp.where(here, tiled(weights[k][0], BLOCK), high)
        low = jnp.where(here, tiled(weights[k][1], BLOCK), low)
    return high, low


def own_kernel(step, tile_count, self_ref, field, departure, fraction, spilled, payload, out, own_ref, both_ref):
    departure = departure[step : step + 1, :]
    fraction = fraction[step : step + 1, :]
    place, offset = locate(departure, self_ref[0], tile_count)
    own_table = spread_table(place, [jnp.where(offset == 0, w, 0.0) for w in cubic_weights(fraction)])
    high, low = halves(field[...])
    own_ref[:, :LEV] = high
    own_ref[:, LEV:] = low
    table = payload_table(payload, both_ref, 0)

    @pl.loop(0, COLS // BLOCK)
    def _(b):
        high, low = spread_block(b * BLOCK, own_table)
        wide = dot(high, own_ref[...]) + dot(low, own_ref[...])
        high, low = spread_block(b * BLOCK, table)
        wide = wide + dot(high, both_ref[0]) + dot(low, both_ref[0])
        out[pl.ds(b * BLOCK, BLOCK), :] = wide[:, :LEV] + wide[:, LEV:]

    add_spill(out, spilled[...] + payload[CAP : CAP + 8, :])


def payload_table(payload, both_ref, which):
    high, low = halves(payload[0:CAP, :])
    both_ref[which, :, :LEV] = high
    both_ref[which, :, LEV:] = low
    rows = [payload[CAP + 8 + c : CAP + 9 + c, :] for c in range(8)]
    fraction = jnp.concatenate(rows[:4], axis=1)
    place = jnp.concatenate(rows[4:], axis=1).astype(jnp.int32)
    return spread_table(place, cubic_weights(fraction))


def add_spill(out, block):
    row = lax.broadcasted_iota(jnp.int32, (8, LEV), 0)
    out[0:8, :] = out[0:8, :] + jnp.where(row < 2, block, 0.0)
    out[COLS - 8 : COLS, :] = out[COLS - 8 : COLS, :] + jnp.where(row == 7, block, 0.0)


def deposit_block(b, start, tables, both_ref):
    wide = jnp.zeros((BLOCK, 2 * LEV), F32)
    for which, table in enumerate(tables):
        high, low = spread_block(b * BLOCK, table)
        wide = wide + dot(high, both_ref[which]) + dot(low, both_ref[which])
    return start[pl.ds(b * BLOCK, BLOCK), :] + wide[:, :LEV] + wide[:, LEV:]


def middle_kernel(start, p0, p1, out, both_ref):
    tables = [payload_table(p, both_ref, which) for which, p in enumerate((p0, p1))]

    @pl.loop(0, COLS // BLOCK)
    def _(b):
        out[pl.ds(b * BLOCK, BLOCK), :] = deposit_block(b, start, tables, both_ref)

    add_spill(out, p0[CAP : CAP + 8, :] + p1[CAP : CAP + 8, :])


def last_kernel(step, start, payload, tiny_a, tiny_b, level_map, out, both_ref, sum_ref, lifted_ref, sems):
    tables = [payload_table(payload, both_ref, 0)]

    @pl.loop(0, COLS // BLOCK)
    def _(b):
        sum_ref[pl.ds(b * BLOCK, BLOCK), :] = deposit_block(b, start, tables, both_ref)

    add_spill(sum_ref, payload[CAP : CAP + 8, :] + tiny_a[...] + tiny_b[...])
    map_high, map_low = halves(level_map[step])

    def lift(rows):
        high, low = halves(sum_ref[rows, :])
        return dot_nt(high, map_high) + (dot_nt(high, map_low) + dot_nt(low, map_high))

    if step == 1:
        out[...] = lift(slice(0, COLS))
        return
    copies = []
    for b in range(COLS // BLOCK):
        rows = slice(b * BLOCK, (b + 1) * BLOCK)
        lifted_ref[rows, :] = lift(rows)
        copies.append(pltpu.make_async_copy(lifted_ref.at[rows, :], out.at[rows, :], sems.at[b]))
        copies[-1].start()
    for copy in copies:
        copy.wait()


def couple_kernel(table, x, out):
    count = x.shape[0]

    @pl.loop(0, x.shape[1] // 8)
    def _(r):
        rows = [x[e, pl.ds(r * 8, 8), :] for e in range(count)]
        for b in range(count):
            total = rows[0] * table[count * b : count * b + 1, :]
            for e in range(1, count):
                total = total + rows[e] * table[count * b + e : count * b + e + 1, :]
            out[b, pl.ds(r * 8, 8), :] = total


VM = pl.BlockSpec(memory_space=pltpu.MemorySpace.VMEM)
HBM = pl.BlockSpec(memory_space=pltpu.MemorySpace.HBM)
SM = pl.BlockSpec(memory_space=pltpu.MemorySpace.SMEM)
PARAMS = pltpu.CompilerParams(vmem_limit_bytes=40 * 1024 * 1024)
SPREAD_ROWS = 8 * (2 * REACH + 1)
FAR = [
    jax.ShapeDtypeStruct((WIDE_ROWS, LEV), F32),
    jax.ShapeDtypeStruct((WIDE_ROWS, LEV), F32),
    jax.ShapeDtypeStruct((COLS, 2 * LEV), BF),
    jax.ShapeDtypeStruct((SPREAD_ROWS, LEV), F32),
]
NEAR = [jax.ShapeDtypeStruct((rows, LEV), F32) for rows in (ROWS, ROWS, 8, 8)]
KEYS = jax.ShapeDtypeStruct((1, COLS), jnp.int32)


def call(kernel, out_shape, in_specs, scratch=(), flops=0, out_spec=None):
    multiple = isinstance(out_shape, (list, tuple))
    return pl.pallas_call(
        kernel,
        out_shape=out_shape,
        in_specs=in_specs,
        out_specs=[VM] * len(out_shape) if multiple else out_spec or VM,
        scratch_shapes=list(scratch),
        compiler_params=PARAMS,
        cost_estimate=pl.CostEstimate(flops=flops, transcendentals=0, bytes_accessed=flops // 256),
    )


def transported(step, packed, keys, meta, tile_count, tile_self, field, departure, fraction, level_map):
    near = call(functools.partial(near_pack_kernel, step), NEAR, [SM] + [VM] * 4, (), 10**9)(
        tile_self, packed[2], packed[3], keys, meta
    )
    index = None
    ready = packed[:2]
    if step == 1:
        after = lax.optimization_barrier((tile_self, near))
        index = call(
            functools.partial(index_kernel, tile_count),
            [
                KEYS,
                jax.ShapeDtypeStruct((2 * SPREAD_ROWS, COLS), BF),
                jax.ShapeDtypeStruct((32, LEV), F32),
            ],
            [SM, VM, VM],
            (),
            3 * 10**8,
        )(after[0], departure, fraction)
        near = after[1]
        ready, near, index = lax.optimization_barrier((ready, near, index))
    far = [swapped(x, w) for w, x in enumerate(ready)]
    cross = swapped(near[0], 2)
    partner = swapped(near[1], 3)
    late = lax.optimization_barrier((near[2], partner))
    tiny = swapped(late[0], 5)
    total = jax.ShapeDtypeStruct((COLS, LEV), F32)
    one = pltpu.VMEM((1, CAP, 2 * LEV), BF)
    work = 10000000
    own = call(
        functools.partial(own_kernel, step, tile_count),
        total,
        [SM] + [VM] * 5,
        [pltpu.VMEM((COLS, 2 * LEV), BF), one],
        10000000,
    )(tile_self, field, departure, fraction, near[3], partner)
    own, *far = lax.optimization_barrier((own, *far))
    handed = swapped(far[0][CAP + 16 :] + far[1][CAP + 16 :], 3)
    summed = call(middle_kernel, total, [VM] * 3, [pltpu.VMEM((2, CAP, 2 * LEV), BF)], work)(own, *far)
    result = call(
        functools.partial(last_kernel, step),
        total,
        [VM] * 5,
        [
            one,
            pltpu.VMEM((COLS, LEV), F32),
            pltpu.VMEM((COLS, LEV), F32),
            pltpu.SemaphoreType.DMA((COLS // BLOCK,)),
        ],
        work,
        HBM if step == 0 else VM,
    )(summed, cross, tiny, handed, level_map)
    return result, index


def body(adjoint_in, departure, fraction, level_map, coarse_map):
    tile_count = lax.axis_size("tile")
    groups = lax.axis_size("grp")
    tile_self = lax.axis_index("tile").astype(jnp.int32).reshape(1)
    first_scratch = [
        pltpu.VMEM((COLS, LEV), F32),
        pltpu.VMEM((2, COLS), jnp.int32),
        pltpu.VMEM((2, COLS), F32),
        pltpu.SemaphoreType.DMA((3,)),
    ]
    outputs = FAR + [KEYS, jax.ShapeDtypeStruct((8, COLS), BF)]
    packed = call(functools.partial(first_far_kernel, tile_count), outputs, [SM, HBM, HBM, HBM], first_scratch)(
        tile_self, *[pltpu.with_memory_space_constraint(x, pltpu.MemorySpace.HBM) for x in (adjoint_in, departure, fraction)]
    )
    table = coarse_map.transpose(1, 2, 0).reshape(groups * groups, LEV)
    second, index = transported(
        1, packed, packed[4], packed[5], tile_count, tile_self, adjoint_in, departure, fraction, level_map
    )

    parts = lax.all_to_all(second.reshape(groups, COLS // groups, LEV), "grp", 0, 0)
    mixed = call(couple_kernel, jax.ShapeDtypeStruct(parts.shape, F32), [VM, VM])(table, parts)
    coupled = lax.all_to_all(mixed, "grp", 0, 0).reshape(COLS, LEV)

    keys, spills, meta = index
    packed = call(second_far_kernel, FAR, [SM] + [VM] * 4)(tile_self, coupled, keys, spills, meta)
    return transported(
        0, packed, keys, meta, tile_count, tile_self, coupled, departure, fraction, level_map
    )[0]


def solution(mesh):
    return jax.shard_map(
        body,
        mesh=mesh,
        in_specs=(
            P(("grp", "tile"), None),
            P(None, ("grp", "tile")),
            P(None, ("grp", "tile")),
            P(),
            P(),
        ),
        out_specs=P(("grp", "tile"), None),
        check_vma=False,
    )
```

```python
import functools

import jax
import jax.numpy as jnp
from jax import lax
from jax.experimental import pallas as pl
from jax.experimental.pallas import tpu as pltpu
from jax.sharding import PartitionSpec as P

REACH = 2
SWAPS = 4
COLS = 1024
LEV = 128
CAP = 512
ROWS = CAP + 16
WIDE_ROWS = CAP + 24
BF = jnp.bfloat16
F32 = jnp.float32


def signs(tile):
    core = 1 - 2 * (tile % 2)
    chip = 1 - 2 * ((tile // 2) % 2)
    return (2 * chip, -2 * chip, -core, core, 3 * core, -3 * core)


def swapped(x, which):
    length = lax.axis_size("tile")
    return lax.ppermute(x, "tile", [(i, (i + signs(i)[which]) % length) for i in range(length)])


def halves(x):
    high = x.astype(BF)
    low = (x - high.astype(F32)).astype(BF)
    return high, low


def dot(a, b):
    return lax.dot_general(a, b, (((1,), (0,)), ((), ())), preferred_element_type=F32)


def dot_nt(a, b):
    return lax.dot_general(a, b, (((1,), (1,)), ((), ())), preferred_element_type=F32)


def cubic_weights(a):
    return (
        -a * (1.0 - a) * (2.0 - a) * (1.0 / 6.0),
        (1.0 + a) * (1.0 - a) * (2.0 - a) * 0.5,
        (1.0 + a) * a * (2.0 - a) * 0.5,
        -(1.0 + a) * a * (1.0 - a) * (1.0 / 6.0),
    )


def locate(departure, tile_self, tile_count):
    place = departure % COLS
    target = (departure // COLS) % tile_count
    offset = (target - tile_self + REACH + tile_count) % tile_count - REACH
    return place, offset


def slots_of(offset, shifts):
    row = lax.broadcasted_iota(jnp.int32, (8, LEV), 0)
    lane_a = lax.broadcasted_iota(jnp.int32, (LEV, LEV), 0)
    lane_b = lax.broadcasted_iota(jnp.int32, (LEV, LEV), 1)
    before = jnp.where(lane_a < lane_b, 1.0, 0.0).astype(BF)
    number = jnp.full((1, COLS), 4, jnp.int32)
    for which, shift in enumerate(shifts[:SWAPS]):
        number = jnp.where(offset == shift, which, number)
    members = []
    for c in range(COLS // LEV):
        part = number[:, c * LEV : (c + 1) * LEV]
        members.append(jnp.where(row == part, 1.0, 0.0))
    member = jnp.concatenate(members, axis=0)
    inside = dot(member.astype(BF), before)
    totals = jnp.sum(member, axis=1, keepdims=True)
    start = jnp.zeros((8, 1), F32)
    keys = []
    for c in range(COLS // LEV):
        block = slice(8 * c, 8 * c + 8)
        rank = inside[block] + start
        start = start + totals[block]
        key = jnp.sum(member[block] * (rank + row.astype(F32) * CAP), axis=0, keepdims=True)
        keys.append(key)
    return jnp.concatenate(keys, axis=1).astype(jnp.int32)


def spill_rows(place, offset, weights):
    row = lax.broadcasted_iota(jnp.int32, (8, COLS), 0)
    last = place == COLS - 1
    first_a = jnp.where(last, weights[2], jnp.where(place == COLS - 2, weights[3], 0.0))
    first_b = jnp.where(last, weights[3], 0.0)
    end = jnp.where(place == 0, weights[0], 0.0)
    rows = jnp.where(row == 0, first_a, jnp.where(row == 1, first_b, jnp.where(row == 7, end, 0.0)))
    spread = [jnp.where(offset == o, rows, 0.0) for o in range(-REACH, REACH + 1)]
    high, low = halves(jnp.concatenate(spread, axis=0))
    return jnp.concatenate([high, low], axis=0)


def meta_rows(place, fraction):
    a = fraction.astype(BF)
    rest = fraction - a.astype(F32)
    b = rest.astype(BF)
    c = rest - b.astype(F32)
    p_high = (place // 32).astype(F32)
    p_low = (place % 32).astype(F32)
    row = lax.broadcasted_iota(jnp.int32, (8, COLS), 0)
    out = jnp.where(row == 0, a.astype(F32), 0.0)
    out = jnp.where(row == 1, b.astype(F32), out)
    out = jnp.where(row == 2, c, out)
    out = jnp.where(row == 3, p_high, out)
    out = jnp.where(row == 4, p_low, out)
    return out.astype(BF)


def choose(keys, which):
    slot = lax.broadcasted_iota(jnp.int32, (CAP, COLS), 0).astype(jnp.int16)
    wanted = jnp.broadcast_to(keys - which * CAP, (16, COLS)).astype(jnp.int16)
    wanted = jnp.concatenate([wanted] * (CAP // 16), axis=0)
    return jnp.where(slot == wanted, BF(1.0), BF(0.0))


def spill_block(spilled, target):
    row = lax.broadcasted_iota(jnp.int32, (8, LEV), 0)
    from_cell = jnp.where(row < 2, target - 1, jnp.where(row == 7, target + 1, -9))
    out = jnp.zeros((8, LEV), F32)
    for o in range(-REACH, REACH + 1):
        block = spilled[8 * (o + REACH) : 8 * (o + REACH) + 8]
        out = out + jnp.where(from_cell == o, block, 0.0)
    return out


def spill_sums(spills, both):
    wide = dot(spills, both)
    count = 8 * (2 * REACH + 1)
    return (wide[:count, :LEV] + wide[:count, LEV:]) + (wide[count:, :LEV] + wide[count:, LEV:])


def index_values(self_ref, departure, fraction, tile_count):
    place, offset = locate(departure, self_ref[0], tile_count)
    keys = slots_of(offset, signs(self_ref[0]))
    weights = cubic_weights(fraction)
    return place, offset, keys, weights


def write_meta(meta_out, base, meta, one_hot):
    got = dot_nt(meta, one_hot)
    fraction = got[0:1] + got[1:2] + got[2:3]
    place = got[3:4] * 32.0 + got[4:5]
    for c in range(CAP // LEV):
        meta_out[base + c : base + c + 1, :] = fraction[:, c * LEV : (c + 1) * LEV]
        meta_out[base + 4 + c : base + 5 + c, :] = place[:, c * LEV : (c + 1) * LEV]


def pack_payload(out, one_hot, both, spilled, shift):
    wide = dot(one_hot, both)
    out[0:CAP, :] = wide[:, :LEV] + wide[:, LEV:]
    out[CAP : CAP + 8, :] = spill_block(spilled, shift)


def pack_far(outs, keys, both, spilled, shifts):
    block = spill_block(spilled, shifts[4])
    for which in range(2):
        one_hot = choose(keys, which)
        pack_payload(outs[which], one_hot, both, spilled, shifts[which])
        outs[which][CAP + 16 : CAP + 24, :] = jnp.where(shifts[which] * shifts[4] > 0, block, 0.0)
        yield one_hot


def first_far_kernel(tile_count, self_ref, field_hbm, departure_hbm, fraction_hbm, *refs):
    outs, (field, departure, fraction, sems) = refs[:-4], refs[-4:]
    copies = [
        pltpu.make_async_copy(departure_hbm, departure, sems.at[0]),
        pltpu.make_async_copy(fraction_hbm, fraction, sems.at[1]),
        pltpu.make_async_copy(field_hbm, field, sems.at[2]),
    ]
    for copy in copies:
        copy.start()
    copies[0].wait()
    copies[1].wait()
    place, offset, keys, weights = index_values(self_ref, departure[1:2, :], fraction[1:2, :], tile_count)
    meta = meta_rows(place, fraction[1:2, :])
    spills = spill_rows(place, offset, weights)
    copies[2].wait()
    high, low = halves(field[...])
    both = jnp.concatenate([high, low], axis=1)
    spilled = spill_sums(spills, both)
    outs[2][...] = both
    outs[3][...] = spilled
    outs[4][...] = keys
    outs[5][...] = meta
    for which, one_hot in enumerate(pack_far(outs, keys, both, spilled, signs(self_ref[0]))):
        write_meta(outs[which], CAP + 8, meta, one_hot)


def second_far_kernel(self_ref, field, keys, spills, meta, *outs):
    high, low = halves(field[...])
    both = jnp.concatenate([high, low], axis=1)
    spilled = spill_sums(spills[...], both)
    outs[2][...] = both
    outs[3][...] = spilled
    for which, _ in enumerate(pack_far(outs, keys[...], both, spilled, signs(self_ref[0]))):
        outs[which][CAP + 8 : CAP + 16, :] = meta[8 * which : 8 * which + 8, :]


def near_pack_kernel(step, self_ref, both, spilled, keys, meta, *outs):
    shifts = signs(self_ref[0])
    sums = spilled[...]
    outs[2][...] = spill_block(sums, shifts[5])
    outs[3][...] = spill_block(sums, 0)
    for out, which in zip(outs, (2, 3)):
        one_hot = choose(keys[...], which)
        pack_payload(out, one_hot, both[...], sums, shifts[which])
        if step == 1:
            write_meta(out, CAP + 8, meta[...], one_hot)
        else:
            out[CAP + 8 : CAP + 16, :] = meta[8 * which : 8 * which + 8, :]


def index_kernel(tile_count, self_ref, departure, fraction, keys_out, spill_out, meta_out):
    place, offset, keys, weights = index_values(self_ref, departure[0:1, :], fraction[0:1, :], tile_count)
    meta = meta_rows(place, fraction[0:1, :])
    keys_out[...] = keys
    spill_out[...] = spill_rows(place, offset, weights)
    for which in range(SWAPS):
        write_meta(meta_out, 8 * which, meta, choose(keys, which))


def second_pack_kernel(self_ref, field, keys, spills, meta, *outs):
    high, low = halves(field[...])
    both = jnp.concatenate([high, low], axis=1)
    spilled = spill_sums(spills[...], both)
    shifts = signs(self_ref[0])
    beyond(outs, spilled, shifts)
    outs[4][...] = spill_block(spilled, shifts[5])
    outs[5][...] = spill_block(spilled, 0)
    for which, shift in enumerate(shifts[:SWAPS]):
        pack_payload(outs[which], choose(keys[...], which), both, spilled, shift)
        outs[which][CAP + 8 : CAP + 16, :] = meta[8 * which : 8 * which + 8, :]


BLOCK = 1024
HALF = 512
I16 = jnp.int16


def tiled(x, rows):
    return jnp.concatenate([x] * (rows // 16), axis=0)


def spread_table(place, weights):
    shape = (16, place.shape[1])
    start = jnp.broadcast_to(place - 1, shape).astype(I16)
    return start, [halves(jnp.broadcast_to(w, shape)) for w in weights]


def spread_block(first_cell, table):
    start, weights = table
    columns = start.shape[1]
    cells = lax.broadcasted_iota(jnp.int32, (BLOCK, columns), 0).astype(I16)
    first = jnp.full((16, columns), first_cell, jnp.int32).astype(I16)
    distance = cells - tiled(start - first, BLOCK)
    high = jnp.zeros((BLOCK, columns), BF)
    low = high
    for k in range(4):
        here = distance == I16(k)
        high = jnp.where(here, tiled(weights[k][0], BLOCK), high)
        low = jnp.where(here, tiled(weights[k][1], BLOCK), low)
    return high, low


def own_kernel(step, tile_count, self_ref, field, departure, fraction, spilled, payload, out, own_ref, both_ref):
    departure = departure[step : step + 1, :]
    fraction = fraction[step : step + 1, :]
    place, offset = locate(departure, self_ref[0], tile_count)
    own_table = spread_table(place, [jnp.where(offset == 0, w, 0.0) for w in cubic_weights(fraction)])
    high, low = halves(field[...])
    own_ref[:, :LEV] = high
    own_ref[:, LEV:] = low
    table = payload_table(payload, both_ref, 0)

    @pl.loop(0, COLS // BLOCK)
    def _(b):
        high, low = spread_block(b * BLOCK, own_table)
        wide = dot(high, own_ref[...]) + dot(low, own_ref[...])
        high, low = spread_block(b * BLOCK, table)
        wide = wide + dot(high, both_ref[0]) + dot(low, both_ref[0])
        out[pl.ds(b * BLOCK, BLOCK), :] = wide[:, :LEV] + wide[:, LEV:]

    add_spill(out, spilled[...] + payload[CAP : CAP + 8, :])


def payload_table(payload, both_ref, which):
    high, low = halves(payload[0:CAP, :])
    both_ref[which, :, :LEV] = high
    both_ref[which, :, LEV:] = low
    rows = [payload[CAP + 8 + c : CAP + 9 + c, :] for c in range(8)]
    fraction = jnp.concatenate(rows[:4], axis=1)
    place = jnp.concatenate(rows[4:], axis=1).astype(jnp.int32)
    return spread_table(place, cubic_weights(fraction))


def add_spill(out, block):
    row = lax.broadcasted_iota(jnp.int32, (8, LEV), 0)
    out[0:8, :] = out[0:8, :] + jnp.where(row < 2, block, 0.0)
    out[COLS - 8 : COLS, :] = out[COLS - 8 : COLS, :] + jnp.where(row == 7, block, 0.0)


def deposit_block(b, start, tables, both_ref):
    wide = jnp.zeros((BLOCK, 2 * LEV), F32)
    for which, table in enumerate(tables):
        high, low = spread_block(b * BLOCK, table)
        wide = wide + dot(high, both_ref[which]) + dot(low, both_ref[which])
    return start[pl.ds(b * BLOCK, BLOCK), :] + wide[:, :LEV] + wide[:, LEV:]


def middle_kernel(start, p0, p1, out, both_ref):
    tables = [payload_table(p, both_ref, which) for which, p in enumerate((p0, p1))]

    @pl.loop(0, COLS // BLOCK)
    def _(b):
        out[pl.ds(b * BLOCK, BLOCK), :] = deposit_block(b, start, tables, both_ref)

    add_spill(out, p0[CAP : CAP + 8, :] + p1[CAP : CAP + 8, :])


def last_kernel(step, start, payload, tiny_a, tiny_b, level_map, out, both_ref, sum_ref, lifted_ref, sems):
    tables = [payload_table(payload, both_ref, 0)]

    @pl.loop(0, COLS // BLOCK)
    def _(b):
        sum_ref[pl.ds(b * BLOCK, BLOCK), :] = deposit_block(b, start, tables, both_ref)

    add_spill(sum_ref, payload[CAP : CAP + 8, :] + tiny_a[...] + tiny_b[...])
    map_high, map_low = halves(level_map[step])

    def lift(rows):
        high, low = halves(sum_ref[rows, :])
        return dot_nt(high, map_high) + (dot_nt(high, map_low) + dot_nt(low, map_high))

    if step == 1:
        out[...] = lift(slice(0, COLS))
        return
    copies = []
    for b in range(COLS // HALF):
        rows = slice(b * HALF, (b + 1) * HALF)
        lifted_ref[rows, :] = lift(rows)
        copies.append(pltpu.make_async_copy(lifted_ref.at[rows, :], out.at[rows, :], sems.at[b]))
        copies[-1].start()
    for copy in copies:
        copy.wait()


def couple_kernel(table, x, out):
    count = x.shape[0]

    @pl.loop(0, x.shape[1] // 8)
    def _(r):
        rows = [x[e, pl.ds(r * 8, 8), :] for e in range(count)]
        for b in range(count):
            total = rows[0] * table[count * b : count * b + 1, :]
            for e in range(1, count):
                total = total + rows[e] * table[count * b + e : count * b + e + 1, :]
            out[b, pl.ds(r * 8, 8), :] = total


VM = pl.BlockSpec(memory_space=pltpu.MemorySpace.VMEM)
HBM = pl.BlockSpec(memory_space=pltpu.MemorySpace.HBM)
SM = pl.BlockSpec(memory_space=pltpu.MemorySpace.SMEM)
PARAMS = pltpu.CompilerParams(vmem_limit_bytes=40 * 1024 * 1024)
SPREAD_ROWS = 8 * (2 * REACH + 1)
FAR = [
    jax.ShapeDtypeStruct((WIDE_ROWS, LEV), F32),
    jax.ShapeDtypeStruct((WIDE_ROWS, LEV), F32),
    jax.ShapeDtypeStruct((COLS, 2 * LEV), BF),
    jax.ShapeDtypeStruct((SPREAD_ROWS, LEV), F32),
]
NEAR = [jax.ShapeDtypeStruct((rows, LEV), F32) for rows in (ROWS, ROWS, 8, 8)]
KEYS = jax.ShapeDtypeStruct((1, COLS), jnp.int32)


def call(kernel, out_shape, in_specs, scratch=(), flops=0, out_spec=None):
    multiple = isinstance(out_shape, (list, tuple))
    return pl.pallas_call(
        kernel,
        out_shape=out_shape,
        in_specs=in_specs,
        out_specs=[VM] * len(out_shape) if multiple else out_spec or VM,
        scratch_shapes=list(scratch),
        compiler_params=PARAMS,
        cost_estimate=pl.CostEstimate(flops=flops, transcendentals=0, bytes_accessed=flops // 256),
    )


def transported(step, packed, keys, meta, tile_count, tile_self, field, departure, fraction, level_map):
    far = [swapped(packed[w], w) for w in (0, 1)]
    near = call(functools.partial(near_pack_kernel, step), NEAR, [SM] + [VM] * 4, (), 1000000000)(
        tile_self, packed[2], packed[3], keys, meta
    )
    cross = swapped(near[0], 2)
    partner = swapped(near[1], 3)
    late = lax.optimization_barrier((near[2], partner))
    tiny = swapped(late[0], 5)
    total = jax.ShapeDtypeStruct((COLS, LEV), F32)
    one = pltpu.VMEM((1, CAP, 2 * LEV), BF)
    work = 10000000
    own = call(
        functools.partial(own_kernel, step, tile_count),
        total,
        [SM] + [VM] * 5,
        [pltpu.VMEM((COLS, 2 * LEV), BF), one],
        10000000,
    )(tile_self, field, departure, fraction, near[3], partner)
    index = None
    if step == 1:
        after = lax.optimization_barrier((tile_self, own))
        index = call(
            functools.partial(index_kernel, tile_count),
            [
                KEYS,
                jax.ShapeDtypeStruct((2 * SPREAD_ROWS, COLS), BF),
                jax.ShapeDtypeStruct((32, LEV), F32),
            ],
            [SM, VM, VM],
            (),
            300000000,
        )(after[0], departure, fraction)
        own, index = lax.optimization_barrier((after[1], index))
    own, *far = lax.optimization_barrier((own, *far))
    handed = swapped(far[0][CAP + 16 :] + far[1][CAP + 16 :], 3)
    summed = call(middle_kernel, total, [VM] * 3, [pltpu.VMEM((2, CAP, 2 * LEV), BF)], work)(own, *far)
    result = call(
        functools.partial(last_kernel, step),
        total,
        [VM] * 5,
        [
            one,
            pltpu.VMEM((COLS, LEV), F32),
            pltpu.VMEM((COLS, LEV), F32),
            pltpu.SemaphoreType.DMA((COLS // HALF,)),
        ],
        work,
        HBM if step == 0 else VM,
    )(summed, cross, tiny, handed, level_map)
    return result, index


def body(adjoint_in, departure, fraction, level_map, coarse_map):
    tile_count = lax.axis_size("tile")
    groups = lax.axis_size("grp")
    tile_self = lax.axis_index("tile").astype(jnp.int32).reshape(1)
    first_scratch = [
        pltpu.VMEM((COLS, LEV), F32),
        pltpu.VMEM((2, COLS), jnp.int32),
        pltpu.VMEM((2, COLS), F32),
        pltpu.SemaphoreType.DMA((3,)),
    ]
    outputs = FAR + [KEYS, jax.ShapeDtypeStruct((8, COLS), BF)]
    packed = call(functools.partial(first_far_kernel, tile_count), outputs, [SM, HBM, HBM, HBM], first_scratch)(
        tile_self, *[pltpu.with_memory_space_constraint(x, pltpu.MemorySpace.HBM) for x in (adjoint_in, departure, fraction)]
    )
    table = coarse_map.transpose(1, 2, 0).reshape(groups * groups, LEV)
    second, index = transported(
        1, packed, packed[4], packed[5], tile_count, tile_self, adjoint_in, departure, fraction, level_map
    )

    parts = lax.all_to_all(second.reshape(groups, COLS // groups, LEV), "grp", 0, 0)
    mixed = call(couple_kernel, jax.ShapeDtypeStruct(parts.shape, F32), [VM, VM])(table, parts)
    coupled = lax.all_to_all(mixed, "grp", 0, 0).reshape(COLS, LEV)

    keys, spills, meta = index
    packed = call(second_far_kernel, FAR, [SM] + [VM] * 4)(tile_self, coupled, keys, spills, meta)
    return transported(
        0, packed, keys, meta, tile_count, tile_self, coupled, departure, fraction, level_map
    )[0]


def solution(mesh):
    return jax.shard_map(
        body,
        mesh=mesh,
        in_specs=(
            P(("grp", "tile"), None),
            P(None, ("grp", "tile")),
            P(None, ("grp", "tile")),
            P(),
            P(),
        ),
        out_specs=P(("grp", "tile"), None),
        check_vma=False,
    )
```

```python
import functools

import jax
import jax.numpy as jnp
from jax import lax
from jax.experimental import pallas as pl
from jax.experimental.pallas import tpu as pltpu
from jax.sharding import PartitionSpec as P

REACH = 2
SWAPS = 4
COLS = 1024
LEV = 128
CAP = 512
ROWS = CAP + 16
WIDE_ROWS = CAP + 24
BF = jnp.bfloat16
F32 = jnp.float32


def signs(tile):
    core = 1 - 2 * (tile % 2)
    chip = 1 - 2 * ((tile // 2) % 2)
    return (2 * chip, -2 * chip, -core, core, 3 * core, -3 * core)


def swapped(x, which):
    length = lax.axis_size("tile")
    return lax.ppermute(x, "tile", [(i, (i + signs(i)[which]) % length) for i in range(length)])


def halves(x):
    high = x.astype(BF)
    low = (x - high.astype(F32)).astype(BF)
    return high, low


def dot(a, b):
    return lax.dot_general(a, b, (((1,), (0,)), ((), ())), preferred_element_type=F32)


def dot_nt(a, b):
    return lax.dot_general(a, b, (((1,), (1,)), ((), ())), preferred_element_type=F32)


def cubic_weights(a):
    return (
        -a * (1.0 - a) * (2.0 - a) * (1.0 / 6.0),
        (1.0 + a) * (1.0 - a) * (2.0 - a) * 0.5,
        (1.0 + a) * a * (2.0 - a) * 0.5,
        -(1.0 + a) * a * (1.0 - a) * (1.0 / 6.0),
    )


def locate(departure, tile_self, tile_count):
    place = departure % COLS
    target = (departure // COLS) % tile_count
    offset = (target - tile_self + REACH + tile_count) % tile_count - REACH
    return place, offset


def slots_of(offset, shifts):
    row = lax.broadcasted_iota(jnp.int32, (8, LEV), 0)
    lane_a = lax.broadcasted_iota(jnp.int32, (LEV, LEV), 0)
    lane_b = lax.broadcasted_iota(jnp.int32, (LEV, LEV), 1)
    before = jnp.where(lane_a < lane_b, 1.0, 0.0).astype(BF)
    number = jnp.full((1, COLS), 4, jnp.int32)
    for which, shift in enumerate(shifts[:SWAPS]):
        number = jnp.where(offset == shift, which, number)
    members = []
    for c in range(COLS // LEV):
        part = number[:, c * LEV : (c + 1) * LEV]
        members.append(jnp.where(row == part, 1.0, 0.0))
    member = jnp.concatenate(members, axis=0)
    inside = dot(member.astype(BF), before)
    totals = jnp.sum(member, axis=1, keepdims=True)
    start = jnp.zeros((8, 1), F32)
    keys = []
    for c in range(COLS // LEV):
        block = slice(8 * c, 8 * c + 8)
        rank = inside[block] + start
        start = start + totals[block]
        key = jnp.sum(member[block] * (rank + row.astype(F32) * CAP), axis=0, keepdims=True)
        keys.append(key)
    return jnp.concatenate(keys, axis=1).astype(jnp.int32)


def spill_rows(place, offset, weights):
    row = lax.broadcasted_iota(jnp.int32, (8, COLS), 0)
    last = place == COLS - 1
    first_a = jnp.where(last, weights[2], jnp.where(place == COLS - 2, weights[3], 0.0))
    first_b = jnp.where(last, weights[3], 0.0)
    end = jnp.where(place == 0, weights[0], 0.0)
    rows = jnp.where(row == 0, first_a, jnp.where(row == 1, first_b, jnp.where(row == 7, end, 0.0)))
    spread = [jnp.where(offset == o, rows, 0.0) for o in range(-REACH, REACH + 1)]
    high, low = halves(jnp.concatenate(spread, axis=0))
    return jnp.concatenate([high, low], axis=0)


def meta_rows(place, fraction):
    a = fraction.astype(BF)
    rest = fraction - a.astype(F32)
    b = rest.astype(BF)
    c = rest - b.astype(F32)
    p_high = (place // 32).astype(F32)
    p_low = (place % 32).astype(F32)
    row = lax.broadcasted_iota(jnp.int32, (8, COLS), 0)
    out = jnp.where(row == 0, a.astype(F32), 0.0)
    out = jnp.where(row == 1, b.astype(F32), out)
    out = jnp.where(row == 2, c, out)
    out = jnp.where(row == 3, p_high, out)
    out = jnp.where(row == 4, p_low, out)
    return out.astype(BF)


def choose(keys, which):
    slot = lax.broadcasted_iota(jnp.int32, (CAP, COLS), 0).astype(jnp.int16)
    wanted = jnp.broadcast_to(keys - which * CAP, (16, COLS)).astype(jnp.int16)
    wanted = jnp.concatenate([wanted] * (CAP // 16), axis=0)
    return jnp.where(slot == wanted, BF(1.0), BF(0.0))


def spill_block(spilled, target):
    row = lax.broadcasted_iota(jnp.int32, (8, LEV), 0)
    from_cell = jnp.where(row < 2, target - 1, jnp.where(row == 7, target + 1, -9))
    out = jnp.zeros((8, LEV), F32)
    for o in range(-REACH, REACH + 1):
        block = spilled[8 * (o + REACH) : 8 * (o + REACH) + 8]
        out = out + jnp.where(from_cell == o, block, 0.0)
    return out


def spill_sums(spills, both):
    wide = dot(spills, both)
    count = 8 * (2 * REACH + 1)
    return (wide[:count, :LEV] + wide[:count, LEV:]) + (wide[count:, :LEV] + wide[count:, LEV:])


def index_values(self_ref, departure, fraction, tile_count):
    place, offset = locate(departure, self_ref[0], tile_count)
    keys = slots_of(offset, signs(self_ref[0]))
    weights = cubic_weights(fraction)
    return place, offset, keys, weights


def write_meta(meta_out, base, meta, one_hot):
    got = dot_nt(meta, one_hot)
    fraction = got[0:1] + got[1:2] + got[2:3]
    place = got[3:4] * 32.0 + got[4:5]
    for c in range(CAP // LEV):
        meta_out[base + c : base + c + 1, :] = fraction[:, c * LEV : (c + 1) * LEV]
        meta_out[base + 4 + c : base + 5 + c, :] = place[:, c * LEV : (c + 1) * LEV]


def pack_payload(out, one_hot, both, spilled, shift):
    wide = dot(one_hot, both)
    out[0:CAP, :] = wide[:, :LEV] + wide[:, LEV:]
    out[CAP : CAP + 8, :] = spill_block(spilled, shift)


def pack_far(outs, keys, both, spilled, shifts):
    block = spill_block(spilled, shifts[4])
    for which in range(2):
        one_hot = choose(keys, which)
        pack_payload(outs[which], one_hot, both, spilled, shifts[which])
        outs[which][CAP + 16 : CAP + 24, :] = jnp.where(shifts[which] * shifts[4] > 0, block, 0.0)
        yield one_hot


def first_far_kernel(tile_count, self_ref, field_hbm, departure_hbm, fraction_hbm, *refs):
    outs, (field, departure, fraction, sems) = refs[:-4], refs[-4:]
    copies = [
        pltpu.make_async_copy(departure_hbm, departure, sems.at[0]),
        pltpu.make_async_copy(fraction_hbm, fraction, sems.at[1]),
        pltpu.make_async_copy(field_hbm, field, sems.at[2]),
    ]
    for copy in copies:
        copy.start()
    copies[0].wait()
    copies[1].wait()
    place, offset, keys, weights = index_values(self_ref, departure[1:2, :], fraction[1:2, :], tile_count)
    meta = meta_rows(place, fraction[1:2, :])
    spills = spill_rows(place, offset, weights)
    copies[2].wait()
    high, low = halves(field[...])
    both = jnp.concatenate([high, low], axis=1)
    spilled = spill_sums(spills, both)
    outs[2][...] = both
    outs[3][...] = spilled
    outs[4][...] = keys
    outs[5][...] = meta
    for which, one_hot in enumerate(pack_far(outs, keys, both, spilled, signs(self_ref[0]))):
        write_meta(outs[which], CAP + 8, meta, one_hot)


def second_far_kernel(self_ref, field, keys, spills, meta, *outs):
    high, low = halves(field[...])
    both = jnp.concatenate([high, low], axis=1)
    spilled = spill_sums(spills[...], both)
    outs[2][...] = both
    outs[3][...] = spilled
    for which, _ in enumerate(pack_far(outs, keys[...], both, spilled, signs(self_ref[0]))):
        outs[which][CAP + 8 : CAP + 16, :] = meta[8 * which : 8 * which + 8, :]


def near_pack_kernel(step, self_ref, both, spilled, keys, meta, *outs):
    shifts = signs(self_ref[0])
    sums = spilled[...]
    outs[2][...] = spill_block(sums, shifts[5])
    outs[3][...] = spill_block(sums, 0)
    for out, which in zip(outs, (2, 3)):
        one_hot = choose(keys[...], which)
        pack_payload(out, one_hot, both[...], sums, shifts[which])
        if step == 1:
            write_meta(out, CAP + 8, meta[...], one_hot)
        else:
            out[CAP + 8 : CAP + 16, :] = meta[8 * which : 8 * which + 8, :]


def index_kernel(tile_count, self_ref, departure, fraction, keys_out, spill_out, meta_out):
    place, offset, keys, weights = index_values(self_ref, departure[0:1, :], fraction[0:1, :], tile_count)
    meta = meta_rows(place, fraction[0:1, :])
    keys_out[...] = keys
    spill_out[...] = spill_rows(place, offset, weights)
    for which in range(SWAPS):
        write_meta(meta_out, 8 * which, meta, choose(keys, which))


def second_pack_kernel(self_ref, field, keys, spills, meta, *outs):
    high, low = halves(field[...])
    both = jnp.concatenate([high, low], axis=1)
    spilled = spill_sums(spills[...], both)
    shifts = signs(self_ref[0])
    beyond(outs, spilled, shifts)
    outs[4][...] = spill_block(spilled, shifts[5])
    outs[5][...] = spill_block(spilled, 0)
    for which, shift in enumerate(shifts[:SWAPS]):
        pack_payload(outs[which], choose(keys[...], which), both, spilled, shift)
        outs[which][CAP + 8 : CAP + 16, :] = meta[8 * which : 8 * which + 8, :]


BLOCK = 1024
HALF = 512
I16 = jnp.int16


def tiled(x, rows):
    return jnp.concatenate([x] * (rows // 16), axis=0)


def spread_table(place, weights):
    shape = (16, place.shape[1])
    start = jnp.broadcast_to(place - 1, shape).astype(I16)
    return start, [halves(jnp.broadcast_to(w, shape)) for w in weights]


def spread_block(first_cell, table):
    start, weights = table
    columns = start.shape[1]
    cells = lax.broadcasted_iota(jnp.int32, (BLOCK, columns), 0).astype(I16)
    first = jnp.full((16, columns), first_cell, jnp.int32).astype(I16)
    distance = cells - tiled(start - first, BLOCK)
    high = jnp.zeros((BLOCK, columns), BF)
    low = high
    for k in range(4):
        here = distance == I16(k)
        high = jnp.where(here, tiled(weights[k][0], BLOCK), high)
        low = jnp.where(here, tiled(weights[k][1], BLOCK), low)
    return high, low


def own_kernel(step, tile_count, self_ref, field, departure, fraction, spilled, payload, out, own_ref, both_ref):
    departure = departure[step : step + 1, :]
    fraction = fraction[step : step + 1, :]
    place, offset = locate(departure, self_ref[0], tile_count)
    own_table = spread_table(place, [jnp.where(offset == 0, w, 0.0) for w in cubic_weights(fraction)])
    high, low = halves(field[...])
    own_ref[:, :LEV] = high
    own_ref[:, LEV:] = low
    table = payload_table(payload, both_ref, 0)

    @pl.loop(0, COLS // BLOCK)
    def _(b):
        high, low = spread_block(b * BLOCK, own_table)
        wide = dot(high, own_ref[...])
        slim = dot(low, own_ref[:, :LEV])
        high, low = spread_block(b * BLOCK, table)
        wide = wide + dot(high, both_ref[0])
        slim = slim + dot(low, both_ref[0, :, :LEV])
        out[pl.ds(b * BLOCK, BLOCK), :] = wide[:, :LEV] + (wide[:, LEV:] + slim)

    add_spill(out, spilled[...] + payload[CAP : CAP + 8, :])


def payload_table(payload, both_ref, which):
    high, low = halves(payload[0:CAP, :])
    both_ref[which, :, :LEV] = high
    both_ref[which, :, LEV:] = low
    rows = [payload[CAP + 8 + c : CAP + 9 + c, :] for c in range(8)]
    fraction = jnp.concatenate(rows[:4], axis=1)
    place = jnp.concatenate(rows[4:], axis=1).astype(jnp.int32)
    return spread_table(place, cubic_weights(fraction))


def add_spill(out, block):
    row = lax.broadcasted_iota(jnp.int32, (8, LEV), 0)
    out[0:8, :] = out[0:8, :] + jnp.where(row < 2, block, 0.0)
    out[COLS - 8 : COLS, :] = out[COLS - 8 : COLS, :] + jnp.where(row == 7, block, 0.0)


def deposit_block(b, start, tables, both_ref):
    wide = jnp.zeros((BLOCK, 2 * LEV), F32)
    slim = jnp.zeros((BLOCK, LEV), F32)
    for which, table in enumerate(tables):
        high, low = spread_block(b * BLOCK, table)
        wide = wide + dot(high, both_ref[which])
        slim = slim + dot(low, both_ref[which, :, :LEV])
    return start[pl.ds(b * BLOCK, BLOCK), :] + wide[:, :LEV] + (wide[:, LEV:] + slim)


def middle_kernel(start, p0, p1, out, both_ref):
    tables = [payload_table(p, both_ref, which) for which, p in enumerate((p0, p1))]

    @pl.loop(0, COLS // BLOCK)
    def _(b):
        out[pl.ds(b * BLOCK, BLOCK), :] = deposit_block(b, start, tables, both_ref)

    add_spill(out, p0[CAP : CAP + 8, :] + p1[CAP : CAP + 8, :])


def last_kernel(step, start, payload, tiny_a, tiny_b, level_map, out, both_ref, sum_ref, lifted_ref, sems):
    tables = [payload_table(payload, both_ref, 0)]

    @pl.loop(0, COLS // BLOCK)
    def _(b):
        sum_ref[pl.ds(b * BLOCK, BLOCK), :] = deposit_block(b, start, tables, both_ref)

    add_spill(sum_ref, payload[CAP : CAP + 8, :] + tiny_a[...] + tiny_b[...])
    map_high, map_low = halves(level_map[step])

    def lift(rows):
        high, low = halves(sum_ref[rows, :])
        return dot_nt(high, map_high) + (dot_nt(high, map_low) + dot_nt(low, map_high))

    if step == 1:
        out[...] = lift(slice(0, COLS))
        return
    copies = []
    for b in range(COLS // HALF):
        rows = slice(b * HALF, (b + 1) * HALF)
        lifted_ref[rows, :] = lift(rows)
        copies.append(pltpu.make_async_copy(lifted_ref.at[rows, :], out.at[rows, :], sems.at[b]))
        copies[-1].start()
    for copy in copies:
        copy.wait()


def couple_kernel(table, x, out):
    count = x.shape[0]

    @pl.loop(0, x.shape[1] // 8)
    def _(r):
        rows = [x[e, pl.ds(r * 8, 8), :] for e in range(count)]
        for b in range(count):
            total = rows[0] * table[count * b : count * b + 1, :]
            for e in range(1, count):
                total = total + rows[e] * table[count * b + e : count * b + e + 1, :]
            out[b, pl.ds(r * 8, 8), :] = total


VM = pl.BlockSpec(memory_space=pltpu.MemorySpace.VMEM)
HBM = pl.BlockSpec(memory_space=pltpu.MemorySpace.HBM)
SM = pl.BlockSpec(memory_space=pltpu.MemorySpace.SMEM)
PARAMS = pltpu.CompilerParams(vmem_limit_bytes=40 * 1024 * 1024)
SPREAD_ROWS = 8 * (2 * REACH + 1)
FAR = [
    jax.ShapeDtypeStruct((WIDE_ROWS, LEV), F32),
    jax.ShapeDtypeStruct((WIDE_ROWS, LEV), F32),
    jax.ShapeDtypeStruct((COLS, 2 * LEV), BF),
    jax.ShapeDtypeStruct((SPREAD_ROWS, LEV), F32),
]
NEAR = [jax.ShapeDtypeStruct((rows, LEV), F32) for rows in (ROWS, ROWS, 8, 8)]
KEYS = jax.ShapeDtypeStruct((1, COLS), jnp.int32)


def call(kernel, out_shape, in_specs, scratch=(), flops=0, out_spec=None):
    multiple = isinstance(out_shape, (list, tuple))
    return pl.pallas_call(
        kernel,
        out_shape=out_shape,
        in_specs=in_specs,
        out_specs=[VM] * len(out_shape) if multiple else out_spec or VM,
        scratch_shapes=list(scratch),
        compiler_params=PARAMS,
        cost_estimate=pl.CostEstimate(flops=flops, transcendentals=0, bytes_accessed=flops // 256),
    )


def transported(step, packed, keys, meta, tile_count, tile_self, field, departure, fraction, level_map):
    far = [swapped(packed[w], w) for w in (0, 1)]
    near = call(functools.partial(near_pack_kernel, step), NEAR, [SM] + [VM] * 4, (), 1000000000)(
        tile_self, packed[2], packed[3], keys, meta
    )
    cross = swapped(near[0], 2)
    partner = swapped(near[1], 3)
    late = lax.optimization_barrier((near[2], partner))
    tiny = swapped(late[0], 5)
    total = jax.ShapeDtypeStruct((COLS, LEV), F32)
    one = pltpu.VMEM((1, CAP, 2 * LEV), BF)
    work = 10000000
    own = call(
        functools.partial(own_kernel, step, tile_count),
        total,
        [SM] + [VM] * 5,
        [pltpu.VMEM((COLS, 2 * LEV), BF), one],
        10000000,
    )(tile_self, field, departure, fraction, near[3], partner)
    index = None
    if step == 1:
        after = lax.optimization_barrier((tile_self, own))
        index = call(
            functools.partial(index_kernel, tile_count),
            [
                KEYS,
                jax.ShapeDtypeStruct((2 * SPREAD_ROWS, COLS), BF),
                jax.ShapeDtypeStruct((32, LEV), F32),
            ],
            [SM, VM, VM],
            (),
            300000000,
        )(after[0], departure, fraction)
        own, index = lax.optimization_barrier((after[1], index))
    own, *far = lax.optimization_barrier((own, *far))
    handed = swapped(far[0][CAP + 16 :] + far[1][CAP + 16 :], 3)
    summed = call(middle_kernel, total, [VM] * 3, [pltpu.VMEM((2, CAP, 2 * LEV), BF)], work)(own, *far)
    result = call(
        functools.partial(last_kernel, step),
        total,
        [VM] * 5,
        [
            one,
            pltpu.VMEM((COLS, LEV), F32),
            pltpu.VMEM((COLS, LEV), F32),
            pltpu.SemaphoreType.DMA((COLS // HALF,)),
        ],
        work,
        HBM if step == 0 else VM,
    )(summed, cross, tiny, handed, level_map)
    return result, index


def body(adjoint_in, departure, fraction, level_map, coarse_map):
    tile_count = lax.axis_size("tile")
    groups = lax.axis_size("grp")
    tile_self = lax.axis_index("tile").astype(jnp.int32).reshape(1)
    first_scratch = [
        pltpu.VMEM((COLS, LEV), F32),
        pltpu.VMEM((2, COLS), jnp.int32),
        pltpu.VMEM((2, COLS), F32),
        pltpu.SemaphoreType.DMA((3,)),
    ]
    outputs = FAR + [KEYS, jax.ShapeDtypeStruct((8, COLS), BF)]
    packed = call(functools.partial(first_far_kernel, tile_count), outputs, [SM, HBM, HBM, HBM], first_scratch)(
        tile_self, *[pltpu.with_memory_space_constraint(x, pltpu.MemorySpace.HBM) for x in (adjoint_in, departure, fraction)]
    )
    table = coarse_map.transpose(1, 2, 0).reshape(groups * groups, LEV)
    second, index = transported(
        1, packed, packed[4], packed[5], tile_count, tile_self, adjoint_in, departure, fraction, level_map
    )

    parts = lax.all_to_all(second.reshape(groups, COLS // groups, LEV), "grp", 0, 0)
    mixed = call(couple_kernel, jax.ShapeDtypeStruct(parts.shape, F32), [VM, VM])(table, parts)
    coupled = lax.all_to_all(mixed, "grp", 0, 0).reshape(COLS, LEV)

    keys, spills, meta = index
    packed = call(second_far_kernel, FAR, [SM] + [VM] * 4)(tile_self, coupled, keys, spills, meta)
    return transported(
        0, packed, keys, meta, tile_count, tile_self, coupled, departure, fraction, level_map
    )[0]


def solution(mesh):
    return jax.shard_map(
        body,
        mesh=mesh,
        in_specs=(
            P(("grp", "tile"), None),
            P(None, ("grp", "tile")),
            P(None, ("grp", "tile")),
            P(),
            P(),
        ),
        out_specs=P(("grp", "tile"), None),
        check_vma=False,
    )
```

```python
import functools

import jax
import jax.numpy as jnp
from jax import lax
from jax.experimental import pallas as pl
from jax.experimental.pallas import tpu as pltpu
from jax.sharding import PartitionSpec as P

REACH = 2
SWAPS = 4
COLS = 1024
LEV = 128
CAP = 512
ROWS = CAP + 16
WIDE_ROWS = CAP + 24
BF = jnp.bfloat16
F32 = jnp.float32


def signs(tile):
    core = 1 - 2 * (tile % 2)
    chip = 1 - 2 * ((tile // 2) % 2)
    return (2 * chip, -2 * chip, -core, core, 3 * core, -3 * core)


def swapped(x, which):
    length = lax.axis_size("tile")
    return lax.ppermute(x, "tile", [(i, (i + signs(i)[which]) % length) for i in range(length)])


def halves(x):
    high = x.astype(BF)
    low = (x - high.astype(F32)).astype(BF)
    return high, low


def dot(a, b):
    return lax.dot_general(a, b, (((1,), (0,)), ((), ())), preferred_element_type=F32)


def dot_nt(a, b):
    return lax.dot_general(a, b, (((1,), (1,)), ((), ())), preferred_element_type=F32)


def cubic_weights(a):
    return (
        -a * (1.0 - a) * (2.0 - a) * (1.0 / 6.0),
        (1.0 + a) * (1.0 - a) * (2.0 - a) * 0.5,
        (1.0 + a) * a * (2.0 - a) * 0.5,
        -(1.0 + a) * a * (1.0 - a) * (1.0 / 6.0),
    )


def locate(departure, tile_self, tile_count):
    place = departure % COLS
    target = (departure // COLS) % tile_count
    offset = (target - tile_self + REACH + tile_count) % tile_count - REACH
    return place, offset


def slots_of(offset, shifts):
    row = lax.broadcasted_iota(jnp.int32, (8, LEV), 0)
    lane_a = lax.broadcasted_iota(jnp.int32, (LEV, LEV), 0)
    lane_b = lax.broadcasted_iota(jnp.int32, (LEV, LEV), 1)
    before = jnp.where(lane_a < lane_b, 1.0, 0.0).astype(BF)
    number = jnp.full((1, COLS), 4, jnp.int32)
    for which, shift in enumerate(shifts[:SWAPS]):
        number = jnp.where(offset == shift, which, number)
    members = []
    for c in range(COLS // LEV):
        part = number[:, c * LEV : (c + 1) * LEV]
        members.append(jnp.where(row == part, 1.0, 0.0))
    member = jnp.concatenate(members, axis=0)
    inside = dot(member.astype(BF), before)
    totals = jnp.sum(member, axis=1, keepdims=True)
    start = jnp.zeros((8, 1), F32)
    keys = []
    for c in range(COLS // LEV):
        block = slice(8 * c, 8 * c + 8)
        rank = inside[block] + start
        start = start + totals[block]
        key = jnp.sum(member[block] * (rank + row.astype(F32) * CAP), axis=0, keepdims=True)
        keys.append(key)
    return jnp.concatenate(keys, axis=1).astype(jnp.int32)


def spill_rows(place, offset, weights):
    row = lax.broadcasted_iota(jnp.int32, (8, COLS), 0)
    last = place == COLS - 1
    first_a = jnp.where(last, weights[2], jnp.where(place == COLS - 2, weights[3], 0.0))
    first_b = jnp.where(last, weights[3], 0.0)
    end = jnp.where(place == 0, weights[0], 0.0)
    rows = jnp.where(row == 0, first_a, jnp.where(row == 1, first_b, jnp.where(row == 7, end, 0.0)))
    spread = [jnp.where(offset == o, rows, 0.0) for o in range(-REACH, REACH + 1)]
    high, low = halves(jnp.concatenate(spread, axis=0))
    return jnp.concatenate([high, low], axis=0)


def meta_rows(place, fraction):
    a = fraction.astype(BF)
    rest = fraction - a.astype(F32)
    b = rest.astype(BF)
    c = rest - b.astype(F32)
    p_high = (place // 32).astype(F32)
    p_low = (place % 32).astype(F32)
    row = lax.broadcasted_iota(jnp.int32, (8, COLS), 0)
    out = jnp.where(row == 0, a.astype(F32), 0.0)
    out = jnp.where(row == 1, b.astype(F32), out)
    out = jnp.where(row == 2, c, out)
    out = jnp.where(row == 3, p_high, out)
    out = jnp.where(row == 4, p_low, out)
    return out.astype(BF)


def choose(keys, which):
    slot = lax.broadcasted_iota(jnp.int32, (CAP, COLS), 0).astype(jnp.int16)
    wanted = jnp.broadcast_to(keys - which * CAP, (16, COLS)).astype(jnp.int16)
    wanted = jnp.concatenate([wanted] * (CAP // 16), axis=0)
    return jnp.where(slot == wanted, BF(1.0), BF(0.0))


def spill_block(spilled, target):
    row = lax.broadcasted_iota(jnp.int32, (8, LEV), 0)
    from_cell = jnp.where(row < 2, target - 1, jnp.where(row == 7, target + 1, -9))
    out = jnp.zeros((8, LEV), F32)
    for o in range(-REACH, REACH + 1):
        block = spilled[8 * (o + REACH) : 8 * (o + REACH) + 8]
        out = out + jnp.where(from_cell == o, block, 0.0)
    return out


def spill_sums(spills, both):
    wide = dot(spills, both)
    count = 8 * (2 * REACH + 1)
    return (wide[:count, :LEV] + wide[:count, LEV:]) + (wide[count:, :LEV] + wide[count:, LEV:])


def index_values(self_ref, departure, fraction, tile_count):
    place, offset = locate(departure, self_ref[0], tile_count)
    keys = slots_of(offset, signs(self_ref[0]))
    weights = cubic_weights(fraction)
    return place, offset, keys, weights


def write_meta(meta_out, base, meta, one_hot):
    got = dot_nt(meta, one_hot)
    fraction = got[0:1] + got[1:2] + got[2:3]
    place = got[3:4] * 32.0 + got[4:5]
    for c in range(CAP // LEV):
        meta_out[base + c : base + c + 1, :] = fraction[:, c * LEV : (c + 1) * LEV]
        meta_out[base + 4 + c : base + 5 + c, :] = place[:, c * LEV : (c + 1) * LEV]


def pack_payload(out, one_hot, both, spilled, shift):
    wide = dot(one_hot, both)
    out[0:CAP, :] = wide[:, :LEV] + wide[:, LEV:]
    out[CAP : CAP + 8, :] = spill_block(spilled, shift)


def pack_far(outs, keys, both, spilled, shifts):
    block = spill_block(spilled, shifts[4])
    for which in range(2):
        one_hot = choose(keys, which)
        pack_payload(outs[which], one_hot, both, spilled, shifts[which])
        outs[which][CAP + 16 : CAP + 24, :] = jnp.where(shifts[which] * shifts[4] > 0, block, 0.0)
        yield one_hot


def first_far_kernel(tile_count, self_ref, field_hbm, departure_hbm, fraction_hbm, *refs):
    outs, (field, departure, fraction, sems) = refs[:-4], refs[-4:]
    copies = [
        pltpu.make_async_copy(departure_hbm, departure, sems.at[0]),
        pltpu.make_async_copy(fraction_hbm, fraction, sems.at[1]),
        pltpu.make_async_copy(field_hbm, field, sems.at[2]),
    ]
    for copy in copies:
        copy.start()
    copies[0].wait()
    copies[1].wait()
    place, offset, keys, weights = index_values(self_ref, departure[1:2, :], fraction[1:2, :], tile_count)
    meta = meta_rows(place, fraction[1:2, :])
    spills = spill_rows(place, offset, weights)
    copies[2].wait()
    high, low = halves(field[...])
    both = jnp.concatenate([high, low], axis=1)
    spilled = spill_sums(spills, both)
    outs[2][...] = both
    outs[3][...] = spilled
    outs[4][...] = keys
    outs[5][...] = meta
    for which, one_hot in enumerate(pack_far(outs, keys, both, spilled, signs(self_ref[0]))):
        write_meta(outs[which], CAP + 8, meta, one_hot)


def second_far_kernel(self_ref, field, keys, spills, meta, *outs):
    high, low = halves(field[...])
    both = jnp.concatenate([high, low], axis=1)
    spilled = spill_sums(spills[...], both)
    outs[2][...] = both
    outs[3][...] = spilled
    for which, _ in enumerate(pack_far(outs, keys[...], both, spilled, signs(self_ref[0]))):
        outs[which][CAP + 8 : CAP + 16, :] = meta[8 * which : 8 * which + 8, :]


def near_pack_kernel(step, self_ref, both, spilled, keys, meta, *outs):
    shifts = signs(self_ref[0])
    sums = spilled[...]
    outs[2][...] = spill_block(sums, shifts[5])
    outs[3][...] = spill_block(sums, 0)
    for out, which in zip(outs, (2, 3)):
        one_hot = choose(keys[...], which)
        pack_payload(out, one_hot, both[...], sums, shifts[which])
        if step == 1:
            write_meta(out, CAP + 8, meta[...], one_hot)
        else:
            out[CAP + 8 : CAP + 16, :] = meta[8 * which : 8 * which + 8, :]


def index_kernel(tile_count, self_ref, departure, fraction, keys_out, spill_out, meta_out):
    place, offset, keys, weights = index_values(self_ref, departure[0:1, :], fraction[0:1, :], tile_count)
    meta = meta_rows(place, fraction[0:1, :])
    keys_out[...] = keys
    spill_out[...] = spill_rows(place, offset, weights)
    for which in range(SWAPS):
        write_meta(meta_out, 8 * which, meta, choose(keys, which))


def second_pack_kernel(self_ref, field, keys, spills, meta, *outs):
    high, low = halves(field[...])
    both = jnp.concatenate([high, low], axis=1)
    spilled = spill_sums(spills[...], both)
    shifts = signs(self_ref[0])
    beyond(outs, spilled, shifts)
    outs[4][...] = spill_block(spilled, shifts[5])
    outs[5][...] = spill_block(spilled, 0)
    for which, shift in enumerate(shifts[:SWAPS]):
        pack_payload(outs[which], choose(keys[...], which), both, spilled, shift)
        outs[which][CAP + 8 : CAP + 16, :] = meta[8 * which : 8 * which + 8, :]


BLOCK = 1024
HALF = 256
I16 = jnp.int16


def tiled(x, rows):
    return jnp.concatenate([x] * (rows // 16), axis=0)


def spread_table(place, weights):
    shape = (16, place.shape[1])
    start = jnp.broadcast_to(place - 1, shape).astype(I16)
    return start, [halves(jnp.broadcast_to(w, shape)) for w in weights]


def spread_block(first_cell, table):
    start, weights = table
    columns = start.shape[1]
    cells = lax.broadcasted_iota(jnp.int32, (BLOCK, columns), 0).astype(I16)
    first = jnp.full((16, columns), first_cell, jnp.int32).astype(I16)
    distance = cells - tiled(start - first, BLOCK)
    high = jnp.zeros((BLOCK, columns), BF)
    low = high
    for k in range(4):
        here = distance == I16(k)
        high = jnp.where(here, tiled(weights[k][0], BLOCK), high)
        low = jnp.where(here, tiled(weights[k][1], BLOCK), low)
    return high, low


def own_kernel(step, tile_count, self_ref, field, departure, fraction, spilled, payload, out, own_ref, both_ref):
    departure = departure[step : step + 1, :]
    fraction = fraction[step : step + 1, :]
    place, offset = locate(departure, self_ref[0], tile_count)
    own_table = spread_table(place, [jnp.where(offset == 0, w, 0.0) for w in cubic_weights(fraction)])
    high, low = halves(field[...])
    own_ref[:, :LEV] = high
    own_ref[:, LEV:] = low
    table = payload_table(payload, both_ref, 0)

    @pl.loop(0, COLS // BLOCK)
    def _(b):
        high, low = spread_block(b * BLOCK, own_table)
        wide = dot(high, own_ref[...])
        slim = dot(low, own_ref[:, :LEV])
        high, low = spread_block(b * BLOCK, table)
        wide = wide + dot(high, both_ref[0])
        slim = slim + dot(low, both_ref[0, :, :LEV])
        out[pl.ds(b * BLOCK, BLOCK), :] = wide[:, :LEV] + (wide[:, LEV:] + slim)

    add_spill(out, spilled[...] + payload[CAP : CAP + 8, :])


def payload_table(payload, both_ref, which):
    high, low = halves(payload[0:CAP, :])
    both_ref[which, :, :LEV] = high
    both_ref[which, :, LEV:] = low
    rows = [payload[CAP + 8 + c : CAP + 9 + c, :] for c in range(8)]
    fraction = jnp.concatenate(rows[:4], axis=1)
    place = jnp.concatenate(rows[4:], axis=1).astype(jnp.int32)
    return spread_table(place, cubic_weights(fraction))


def add_spill(out, block):
    row = lax.broadcasted_iota(jnp.int32, (8, LEV), 0)
    out[0:8, :] = out[0:8, :] + jnp.where(row < 2, block, 0.0)
    out[COLS - 8 : COLS, :] = out[COLS - 8 : COLS, :] + jnp.where(row == 7, block, 0.0)


def deposit_block(b, start, tables, both_ref):
    wide = jnp.zeros((BLOCK, 2 * LEV), F32)
    slim = jnp.zeros((BLOCK, LEV), F32)
    for which, table in enumerate(tables):
        high, low = spread_block(b * BLOCK, table)
        wide = wide + dot(high, both_ref[which])
        slim = slim + dot(low, both_ref[which, :, :LEV])
    return start[pl.ds(b * BLOCK, BLOCK), :] + wide[:, :LEV] + (wide[:, LEV:] + slim)


def middle_kernel(start, p0, p1, out, both_ref):
    tables = [payload_table(p, both_ref, which) for which, p in enumerate((p0, p1))]

    @pl.loop(0, COLS // BLOCK)
    def _(b):
        out[pl.ds(b * BLOCK, BLOCK), :] = deposit_block(b, start, tables, both_ref)

    add_spill(out, p0[CAP : CAP + 8, :] + p1[CAP : CAP + 8, :])


def last_kernel(step, start, payload, tiny_a, tiny_b, level_map, out, both_ref, sum_ref, lifted_ref, sems):
    tables = [payload_table(payload, both_ref, 0)]

    @pl.loop(0, COLS // BLOCK)
    def _(b):
        sum_ref[pl.ds(b * BLOCK, BLOCK), :] = deposit_block(b, start, tables, both_ref)

    add_spill(sum_ref, payload[CAP : CAP + 8, :] + tiny_a[...] + tiny_b[...])
    map_high, map_low = halves(level_map[step])

    def lift(rows):
        high, low = halves(sum_ref[rows, :])
        return dot_nt(high, map_high) + (dot_nt(high, map_low) + dot_nt(low, map_high))

    if step == 1:
        out[...] = lift(slice(0, COLS))
        return
    copies = []
    for b in range(COLS // HALF):
        rows = slice(b * HALF, (b + 1) * HALF)
        lifted_ref[rows, :] = lift(rows)
        copies.append(pltpu.make_async_copy(lifted_ref.at[rows, :], out.at[rows, :], sems.at[b]))
        copies[-1].start()
    for copy in copies:
        copy.wait()


def couple_kernel(table, x, out):
    count = x.shape[0]

    @pl.loop(0, x.shape[1] // 8)
    def _(r):
        rows = [x[e, pl.ds(r * 8, 8), :] for e in range(count)]
        for b in range(count):
            total = rows[0] * table[count * b : count * b + 1, :]
            for e in range(1, count):
                total = total + rows[e] * table[count * b + e : count * b + e + 1, :]
            out[b, pl.ds(r * 8, 8), :] = total


VM = pl.BlockSpec(memory_space=pltpu.MemorySpace.VMEM)
HBM = pl.BlockSpec(memory_space=pltpu.MemorySpace.HBM)
SM = pl.BlockSpec(memory_space=pltpu.MemorySpace.SMEM)
PARAMS = pltpu.CompilerParams(vmem_limit_bytes=40 * 1024 * 1024)
SPREAD_ROWS = 8 * (2 * REACH + 1)
FAR = [
    jax.ShapeDtypeStruct((WIDE_ROWS, LEV), F32),
    jax.ShapeDtypeStruct((WIDE_ROWS, LEV), F32),
    jax.ShapeDtypeStruct((COLS, 2 * LEV), BF),
    jax.ShapeDtypeStruct((SPREAD_ROWS, LEV), F32),
]
NEAR = [jax.ShapeDtypeStruct((rows, LEV), F32) for rows in (ROWS, ROWS, 8, 8)]
KEYS = jax.ShapeDtypeStruct((1, COLS), jnp.int32)


def call(kernel, out_shape, in_specs, scratch=(), flops=0, out_spec=None):
    multiple = isinstance(out_shape, (list, tuple))
    return pl.pallas_call(
        kernel,
        out_shape=out_shape,
        in_specs=in_specs,
        out_specs=[VM] * len(out_shape) if multiple else out_spec or VM,
        scratch_shapes=list(scratch),
        compiler_params=PARAMS,
        cost_estimate=pl.CostEstimate(flops=flops, transcendentals=0, bytes_accessed=flops // 256),
    )


def transported(step, packed, keys, meta, tile_count, tile_self, field, departure, fraction, level_map):
    far = [swapped(packed[w], w) for w in (0, 1)]
    near = call(functools.partial(near_pack_kernel, step), NEAR, [SM] + [VM] * 4, (), 1000000000)(
        tile_self, packed[2], packed[3], keys, meta
    )
    cross = swapped(near[0], 2)
    partner = swapped(near[1], 3)
    late = lax.optimization_barrier((near[2], partner))
    tiny = swapped(late[0], 5)
    total = jax.ShapeDtypeStruct((COLS, LEV), F32)
    one = pltpu.VMEM((1, CAP, 2 * LEV), BF)
    work = 10000000
    own = call(
        functools.partial(own_kernel, step, tile_count),
        total,
        [SM] + [VM] * 5,
        [pltpu.VMEM((COLS, 2 * LEV), BF), one],
        10000000,
    )(tile_self, field, departure, fraction, near[3], partner)
    index = None
    if step == 1:
        after = lax.optimization_barrier((tile_self, own))
        index = call(
            functools.partial(index_kernel, tile_count),
            [
                KEYS,
                jax.ShapeDtypeStruct((2 * SPREAD_ROWS, COLS), BF),
                jax.ShapeDtypeStruct((32, LEV), F32),
            ],
            [SM, VM, VM],
            (),
            300000000,
        )(after[0], departure, fraction)
        own, index = lax.optimization_barrier((after[1], index))
    own, *far = lax.optimization_barrier((own, *far))
    handed = swapped(far[0][CAP + 16 :] + far[1][CAP + 16 :], 3)
    summed = call(middle_kernel, total, [VM] * 3, [pltpu.VMEM((2, CAP, 2 * LEV), BF)], work)(own, *far)
    result = call(
        functools.partial(last_kernel, step),
        total,
        [VM] * 5,
        [
            one,
            pltpu.VMEM((COLS, LEV), F32),
            pltpu.VMEM((COLS, LEV), F32),
            pltpu.SemaphoreType.DMA((COLS // HALF,)),
        ],
        work,
        HBM if step == 0 else VM,
    )(summed, cross, tiny, handed, level_map)
    return result, index


def body(adjoint_in, departure, fraction, level_map, coarse_map):
    tile_count = lax.axis_size("tile")
    groups = lax.axis_size("grp")
    tile_self = lax.axis_index("tile").astype(jnp.int32).reshape(1)
    first_scratch = [
        pltpu.VMEM((COLS, LEV), F32),
        pltpu.VMEM((2, COLS), jnp.int32),
        pltpu.VMEM((2, COLS), F32),
        pltpu.SemaphoreType.DMA((3,)),
    ]
    outputs = FAR + [KEYS, jax.ShapeDtypeStruct((8, COLS), BF)]
    packed = call(functools.partial(first_far_kernel, tile_count), outputs, [SM, HBM, HBM, HBM], first_scratch)(
        tile_self, *[pltpu.with_memory_space_constraint(x, pltpu.MemorySpace.HBM) for x in (adjoint_in, departure, fraction)]
    )
    table = coarse_map.transpose(1, 2, 0).reshape(groups * groups, LEV)
    second, index = transported(
        1, packed, packed[4], packed[5], tile_count, tile_self, adjoint_in, departure, fraction, level_map
    )

    parts = lax.all_to_all(second.reshape(groups, COLS // groups, LEV), "grp", 0, 0)
    mixed = call(couple_kernel, jax.ShapeDtypeStruct(parts.shape, F32), [VM, VM])(table, parts)
    coupled = lax.all_to_all(mixed, "grp", 0, 0).reshape(COLS, LEV)

    keys, spills, meta = index
    packed = call(second_far_kernel, FAR, [SM] + [VM] * 4)(tile_self, coupled, keys, spills, meta)
    return transported(
        0, packed, keys, meta, tile_count, tile_self, coupled, departure, fraction, level_map
    )[0]


def solution(mesh):
    return jax.shard_map(
        body,
        mesh=mesh,
        in_specs=(
            P(("grp", "tile"), None),
            P(None, ("grp", "tile")),
            P(None, ("grp", "tile")),
            P(),
            P(),
        ),
        out_specs=P(("grp", "tile"), None),
        check_vma=False,
    )
```
